128 devices in a mesh: ckpt: 4 (over z_hi, core), space: 32 (over y, x, z_lo).
Axes of the slice: x: 4, y: 4, z: 4 (z_hi: 2, z_lo: 2; z = z_hi * 2 + z_lo), core: 2. Of those that a mesh axis runs over, the one named last changes fastest.
Arguments:
- checkpoint: float32 [32, 6, 16, 16, 128], P('space', None, 'ckpt'), may hold values from -5 to 5
- seeds: float32 [4, 32, 6, 16, 16, 128], P('ckpt', 'space'), may hold values from -6 to 6
- cell_rate: float32 [32, 16, 16, 128], P('space'), may hold values from 0.5 to 2
- flux_mats: float32 [3, 6, 6], replicated, may hold values from -1.25 to 1.25
- owner: int32 [32], replicated, may hold values from 0 to 31, each once
- neighbours: int32 [32, 6], replicated, may hold values from 0 to 31, as said below
- orientation: int32 [32, 6], replicated, may hold values from 0 to 3, as said below
Outputs:
- adjoint: float32 [4, 32, 6, 16, 16, 128], P('ckpt', 'space')
- final_state: float32 [32, 6, 16, 16, 128], P('space')
The draws below stay inside these ranges and needn't reach their ends.
Inputs may be any that keep to these rules, and one draw needn't show every extreme that they name: owner lists each space index once. The block across the -x face of neighbours[b, 0] is b, across the +x face of neighbours[b, 1] is b, and likewise for y and z; a block may be its own neighbour. orientation[b, f] equals the code of the same face seen from the block across it.
All inputs are finite; a program needn't handle non-finite values.
Results may differ from the reference program's by a relative error of at most 0.0001.
Values sent between devices are 32-bit elements; how exact they have to be, the bound alone decides.
A program may use at most 128 MiB of HBM per device.

```python
import math
import jax
import jax.numpy as jnp
from jax import lax

CX = 16
CY = 16
CZ = 128
VARS = 6
STEPS = 2
NBLK = 32
NOBJ = 4


def glue_links(key):
    subkeys = jax.random.split(jax.random.fold_in(key, 11), 6)
    across = []
    flips = []
    for dimension in range(3):
        forward_map = jax.random.permutation(subkeys[dimension], NBLK).astype(jnp.int32)
        inverse = jnp.argsort(forward_map, stable=True).astype(jnp.int32)
        codes_here = jax.random.randint(subkeys[3 + dimension], (NBLK,), 0, 4, dtype=jnp.int32)
        across = across + [forward_map, inverse]
        flips = flips + [codes_here, codes_here[inverse]]
    return (jnp.stack(across, axis=1), jnp.stack(flips, axis=1))


def draw_neighbours(key, part):
    return glue_links(key)[0]


def draw_orientation(key, part):
    return glue_links(key)[1]


def levels(rng, shape, shards, low, top_value):
    def one(axis_at, parts):
        steps = jax.random.uniform(jax.random.fold_in(jax.random.fold_in(rng, 6), axis_at), (parts,), jnp.float32, low / len(shards), top_value / len(shards))
        return jnp.repeat(jnp.exp(steps), shape[axis_at] // parts).reshape((-1,) + (1,) * (len(shape) - axis_at - 1))

    gain = one(*shards[0])
    for cut in shards[1:]:
        gain = gain * one(*cut)
    return gain


def noise(stream_key, dims, deviation, bound, cuts=(), kind=jnp.bfloat16):
    loudness = levels(stream_key, dims, cuts, -0.22, 0.18) if cuts else 1.0
    entries = jax.random.normal(stream_key, dims, jnp.float32) * deviation * loudness
    return jnp.minimum(jnp.maximum(entries, -bound), bound).astype(kind)


def setup_inputs(seed: int = 0) -> dict:
    key_of = jax.random.split(jax.random.key(seed), 8)
    return {
        "checkpoint": noise(key_of[0], (NBLK, VARS, CX, CY, CZ), 1.0, 5.0, ((0, 32), (2, 4)), jnp.float32),
        "seeds": noise(key_of[1], (NOBJ, NBLK, VARS, CX, CY, CZ), 1.0, 6.0, ((0, 4), (1, 32)), jnp.float32),
        "cell_rate": jnp.clip(jnp.exp(math.log(2.0) - 1.3862944 * jax.random.uniform(key_of[2], (NBLK, CX, CY, CZ), jnp.float32) ** levels(key_of[2], (NBLK, CX, CY, CZ), ((0, 32),), -0.2, 0.2)), 0.5, 2.0),
        "flux_mats": noise(key_of[3], (3, VARS, VARS), 24 ** -0.5, 1.25, (), jnp.float32),
        "owner": jax.random.permutation(key_of[4], NBLK).astype(jnp.int32),
        "neighbours": draw_neighbours(jax.random.fold_in(key_of[7], 71), 0),
        "orientation": draw_orientation(jax.random.fold_in(key_of[7], 71), 0),
    }


time_step = 0.05
damping = 0.015

def boundary(field, side):
    layer_axis = field.ndim - 3 + side // 2
    location = field.shape[layer_axis] - 1 if side % 2 == 0 else 0
    return lax.index_in_dim(field, location, layer_axis, keepdims=False)

def reorient(face, flips):
    face = jnp.where(flips % 2 == 1, jnp.flip(face, -2), face)
    return jnp.where(flips // 2 % 2 == 1, jnp.flip(face, -1), face)

def pad_with(field, ghosts):
    padded = jnp.pad(field, [(0, 0)] * (field.ndim - 3) + [(1, 1)] * 3)
    for side in range(6):
        layer_axis = side // 2
        location = padded.shape[padded.ndim - 3 + layer_axis] - 1 if side % 2 == 0 else 0
        if layer_axis == 0:
            padded = padded.at[..., location, 1:-1, 1:-1].set(ghosts[side])
        elif layer_axis == 1:
            padded = padded.at[..., 1:-1, location, 1:-1].set(ghosts[side])
        else:
            padded = padded.at[..., 1:-1, 1:-1, location].set(ghosts[side])
    return padded

def advance(padded, rates, flux_mats):
    interior = padded[:, 1:-1, 1:-1, 1:-1]
    divergence = jnp.zeros_like(interior)
    for direction in range(3):
        if direction == 0:
            strip = padded[:, :, 1:-1, 1:-1]
        elif direction == 1:
            strip = padded[:, 1:-1, :, 1:-1]
        else:
            strip = padded[:, 1:-1, 1:-1, :]
        length = strip.shape[direction + 1]
        left_cells = lax.slice_in_dim(strip, 0, length - 1, axis=direction + 1)
        right_cells = lax.slice_in_dim(strip, 1, length, axis=direction + 1)
        average = 0.5 * (left_cells + right_cells)
        difference = right_cells - left_cells
        spread = jnp.sqrt(1.0 + average[0] * average[0])
        face_flux = jnp.einsum('ij,jxyz->ixyz', flux_mats[direction], average, precision=lax.Precision.HIGHEST) - 0.5 * spread * difference
        count = face_flux.shape[direction + 1]
        divergence = divergence + lax.slice_in_dim(face_flux, 1, count, axis=direction + 1) - lax.slice_in_dim(face_flux, 0, count - 1, axis=direction + 1)
    return interior - time_step * rates * divergence - damping * jnp.tanh(interior)

def reference(checkpoint, seeds, cell_rate, flux_mats, owner, neighbours, orientation):
    block_count = owner.shape[0]
    indices = jnp.arange(block_count, dtype=jnp.int32)
    blocks = jnp.zeros((block_count,), jnp.int32).at[owner].set(indices)
    source_rows = owner[neighbours[blocks]].astype(jnp.int32)
    flips = orientation[blocks].astype(jnp.int32)

    def with_ghosts(field):
        ghosts = []
        for side in range(6):
            source = boundary(field[source_rows[:, side]], side ^ 1)
            ghosts.append(reorient(source, flips[:, side].reshape((block_count, 1, 1, 1))))
        return pad_with(field, ghosts)

    def forward(initial):
        field = initial
        for section in range(STEPS):
            field = jax.vmap(advance, (0, 0, None))(with_ghosts(field), cell_rate, flux_mats)
        return field
    final_state, pullback = jax.vjp(forward, checkpoint)
    adjoint = jnp.stack([pullback(seeds[objective])[0] for objective in range(seeds.shape[0])])
    return (adjoint, final_state)
```

```python
import functools

import jax
import jax.numpy as jnp
from jax import lax
from jax.experimental import pallas as pl
from jax.experimental.pallas import tpu as pltpu
from jax.sharding import PartitionSpec as P

MESH = pl.DeviceIdType.MESH
VMEM = pltpu.VMEM
F32 = jnp.float32

NX, NY, NZ, NC = 4, 4, 2, 4
NV, CX, CY, CZ = 6, 16, 16, 128
ROWS = NV * CX * CY
FACE = NV * CX
EXT = (CX + 2) * CY
TAU = 0.05
DAMP = 0.015
HALF = 2 * FACE + CY
QROW = FACE // NC
QA, QB = 2 * QROW + 8, 2 * QROW
SEGS = ((0, FACE), (FACE, FACE), (2 * FACE, CY))
SEGS_QA = ((0, QROW), (QROW, QROW), (2 * QROW, 8))
SEGS_QB = ((0, QROW), (QROW, QROW))


def lanes(shape):
    return lax.broadcasted_iota(jnp.int32, shape, len(shape) - 1)


def rows_of(start, count, step=16):
    return pl.ds(pl.multiple_of(start, step), count)


def pack_xy(src, pa, pb, scale=None):
    for seg, x in ((0, CX - 1), (FACE, 0)):
        for v in range(NV):
            layer = src[pl.ds(v * 256 + x * 16, 16), :]
            if scale is not None:
                layer = layer * (TAU * scale[pl.ds(x * 16, 16), :])
            pa[pl.ds(seg + v * 16, 16), :] = layer
    for seg, y in ((0, CY - 1), (FACE, 0)):
        factor = None
        if scale is not None:
            factor = TAU * scale[pl.ds(y, CX, stride=CY), :]
        for v in range(NV):
            layer = src[pl.ds(v * 256 + y, CX, stride=CY), :]
            if scale is not None:
                layer = layer * factor
            pb[pl.ds(seg + v * 16, 16), :] = layer


def pack_z(values, x, pa, pb):
    lane = lanes((CY, CZ))
    up = pa[pl.ds(2 * FACE, CY), :]
    low = pb[pl.ds(2 * FACE, CY), :]
    for v in range(NV):
        at = v * 16 + x
        here = lane == at
        up = jnp.where(here, pltpu.roll(values[v], at + 1, 1), up)
        low = jnp.where(here, pltpu.roll(values[v], at, 1), low)
    pa[pl.ds(2 * FACE, CY), :] = up
    pb[pl.ds(2 * FACE, CY), :] = low


def clear_z(pa, pb):
    pa[pl.ds(2 * FACE, CY), :] = jnp.zeros((CY, CZ), F32)
    pb[pl.ds(2 * FACE, CY), :] = jnp.zeros((CY, CZ), F32)


def lane_flip(piece, flag):
    lane = lanes(piece.shape)
    return jnp.take_along_axis(piece, lane + flag * (CZ - 1 - 2 * lane), axis=1)


def row_flip(piece, flag):
    row = lax.broadcasted_iota(jnp.int32, (8, CZ), 0)
    index = row + flag * (7 - 2 * row)
    first, second = piece[:8], piece[8:]
    turned = flag == 1
    lower = jnp.where(turned, second, first)
    upper = jnp.where(turned, first, second)
    return jnp.concatenate(
        [jnp.take_along_axis(lower, index, axis=0), jnp.take_along_axis(upper, index, axis=0)]
    )


def place_ghosts(layer, code, ext, gy, gz):
    for f in (0, 1):
        at = (CX + 1) * CY if f == 0 else 0
        for v in range(NV):
            piece = row_flip(layer(f, v), code[f] & 1)
            for h in (0, 8):
                ext[pl.ds(v * EXT + at + h, 8), :] = lane_flip(
                    piece[h : h + 8], (code[f] >> 1) & 1
                )
    for f in (2, 3):
        for v in range(NV):
            piece = layer(f, v)
            for h in (0, 8):
                gy[pl.ds((f - 2) * FACE + v * 16 + h, 8), :] = lane_flip(
                    piece[h : h + 8], (code[f] >> 1) & 1
                )
    for f in (4, 5):
        gz[pl.ds((f - 4) * CY, CY), :] = row_flip(layer(f, 0), (code[f] >> 1) & 1)


def fill_interior(src, ext):
    for v in range(NV):
        ext[pl.ds(v * EXT + CY, CX * CY), :] = src[pl.ds(v * 256, CX * CY), :]


def forward_layers(ghost):
    def face(f):
        start = {1: 0, 0: QROW, 3: QA, 2: QA + QROW}[f]
        return jnp.concatenate([ghost[c, pl.ds(start, QROW), :] for c in range(NC)])

    faces = {f: face(f) for f in range(4)}

    def layer(f, v):
        if f < 4:
            return faces[f][v * 16 : v * 16 + 16]
        c = 0 if f == 5 else 2
        return jnp.concatenate([ghost[c, pl.ds(2 * QROW, 8), :], ghost[c + 1, pl.ds(2 * QROW, 8), :]])

    return layer


def adjoint_layers(ga, gb):
    def layer(f, v):
        half = ga if f in (0, 1, 5) else gb
        if f < 4:
            return half[pl.ds((1 - f % 2) * FACE + v * 16, 16), :]
        return half[pl.ds(2 * FACE, CY), :]

    return layer


def neighbours_of(ext, gy, gz, code, x):
    row = lax.broadcasted_iota(jnp.int32, (CY, CZ), 0)
    lane = lanes((CY, CZ))
    centre = [ext[rows_of(v * EXT + (x + 1) * CY, CY), :] for v in range(NV)]

    def at(direction):
        ups, lows = [], []
        for v in range(NV):
            u = centre[v]
            if direction == 0:
                up = ext[rows_of(v * EXT + (x + 2) * CY, CY), :]
                low = ext[rows_of(v * EXT + x * CY, CY), :]
            elif direction == 1:
                xu = v * 16 + x + (code[2] & 1) * (CX - 1 - 2 * x)
                xl = v * 16 + x + (code[3] & 1) * (CX - 1 - 2 * x)
                up = jnp.where(row == CY - 1, gy[pl.ds(xu, 1), :], pltpu.roll(u, CY - 1, 0))
                low = jnp.where(row == 0, gy[pl.ds(FACE + xl, 1), :], pltpu.roll(u, 1, 0))
            else:
                xu = v * 16 + x + (code[4] & 1) * (CX - 1 - 2 * x)
                xl = v * 16 + x + (code[5] & 1) * (CX - 1 - 2 * x)
                high = pltpu.roll(gz[pl.ds(0, CY), :], CZ - 1 - xu, 1)
                deep = pltpu.roll(gz[pl.ds(CY, CY), :], lax.rem(CZ - xl, CZ), 1)
                up = jnp.where(lane == CZ - 1, high, pltpu.roll(u, CZ - 1, 1))
                low = jnp.where(lane == 0, deep, pltpu.roll(u, 1, 1))
            ups.append(up)
            lows.append(low)
        return ups, lows

    return centre, at


def spread_of(first, second):
    mean = 0.5 * (first + second)
    t = 1.0 + mean * mean
    r = lax.rsqrt(t)
    return t * r, mean * r


def forward_kernel(code, mats, v_ref, ghost, rate, out, pa, pb, ext, gy, gz):
    fill_interior(v_ref, ext)
    place_ghosts(forward_layers(ghost), code, ext, gy, gz)
    clear_z(pa, pb)

    def step(x, carry):
        u, at = neighbours_of(ext, gy, gz, code, x)
        total = [jnp.zeros((CY, CZ), F32) for _ in range(NV)]
        for d in range(3):
            up, low = at(d)
            su, _ = spread_of(up[0], u[0])
            sl, _ = spread_of(u[0], low[0])
            diff = [up[v] - low[v] for v in range(NV)]
            for i in range(NV):
                acc = total[i] - (su * (up[i] - u[i]) - sl * (u[i] - low[i]))
                for j in range(NV):
                    acc = acc + mats[d, i, j] * diff[j]
                total[i] = acc
        tau = (0.5 * TAU) * rate[rows_of(x * CY, CY), :]
        new = [u[v] - tau * total[v] - DAMP * jnp.tanh(u[v]) for v in range(NV)]
        for v in range(NV):
            out[rows_of(v * 256 + x * CY, CY), :] = new[v]
        pack_z(new, x, pa, pb)
        return carry

    lax.fori_loop(0, CX, step, 0)
    pack_xy(out, pa, pb)


def adjoint_body(
    code, mats, ext, gy, gz, wext, wgy, wgz, lam, rate, out, final, pa, pb
):
    def step(x, carry):
        u, at_u = neighbours_of(ext, gy, gz, code, x)
        w, at_w = neighbours_of(wext, wgy, wgz, code, x)
        total = [jnp.zeros((CY, CZ), F32) for _ in range(NV)]
        flux = [jnp.zeros((CY, CZ), F32) for _ in range(NV)]
        tilt = jnp.zeros((CY, CZ), F32)
        for d in range(3):
            up, low = at_u(d)
            wup, wlow = at_w(d)
            su, ru = spread_of(up[0], u[0])
            sl, rl = spread_of(u[0], low[0])
            dot_u = jnp.zeros((CY, CZ), F32)
            dot_l = jnp.zeros((CY, CZ), F32)
            diff = []
            wdiff = []
            for i in range(NV):
                du, dl = up[i] - u[i], u[i] - low[i]
                gu, gl = wup[i] - w[i], w[i] - wlow[i]
                dot_u = dot_u + du * gu
                dot_l = dot_l + dl * gl
                total[i] = total[i] + (su * gu - sl * gl)
                wdiff.append(wup[i] - wlow[i])
                if final is not None:
                    flux[i] = flux[i] - (su * du - sl * dl)
                    diff.append(up[i] - low[i])
            tilt = tilt + ru * dot_u + rl * dot_l
            for i in range(NV):
                acc = total[i]
                for j in range(NV):
                    acc = acc + mats[d, j, i] * wdiff[j]
                total[i] = acc
            if final is not None:
                for i in range(NV):
                    acc = flux[i]
                    for j in range(NV):
                        acc = acc + mats[d, i, j] * diff[j]
                    flux[i] = acc
        tau = TAU * rate[rows_of(x * CY, CY), :]
        packed = []
        for v in range(NV):
            here = rows_of(v * 256 + x * CY, CY)
            bent = jnp.tanh(u[v])
            old = lam[here, :]
            new = old - DAMP * (1.0 - bent * bent) * old + 0.5 * total[v]
            if v == 0:
                new = new - 0.25 * tilt
            out[here, :] = new
            if final is not None:
                final[here, :] = u[v] - (0.5 * tau) * flux[v] - DAMP * bent
            packed.append(tau * new)
        if pa is not None:
            pack_z(packed, x, pa, pb)
        return carry

    lax.fori_loop(0, CX, step, 0)


def fill_weighted(lam, rate, wext):
    for v in range(NV):
        wext[pl.ds(v * EXT + CY, CX * CY), :] = lam[pl.ds(v * 256, CX * CY), :] * (TAU * rate[...])


def adjoint_mid_kernel(
    code, mats, v_ref, ghost, rate, lam, wa, wb, final, out, pa, pb, ext, gy, gz, wext, wgy, wgz
):
    fill_interior(v_ref, ext)
    place_ghosts(forward_layers(ghost), code, ext, gy, gz)
    fill_weighted(lam, rate, wext)
    place_ghosts(adjoint_layers(wa, wb), code, wext, wgy, wgz)
    clear_z(pa, pb)
    adjoint_body(code, mats, ext, gy, gz, wext, wgy, wgz, lam, rate, out, final, pa, pb)
    pack_xy(out, pa, pb, rate)


def adjoint_end_kernel(
    code, mats, v_ref, ghost, rate, lam, wa, wb, out, ext, gy, gz, wext, wgy, wgz
):
    fill_interior(v_ref, ext)
    place_ghosts(forward_layers(ghost), code, ext, gy, gz)
    fill_weighted(lam, rate, wext)
    place_ghosts(adjoint_layers(wa, wb), code, wext, wgy, wgz)
    adjoint_body(code, mats, ext, gy, gz, wext, wgy, wgz, lam, rate, out, None, None, None)


class Place:
    def __init__(self):
        self.c = lax.axis_index("ckpt")
        s = lax.axis_index("space")
        self.z = lax.rem(s, NZ)
        self.x = lax.rem(lax.div(s, NZ), NX)
        self.y = lax.div(s, NZ * NX)

    def space(self, x, y, z):
        return (y * NX + x) * NZ + z

    def along_x(self, k):
        return (self.c, self.space(lax.rem(self.x + k, NX), self.y, self.z))

    def along_y(self, k):
        return (self.c, self.space(self.x, lax.rem(self.y + k, NY), self.z))

    def across_z(self):
        return (self.c, self.space(self.x, self.y, 1 - self.z))

    def member(self, k):
        return (lax.rem(self.c + k, NC), lax.axis_index("space"))


def greet(place, members):
    barrier = pltpu.get_barrier_semaphore()
    partners = [place.across_z()]
    partners += [place.along_x(k) for k in range(1, NX)]
    partners += [place.along_y(k) for k in range(1, NY)]
    if members:
        partners += [place.member(k) for k in range(1, NC)]
    for partner in partners:
        pl.semaphore_signal(barrier, inc=1, device_id=partner, device_id_type=MESH)
    return lambda: pl.semaphore_wait(barrier, len(partners))


class Tables:
    def __init__(self, place, owner, links):
        self.place = place
        spots = [place.space(place.x, lax.rem(place.y + k, NY), place.z) for k in range(NY)]
        spots += [place.space(lax.rem(place.x + k, NX), place.y, place.z) for k in range(1, NX)]

        def find(b, found):
            who = owner[b]
            return tuple(jnp.where(who == s, b, f) for f, s in zip(found, spots))

        blocks = lax.fori_loop(0, NX * NY * NZ, find, tuple(jnp.int32(0) for _ in spots))
        self.own = blocks[0]
        self.down = {"A": list(blocks[:NY]), "B": [blocks[0]] + list(blocks[NY:])}
        self.owner, self.links = owner, links

    def source(self, block, layer):
        s = self.owner[self.links[block, layer ^ 1]]
        return lax.rem(lax.div(s, NZ), NX), lax.div(s, NZ * NX), lax.rem(s, NZ)

    def slot(self, half, k, layer):
        x, y, z = self.source(self.down[half][k], layer)
        turn = jnp.where(z == self.place.z, 0, 1)
        if half == "A":
            return turn * NX + lax.rem(self.place.x - x + NX, NX)
        return turn * NY + lax.rem(self.place.y - y + NY, NY)

    def last(self, half, layer):
        x, y, _ = self.source(self.own, layer)
        if half == "A":
            return lax.rem(self.place.y - y + NY, NY)
        return lax.rem(self.place.x - x + NX, NX)


RING = NX
HOPS = (2, 1, 3)
N_COPIES = 2 + 6 * len(HOPS)


class Exchange:
    def __init__(self, place, bufs, outs, arrivals, send, recv, base):
        self.place, self.bufs, self.outs, self.arrivals = place, bufs, outs, arrivals
        self.send, self.recv, self.base = send, recv, base
        self.all = []
        self.first = {"A": place.along_x, "B": place.along_y}
        self.second = {"A": place.along_y, "B": place.along_x}
        self.across, self.own, self.passed, self.final = {}, {}, {}, {}

    def copy(self, src, dst, device):
        n = self.base + len(self.all)
        made = pltpu.make_async_remote_copy(
            src_ref=src,
            dst_ref=dst,
            send_sem=self.send.at[n],
            recv_sem=self.recv.at[n],
            device_id=device,
            device_id_type=MESH,
        )
        made.start()
        self.all.append(made)
        return made

    def begin(self):
        for half in "AB":
            buf = self.bufs[half]
            self.across[half] = self.copy(buf.at[0], buf.at[RING], self.place.across_z())
        self.own = {"A": [], "B": []}
        for k in HOPS:
            for half in "AB":
                buf = self.bufs[half]
                self.own[half].append(self.copy(buf.at[0], buf.at[k], self.first[half](k)))

    def relay(self):
        self.passed = {"A": [], "B": []}
        for half in "AB":
            self.across[half].wait_recv()
        for k in HOPS:
            for half in "AB":
                buf = self.bufs[half]
                self.passed[half].append(self.copy(buf.at[RING], buf.at[RING + k], self.first[half](k)))

    def hand_on(self, tables, segments):
        self.final = {"A": [], "B": []}
        for half in "AB":
            for made in self.own[half] + self.passed[half]:
                made.wait_recv()
            buf, out, arrive = self.bufs[half], self.outs[half], self.arrivals[half]
            for k in HOPS + (0,):
                for start, count, layer in segments[half]:
                    picked = buf[tables.slot(half, k, layer), pl.ds(start, count), :]
                    if k == 0:
                        arrive[0, pl.ds(start, count), :] = picked
                    else:
                        out[k - 1, pl.ds(start, count), :] = picked
                if k:
                    self.final[half].append(
                        self.copy(out.at[k - 1], arrive.at[k], self.second[half](k))
                    )

    def take(self, tables, segments, put):
        for half in "AB":
            for made in self.final[half]:
                made.wait_recv()
            for start, count, layer in segments[half]:
                put(half, start, count, self.arrivals[half][tables.last(half, layer), pl.ds(start, count), :])

    def drain(self):
        for made in self.all:
            made.wait_send()


def full_segments():
    return {
        "A": [(s, n, f) for (s, n), f in zip(SEGS, (0, 1, 4))],
        "B": [(s, n, f) for (s, n), f in zip(SEGS, (2, 3, 5))],
    }


def quarter_segments(c):
    zface = jnp.where(c < 2, 4, 5)
    return {
        "A": [(s, n, f) for (s, n), f in zip(SEGS_QA, (0, 1, zface))],
        "B": [(s, n, f) for (s, n), f in zip(SEGS_QB, (2, 3))],
    }


def exchange_scratch(ra, rb):
    return [
        VMEM((2 * RING, ra, CZ), F32),
        VMEM((2 * RING, rb, CZ), F32),
        VMEM((RING - 1, ra, CZ), F32),
        VMEM((RING - 1, rb, CZ), F32),
        VMEM((RING, ra, CZ), F32),
        VMEM((RING, rb, CZ), F32),
    ]


def exchange_of(place, scratch, send, recv, base):
    ba, bb, oa, ob, ra, rb = scratch
    return Exchange(place, {"A": ba, "B": bb}, {"A": oa, "B": ob}, {"A": ra, "B": rb}, send, recv, base)


def quarter_packet(c, pa, pb, ba, bb):
    part = rows_of(c * QROW, QROW, 8)
    part2 = rows_of(FACE + c * QROW, QROW, 8)
    ba[0, pl.ds(0, QROW), :] = pa[part, :]
    ba[0, pl.ds(QROW, QROW), :] = pa[part2, :]
    bb[0, pl.ds(0, QROW), :] = pb[part, :]
    bb[0, pl.ds(QROW, QROW), :] = pb[part2, :]
    zrows = rows_of(2 * FACE + lax.rem(c, 2) * 8, 8, 8)
    ba[0, pl.ds(2 * QROW, 8), :] = jnp.where(c < 2, pa[zrows, :], pb[zrows, :])


def share(place, mine, ghost, send, recv, base):
    made = []
    for k in range(1, NC):
        copy = pltpu.make_async_remote_copy(
            src_ref=mine,
            dst_ref=ghost.at[place.c],
            send_sem=send.at[base + k - 1],
            recv_sem=recv.at[base + k - 1],
            device_id=place.member(k),
            device_id_type=MESH,
        )
        copy.start()
        made.append(copy)
    ghost[place.c] = mine[...]
    return made


def open_kernel(
    owner, links, codes, part, seeds, rate, state, ghost, wa, wb, code, *scratch
):
    fwd, adj = scratch[0:6], scratch[6:12]
    pa, pb, mine, stored, landed, send, recv = scratch[12:]
    place = Place()
    met = greet(place, True)
    pack_xy(seeds, pa, pb, rate)
    clear_z(pa, pb)

    def seed_z(x, carry):
        tau = TAU * rate[rows_of(x * CY, CY), :]
        pack_z([seeds[rows_of(v * 256 + x * CY, CY), :] * tau for v in range(NV)], x, pa, pb)
        return carry

    lax.fori_loop(0, CX, seed_z, 0)
    adj[0][0] = pa[...]
    adj[1][0] = pb[...]
    met()
    parts = []
    for k in range(1, NC):
        copy = pltpu.make_async_remote_copy(
            src_ref=part,
            dst_ref=stored.at[place.c],
            send_sem=send.at[k - 1],
            recv_sem=recv.at[k - 1],
            device_id=place.member(k),
            device_id_type=MESH,
        )
        copy.start()
        parts.append(copy)
    stored[place.c] = part[...]
    late = exchange_of(place, adj, send, recv, 6 + N_COPIES)
    late.begin()
    tables = Tables(place, owner, links)
    for f in range(6):
        code[f] = codes[tables.own, f]
    for copy in parts:
        copy.wait_recv()
    span = CX * CY // NC
    for c in range(NC):
        for v in range(NV):
            state[pl.ds(v * 256 + c * span, span), :] = stored[c, pl.ds(v * span, span), :]
    pack_xy(state, pa, pb)
    clear_z(pa, pb)

    def state_z(x, carry):
        pack_z([state[rows_of(v * 256 + x * CY, CY), :] for v in range(NV)], x, pa, pb)
        return carry

    lax.fori_loop(0, CX, state_z, 0)
    quarter_packet(place.c, pa, pb, fwd[0], fwd[1])
    early = exchange_of(place, fwd, send, recv, 6)
    early.begin()
    early.relay()
    late.relay()
    quarters = quarter_segments(place.c)
    early.hand_on(tables, quarters)

    def put_mine(half, start, count, value):
        mine[pl.ds((0 if half == "A" else QA) + start, count), :] = value

    early.take(tables, quarters, put_mine)
    shared = share(place, mine, landed, send, recv, 3)
    wholes = full_segments()
    late.hand_on(tables, wholes)

    def put_whole(half, start, count, value):
        (wa if half == "A" else wb)[pl.ds(start, count), :] = value

    late.take(tables, wholes, put_whole)
    for copy in shared:
        copy.wait_recv()
    ghost[...] = landed[...]
    for copy in parts + shared:
        copy.wait_send()
    early.drain()
    late.drain()


def forward_exchange_kernel(owner, links, pa, pb, ghost, *scratch):
    fwd = scratch[0:6]
    mine, landed, send, recv = scratch[6:]
    place = Place()
    met = greet(place, True)
    quarter_packet(place.c, pa, pb, fwd[0], fwd[1])
    met()
    early = exchange_of(place, fwd, send, recv, 3)
    early.begin()
    tables = Tables(place, owner, links)
    early.relay()
    quarters = quarter_segments(place.c)
    early.hand_on(tables, quarters)

    def put_mine(half, start, count, value):
        mine[pl.ds((0 if half == "A" else QA) + start, count), :] = value

    early.take(tables, quarters, put_mine)
    shared = share(place, mine, landed, send, recv, 0)
    for copy in shared:
        copy.wait_recv()
    ghost[...] = landed[...]
    for copy in shared:
        copy.wait_send()
    early.drain()


def adjoint_exchange_kernel(owner, links, pa, pb, wa, wb, *scratch):
    adj = scratch[0:6]
    send, recv = scratch[6:]
    place = Place()
    met = greet(place, False)
    adj[0][0] = pa[...]
    adj[1][0] = pb[...]
    met()
    late = exchange_of(place, adj, send, recv, 0)
    late.begin()
    tables = Tables(place, owner, links)
    late.relay()
    wholes = full_segments()
    late.hand_on(tables, wholes)

    def put_whole(half, start, count, value):
        (wa if half == "A" else wb)[pl.ds(start, count), :] = value

    late.take(tables, wholes, put_whole)
    late.drain()


def spec(space):
    return pl.BlockSpec(memory_space=space)


def shape(*dims):
    return jax.ShapeDtypeStruct(dims, F32)


def call(kernel, ins, outs, scratch, ident=None):
    return pl.pallas_call(
        kernel,
        out_shape=tuple(s for _, s in outs),
        in_specs=[spec(m) for m in ins],
        out_specs=tuple(spec(m) for m, _ in outs),
        scratch_shapes=scratch,
        compiler_params=pltpu.CompilerParams(
            collective_id=ident, has_side_effects=ident is not None
        ),
    )


def on_device(checkpoint, seeds, cell_rate, flux_mats, owner, neighbours, orientation):
    vm, sm = pltpu.VMEM, pltpu.SMEM
    part = checkpoint.reshape(ROWS // NC, CZ)
    rate = cell_rate.reshape(CX * CY, CZ)
    lam = seeds.reshape(ROWS, CZ)
    sems = lambda n: [pltpu.SemaphoreType.DMA((n,)), pltpu.SemaphoreType.DMA((n,))]
    quarter, whole = exchange_scratch(QA, QB), exchange_scratch(HALF, HALF)
    half = shape(HALF, CZ)
    ghosts = shape(NC, QA + QB, CZ)
    block = shape(ROWS, CZ)

    state, ghost0, wa, wb, code = call(
        open_kernel,
        (sm, sm, sm, vm, vm, vm),
        (
            (vm, block),
            (vm, ghosts),
            (vm, half),
            (vm, half),
            (sm, jax.ShapeDtypeStruct((8,), jnp.int32)),
        ),
        quarter
        + whole
        + [VMEM((HALF, CZ), F32), VMEM((HALF, CZ), F32), VMEM((QA + QB, CZ), F32)]
        + [VMEM((NC, ROWS // NC, CZ), F32), VMEM((NC, QA + QB, CZ), F32)]
        + sems(6 + 2 * N_COPIES),
        0,
    )(owner, neighbours, orientation, part, lam, rate)

    stencil = [VMEM((NV * EXT, CZ), F32), VMEM((2 * FACE, CZ), F32), VMEM((2 * CY, CZ), F32)]
    state1, pa, pb = call(
        forward_kernel, (sm, sm, vm, vm, vm), ((vm, block), (vm, half), (vm, half)), stencil
    )(code, flux_mats, state, ghost0, rate)

    (ghost1,) = call(
        forward_exchange_kernel,
        (sm, sm, vm, vm),
        ((vm, ghosts),),
        quarter + [VMEM((QA + QB, CZ), F32), VMEM((NC, QA + QB, CZ), F32)] + sems(3 + N_COPIES),
        1,
    )(owner, neighbours, pa, pb)

    final, lam1, pa, pb = call(
        adjoint_mid_kernel,
        (sm, sm) + (vm,) * 6,
        ((vm, block), (vm, block), (vm, half), (vm, half)),
        stencil * 2,
    )(code, flux_mats, state1, ghost1, rate, lam, wa, wb)

    wa, wb = call(
        adjoint_exchange_kernel,
        (sm, sm, vm, vm),
        ((vm, half), (vm, half)),
        whole + sems(N_COPIES),
        2,
    )(owner, neighbours, pa, pb)

    (lam0,) = call(
        adjoint_end_kernel, (sm, sm) + (vm,) * 6, ((vm, block),), stencil * 2
    )(code, flux_mats, state, ghost0, rate, lam1, wa, wb)
    return (
        lam0.reshape(1, 1, NV, CX, CY, CZ),
        final.reshape(1, NV, CX, CY, CZ),
    )


def solution(mesh):
    return jax.shard_map(
        on_device,
        mesh=mesh,
        in_specs=(
            P("space", None, "ckpt", None, None),
            P("ckpt", "space", None, None, None, None),
            P("space", None, None, None),
            P(),
            P(),
            P(),
            P(),
        ),
        out_specs=(P("ckpt", "space", None, None, None, None), P("space", None, None, None, None)),
        check_vma=False,
    )
```

```python
import jax
import jax.numpy as jnp
from jax import lax
from jax.experimental import pallas as pl
from jax.experimental.pallas import tpu as pltpu
from jax.sharding import PartitionSpec as P

MESH = pl.DeviceIdType.MESH
VMEM = pltpu.VMEM
F32 = jnp.float32

NX, NY, NZ, NC = 4, 4, 2, 4
NV, CX, CY, CZ = 6, 16, 16, 128
ROWS = NV * CX * CY
FACE = NV * CX
EXT = (CX + 2) * CY
TAU = 0.05
DAMP = 0.015
HALF = 2 * FACE + CY
QROW = FACE // NC
QA, QB = 2 * QROW + 8, 2 * QROW
SEGS = ((0, FACE), (FACE, FACE), (2 * FACE, CY))
SEGS_QA = ((0, QROW), (QROW, QROW), (2 * QROW, 8))
SEGS_QB = ((0, QROW), (QROW, QROW))


def lanes(shape):
    return lax.broadcasted_iota(jnp.int32, shape, len(shape) - 1)


def rows_of(start, count, step=16):
    return pl.ds(pl.multiple_of(start, step), count)


def cell_rows(v, x):
    return rows_of(v * EXT + (x + 1) * CY, CY)


def pack_xy(ext, pa, pb):
    for seg, x in ((0, CX - 1), (FACE, 0)):
        for v in range(NV):
            pa[pl.ds(seg + v * 16, 16), :] = ext[pl.ds(v * EXT + (x + 1) * CY, CY), :]
    for seg, y in ((0, CY - 1), (FACE, 0)):
        for v in range(NV):
            pb[pl.ds(seg + v * 16, 16), :] = ext[pl.ds(v * EXT + CY + y, CX, stride=CY), :]


def pack_z(values, x, pa, pb):
    lane = lanes((CY, CZ))
    up = pa[pl.ds(2 * FACE, CY), :]
    low = pb[pl.ds(2 * FACE, CY), :]
    for v in range(NV):
        at = v * 16 + x
        here = lane == at
        up = jnp.where(here, pltpu.roll(values[v], at + 1, 1), up)
        low = jnp.where(here, pltpu.roll(values[v], at, 1), low)
    pa[pl.ds(2 * FACE, CY), :] = up
    pb[pl.ds(2 * FACE, CY), :] = low


def clear_z(pa, pb):
    pa[pl.ds(2 * FACE, CY), :] = jnp.zeros((CY, CZ), F32)
    pb[pl.ds(2 * FACE, CY), :] = jnp.zeros((CY, CZ), F32)


def lane_flip(piece, flag, width):
    lane = lanes(piece.shape)
    at = lane & (width - 1)
    return jnp.take_along_axis(piece, lane + flag * (width - 1 - 2 * at), axis=1)


def row_flip(piece, flag):
    row = lax.broadcasted_iota(jnp.int32, (8, CZ), 0)
    index = row + flag * (7 - 2 * row)
    first, second = piece[:8], piece[8:]
    turned = flag == 1
    lower = jnp.where(turned, second, first)
    upper = jnp.where(turned, first, second)
    return [jnp.take_along_axis(lower, index, axis=0), jnp.take_along_axis(upper, index, axis=0)]


def place_ghosts(layer, code, ext, gy, gz):
    for f in range(6):
        first, second = code[f] & 1, (code[f] >> 1) & 1
        if f < 4:
            for v in range(NV):
                for h, piece in enumerate(row_flip(layer(f, v), first)):
                    piece = lane_flip(piece, second, CZ)
                    if f < 2:
                        start = v * EXT + ((CX + 1) * CY if f == 0 else 0)
                        ext[pl.ds(start + 8 * h, 8), :] = piece
                    else:
                        gy[pl.ds((f - 2) * FACE + v * 16 + 8 * h, 8), :] = piece
        else:
            for h, piece in enumerate(row_flip(layer(f, 0), second)):
                gz[pl.ds((f - 4) * CY + 8 * h, 8), :] = lane_flip(piece, first, CX)


def forward_layers(ghost):
    def face(f):
        start = {1: 0, 0: QROW, 3: QA, 2: QA + QROW}[f]
        return jnp.concatenate([ghost[c, pl.ds(start, QROW), :] for c in range(NC)])

    faces = {f: face(f) for f in range(4)}

    def layer(f, v):
        if f < 4:
            return faces[f][v * 16 : v * 16 + 16]
        c = 0 if f == 5 else 2
        return jnp.concatenate([ghost[c, pl.ds(2 * QROW, 8), :], ghost[c + 1, pl.ds(2 * QROW, 8), :]])

    return layer


def adjoint_layers(ga, gb):
    def layer(f, v):
        half = ga if f in (0, 1, 5) else gb
        if f < 4:
            return half[pl.ds((1 - f % 2) * FACE + v * 16, 16), :]
        return half[pl.ds(2 * FACE, CY), :]

    return layer


def neighbours_of(grid, x):
    ext, gy, gz = grid
    row = lax.broadcasted_iota(jnp.int32, (CY, CZ), 0)
    lane = lanes((CY, CZ))
    centre = [ext[cell_rows(v, x), :] for v in range(NV)]

    def at(direction):
        ups, lows = [], []
        for v in range(NV):
            u = centre[v]
            at_x = v * 16 + x
            if direction == 0:
                up = ext[cell_rows(v, x + 1), :]
                low = ext[cell_rows(v, x - 1), :]
            elif direction == 1:
                up = jnp.where(row == CY - 1, gy[pl.ds(at_x, 1), :], pltpu.roll(u, CY - 1, 0))
                low = jnp.where(row == 0, gy[pl.ds(FACE + at_x, 1), :], pltpu.roll(u, 1, 0))
            else:
                high = pltpu.roll(gz[pl.ds(0, CY), :], CZ - 1 - at_x, 1)
                deep = pltpu.roll(gz[pl.ds(CY, CY), :], lax.rem(CZ - at_x, CZ), 1)
                up = jnp.where(lane == CZ - 1, high, pltpu.roll(u, CZ - 1, 1))
                low = jnp.where(lane == 0, deep, pltpu.roll(u, 1, 1))
            ups.append(up)
            lows.append(low)
        return ups, lows

    return centre, at


def spread_of(first, second):
    mean = 0.5 * (first + second)
    t = 1.0 + mean * mean
    r = lax.rsqrt(t)
    return t * r, mean * r


def forward_step(mats, rate, grid, out, pa, pb, x):
    u, at = neighbours_of(grid, x)
    total = [jnp.zeros((CY, CZ), F32) for _ in range(NV)]
    for d in range(3):
        up, low = at(d)
        su, _ = spread_of(up[0], u[0])
        sl, _ = spread_of(u[0], low[0])
        diff = [up[v] - low[v] for v in range(NV)]
        for i in range(NV):
            acc = total[i] - (su * (up[i] - u[i]) - sl * (u[i] - low[i]))
            for j in range(NV):
                acc = acc + mats[d, i, j] * diff[j]
            total[i] = acc
    tau = (0.5 * TAU) * rate[rows_of(x * CY, CY), :]
    new = [u[v] - tau * total[v] - DAMP * jnp.tanh(u[v]) for v in range(NV)]
    for v in range(NV):
        out[cell_rows(v, x), :] = new[v]
    pack_z(new, x, pa, pb)


def adjoint_step(mats, rate, grid, wgrid, lam, out, x, final=None, weighted=None, pa=None, pb=None):
    u, at_u = neighbours_of(grid, x)
    w, at_w = neighbours_of(wgrid, x)
    total = [jnp.zeros((CY, CZ), F32) for _ in range(NV)]
    flux = [jnp.zeros((CY, CZ), F32) for _ in range(NV)]
    tilt = jnp.zeros((CY, CZ), F32)
    for d in range(3):
        up, low = at_u(d)
        wup, wlow = at_w(d)
        su, ru = spread_of(up[0], u[0])
        sl, rl = spread_of(u[0], low[0])
        dot_u = jnp.zeros((CY, CZ), F32)
        dot_l = jnp.zeros((CY, CZ), F32)
        diff = []
        wdiff = []
        for i in range(NV):
            du, dl = up[i] - u[i], u[i] - low[i]
            gu, gl = wup[i] - w[i], w[i] - wlow[i]
            dot_u = dot_u + du * gu
            dot_l = dot_l + dl * gl
            total[i] = total[i] + (su * gu - sl * gl)
            wdiff.append(wup[i] - wlow[i])
            if final is not None:
                flux[i] = flux[i] - (su * du - sl * dl)
                diff.append(up[i] - low[i])
        tilt = tilt + ru * dot_u + rl * dot_l
        for i in range(NV):
            acc = total[i]
            for j in range(NV):
                acc = acc + mats[d, j, i] * wdiff[j]
            total[i] = acc
        if final is not None:
            for i in range(NV):
                acc = flux[i]
                for j in range(NV):
                    acc = acc + mats[d, i, j] * diff[j]
                flux[i] = acc
    tau = TAU * rate[rows_of(x * CY, CY), :]
    packed = []
    for v in range(NV):
        here = rows_of(v * 256 + x * CY, CY)
        bent = jnp.tanh(u[v])
        old = lam[here, :]
        new = old - DAMP * (1.0 - bent * bent) * old + 0.5 * total[v]
        if v == 0:
            new = new - 0.25 * tilt
        out[here, :] = new
        if final is not None:
            final[here, :] = u[v] - (0.5 * tau) * flux[v] - DAMP * bent
            packed.append(tau * new)
            weighted[cell_rows(v, x), :] = packed[v]
    if final is not None:
        pack_z(packed, x, pa, pb)


def each_x(step, start=0, stop=CX):
    def body(x, carry):
        step(x)
        return carry

    lax.fori_loop(start, stop, body, 0)


class Place:
    def __init__(self):
        self.c = lax.axis_index("ckpt")
        s = lax.axis_index("space")
        self.z = lax.rem(s, NZ)
        self.x = lax.rem(lax.div(s, NZ), NX)
        self.y = lax.div(s, NZ * NX)

    def space(self, x, y, z):
        return (y * NX + x) * NZ + z

    def along_x(self, k):
        return (self.c, self.space(lax.rem(self.x + k, NX), self.y, self.z))

    def along_y(self, k):
        return (self.c, self.space(self.x, lax.rem(self.y + k, NY), self.z))

    def across_z(self):
        return (self.c, self.space(self.x, self.y, 1 - self.z))

    def member(self, k):
        return (lax.rem(self.c + k, NC), lax.axis_index("space"))


def greet(place, members):
    barrier = pltpu.get_barrier_semaphore()
    partners = [place.across_z()]
    partners += [place.along_x(k) for k in range(1, NX)]
    partners += [place.along_y(k) for k in range(1, NY)]
    if members:
        partners += [place.member(k) for k in range(1, NC)]
    for partner in partners:
        pl.semaphore_signal(barrier, inc=1, device_id=partner, device_id_type=MESH)
    return lambda: pl.semaphore_wait(barrier, len(partners))


class Tables:
    def __init__(self, place, owner, links):
        self.place = place
        spots = [place.space(place.x, lax.rem(place.y + k, NY), place.z) for k in range(NY)]
        spots += [place.space(lax.rem(place.x + k, NX), place.y, place.z) for k in range(1, NX)]

        def find(b, found):
            who = owner[b]
            return tuple(jnp.where(who == s, b, f) for f, s in zip(found, spots))

        blocks = lax.fori_loop(0, NX * NY * NZ, find, tuple(jnp.int32(0) for _ in spots))
        self.own = blocks[0]
        self.down = {"A": list(blocks[:NY]), "B": [blocks[0]] + list(blocks[NY:])}
        self.owner, self.links = owner, links

    def source(self, block, layer):
        s = self.owner[self.links[block, layer ^ 1]]
        return lax.rem(lax.div(s, NZ), NX), lax.div(s, NZ * NX), lax.rem(s, NZ)

    def slot(self, half, k, layer):
        x, y, z = self.source(self.down[half][k], layer)
        turn = jnp.where(z == self.place.z, 0, 1)
        if half == "A":
            return turn * NX + lax.rem(self.place.x - x + NX, NX)
        return turn * NY + lax.rem(self.place.y - y + NY, NY)

    def last(self, half, layer):
        x, y, _ = self.source(self.own, layer)
        if half == "A":
            return lax.rem(self.place.y - y + NY, NY)
        return lax.rem(self.place.x - x + NX, NX)


RING = NX
HOPS = (2, 1, 3)
N_COPIES = 2 + 6 * len(HOPS)


class Exchange:
    def __init__(self, place, bufs, outs, arrivals, send, recv, base):
        self.place, self.bufs, self.outs, self.arrivals = place, bufs, outs, arrivals
        self.send, self.recv, self.base = send, recv, base
        self.all = []
        self.first = {"A": place.along_x, "B": place.along_y}
        self.second = {"A": place.along_y, "B": place.along_x}
        self.across, self.own, self.passed, self.final = {}, {}, {}, {}

    def copy(self, src, dst, device):
        n = self.base + len(self.all)
        made = pltpu.make_async_remote_copy(
            src_ref=src,
            dst_ref=dst,
            send_sem=self.send.at[n],
            recv_sem=self.recv.at[n],
            device_id=device,
            device_id_type=MESH,
        )
        made.start()
        self.all.append(made)
        return made

    def begin(self):
        for half in "AB":
            buf = self.bufs[half]
            self.across[half] = self.copy(buf.at[0], buf.at[RING], self.place.across_z())
        self.own = {"A": [], "B": []}
        for k in HOPS:
            for half in "AB":
                buf = self.bufs[half]
                self.own[half].append(self.copy(buf.at[0], buf.at[k], self.first[half](k)))

    def relay(self):
        self.passed = {"A": [], "B": []}
        for half in "AB":
            self.across[half].wait_recv()
        for k in HOPS:
            for half in "AB":
                buf = self.bufs[half]
                self.passed[half].append(self.copy(buf.at[RING], buf.at[RING + k], self.first[half](k)))

    def hand_on(self, tables, segments):
        self.final = {"A": [], "B": []}
        for half in "AB":
            for made in self.own[half] + self.passed[half]:
                made.wait_recv()
            buf, out, arrive = self.bufs[half], self.outs[half], self.arrivals[half]
            for k in HOPS + (0,):
                for start, count, layer in segments[half]:
                    picked = buf[tables.slot(half, k, layer), pl.ds(start, count), :]
                    if k == 0:
                        arrive[0, pl.ds(start, count), :] = picked
                    else:
                        out[k - 1, pl.ds(start, count), :] = picked
                if k:
                    self.final[half].append(
                        self.copy(out.at[k - 1], arrive.at[k], self.second[half](k))
                    )

    def take(self, tables, segments, put):
        for half in "AB":
            for made in self.final[half]:
                made.wait_recv()
            for start, count, layer in segments[half]:
                put(half, start, count, self.arrivals[half][tables.last(half, layer), pl.ds(start, count), :])

    def drain(self):
        for made in self.all:
            made.wait_send()


def full_segments():
    return {
        "A": [(s, n, f) for (s, n), f in zip(SEGS, (0, 1, 4))],
        "B": [(s, n, f) for (s, n), f in zip(SEGS, (2, 3, 5))],
    }


def quarter_segments(c):
    zface = jnp.where(c < 2, 4, 5)
    return {
        "A": [(s, n, f) for (s, n), f in zip(SEGS_QA, (0, 1, zface))],
        "B": [(s, n, f) for (s, n), f in zip(SEGS_QB, (2, 3))],
    }


def exchange_scratch(ra, rb):
    return [
        VMEM((2 * RING, ra, CZ), F32),
        VMEM((2 * RING, rb, CZ), F32),
        VMEM((RING - 1, ra, CZ), F32),
        VMEM((RING - 1, rb, CZ), F32),
        VMEM((RING, ra, CZ), F32),
        VMEM((RING, rb, CZ), F32),
    ]


def exchange_of(place, scratch, send, recv, base):
    ba, bb, oa, ob, ra, rb = scratch
    return Exchange(place, {"A": ba, "B": bb}, {"A": oa, "B": ob}, {"A": ra, "B": rb}, send, recv, base)


def quarter_packet(c, pa, pb, ba, bb):
    part = rows_of(c * QROW, QROW, 8)
    part2 = rows_of(FACE + c * QROW, QROW, 8)
    ba[0, pl.ds(0, QROW), :] = pa[part, :]
    ba[0, pl.ds(QROW, QROW), :] = pa[part2, :]
    bb[0, pl.ds(0, QROW), :] = pb[part, :]
    bb[0, pl.ds(QROW, QROW), :] = pb[part2, :]
    zrows = rows_of(2 * FACE + lax.rem(c, 2) * 8, 8, 8)
    ba[0, pl.ds(2 * QROW, 8), :] = jnp.where(c < 2, pa[zrows, :], pb[zrows, :])


def share(place, mine, ghost, send, recv, base):
    made = []
    for k in range(1, NC):
        copy = pltpu.make_async_remote_copy(
            src_ref=mine,
            dst_ref=ghost.at[place.c],
            send_sem=send.at[base + k - 1],
            recv_sem=recv.at[base + k - 1],
            device_id=place.member(k),
            device_id_type=MESH,
        )
        copy.start()
        made.append(copy)
    ghost[place.c] = mine[...]
    return made


def put_into(mine):
    def put(half, start, count, value):
        mine[pl.ds((0 if half == "A" else QA) + start, count), :] = value

    return put


def put_halves(wa, wb):
    def put(half, start, count, value):
        (wa if half == "A" else wb)[pl.ds(start, count), :] = value

    return put


def kernel(owner, links, codes, mats, part, seeds, rate, adjoint, final, *scratch):
    first, second = scratch[0:6], scratch[6:12]
    third, fourth = scratch[12:18], scratch[18:24]
    grid0, grid1, wgrid, wgrid1 = (scratch[24 + 3 * n : 27 + 3 * n] for n in range(4))
    pa, pb, mine, mine1, stored, landed, landed1, wa, wb, lam, send, recv = scratch[36:]
    place = Place()
    met = greet(place, True)

    clear_z(pa, pb)

    def weigh(x):
        tau = TAU * rate[rows_of(x * CY, CY), :]
        values = [seeds[rows_of(v * 256 + x * CY, CY), :] * tau for v in range(NV)]
        for v in range(NV):
            wgrid[0][cell_rows(v, x), :] = values[v]
        pack_z(values, x, pa, pb)

    each_x(weigh)
    pack_xy(wgrid[0], pa, pb)
    third[0][0] = pa[...]
    third[1][0] = pb[...]
    met()

    parts = []
    for k in range(1, NC):
        copy = pltpu.make_async_remote_copy(
            src_ref=part,
            dst_ref=stored.at[place.c],
            send_sem=send.at[k - 1],
            recv_sem=recv.at[k - 1],
            device_id=place.member(k),
            device_id_type=MESH,
        )
        copy.start()
        parts.append(copy)
    stored[place.c] = part[...]
    tables = Tables(place, owner, links)
    code = [codes[tables.own, f] for f in range(6)]
    for copy in parts:
        copy.wait_recv()
    span = CX * CY // NC
    for c in range(NC):
        for v in range(NV):
            grid0[0][pl.ds(v * EXT + CY + c * span, span), :] = stored[c, pl.ds(v * span, span), :]
    pack_xy(grid0[0], pa, pb)
    clear_z(pa, pb)
    each_x(lambda x: pack_z([grid0[0][cell_rows(v, x), :] for v in range(NV)], x, pa, pb))

    quarters, wholes = quarter_segments(place.c), full_segments()
    early = exchange_of(place, first, send, recv, 9)
    late = exchange_of(place, third, send, recv, 9 + N_COPIES)
    again = exchange_of(place, second, send, recv, 9 + 2 * N_COPIES)
    back = exchange_of(place, fourth, send, recv, 9 + 3 * N_COPIES)

    quarter_packet(place.c, pa, pb, first[0], first[1])
    early.begin()
    early.relay()
    early.hand_on(tables, quarters)
    early.take(tables, quarters, put_into(mine))
    shared = share(place, mine, landed, send, recv, 3)
    late.begin()
    clear_z(pa, pb)
    for copy in shared:
        copy.wait_recv()
    place_ghosts(forward_layers(landed), code, *grid0)

    def forward(x):
        forward_step(mats, rate, grid0, grid1[0], pa, pb, x)

    each_x(forward, 0, CX // 2)
    late.relay()
    each_x(forward, CX // 2, CX)
    pack_xy(grid1[0], pa, pb)

    quarter_packet(place.c, pa, pb, second[0], second[1])
    again.begin()
    again.relay()
    late.hand_on(tables, wholes)
    again.hand_on(tables, quarters)
    again.take(tables, quarters, put_into(mine1))
    shared1 = share(place, mine1, landed1, send, recv, 6)
    late.take(tables, wholes, put_halves(wa, wb))
    place_ghosts(adjoint_layers(wa, wb), code, *wgrid)
    clear_z(pa, pb)
    for copy in shared1:
        copy.wait_recv()
    place_ghosts(forward_layers(landed1), code, *grid1)

    def middle(x):
        adjoint_step(mats, rate, grid1, wgrid, seeds, lam, x, final, wgrid1[0], pa, pb)

    each_x(middle)
    pack_xy(wgrid1[0], pa, pb)

    fourth[0][0] = pa[...]
    fourth[1][0] = pb[...]
    back.begin()
    back.relay()
    back.hand_on(tables, wholes)
    back.take(tables, wholes, put_halves(wa, wb))
    place_ghosts(adjoint_layers(wa, wb), code, *wgrid1)
    each_x(lambda x: adjoint_step(mats, rate, grid0, wgrid1, lam, adjoint, x))

    for copy in parts + shared + shared1:
        copy.wait_send()
    for exchange in (early, late, again, back):
        exchange.drain()


def on_device(checkpoint, seeds, cell_rate, flux_mats, owner, neighbours, orientation):
    vm, sm = pltpu.VMEM, pltpu.SMEM
    block = jax.ShapeDtypeStruct((ROWS, CZ), F32)
    quarter, whole = exchange_scratch(QA, QB), exchange_scratch(HALF, HALF)
    grid = [VMEM((NV * EXT, CZ), F32), VMEM((2 * FACE, CZ), F32), VMEM((2 * CY, CZ), F32)]
    half = VMEM((HALF, CZ), F32)
    mine, landed = VMEM((QA + QB, CZ), F32), VMEM((NC, QA + QB, CZ), F32)
    copies = 9 + 4 * N_COPIES
    adjoint, final = pl.pallas_call(
        kernel,
        out_shape=(block, block),
        in_specs=[pl.BlockSpec(memory_space=m) for m in (sm, sm, sm, sm, vm, vm, vm)],
        out_specs=(pl.BlockSpec(memory_space=vm), pl.BlockSpec(memory_space=vm)),
        scratch_shapes=quarter * 2
        + whole * 2
        + grid * 4
        + [half, half, mine, mine, VMEM((NC, ROWS // NC, CZ), F32), landed, landed, half, half]
        + [VMEM((ROWS, CZ), F32)]
        + [pltpu.SemaphoreType.DMA((copies,)), pltpu.SemaphoreType.DMA((copies,))],
        compiler_params=pltpu.CompilerParams(collective_id=0, has_side_effects=True),
    )(
        owner,
        neighbours,
        orientation,
        flux_mats,
        checkpoint.reshape(ROWS // NC, CZ),
        seeds.reshape(ROWS, CZ),
        cell_rate.reshape(CX * CY, CZ),
    )
    return (
        adjoint.reshape(1, 1, NV, CX, CY, CZ),
        final.reshape(1, NV, CX, CY, CZ),
    )


def solution(mesh):
    return jax.shard_map(
        on_device,
        mesh=mesh,
        in_specs=(
            P("space", None, "ckpt", None, None),
            P("ckpt", "space", None, None, None, None),
            P("space", None, None, None),
            P(),
            P(),
            P(),
            P(),
        ),
        out_specs=(P("ckpt", "space", None, None, None, None), P("space", None, None, None, None)),
        check_vma=False,
    )
```

```python
import jax
import jax.numpy as jnp
from jax import lax
from jax.experimental import pallas as pl
from jax.experimental.pallas import tpu as pltpu
from jax.sharding import PartitionSpec as P

MESH = pl.DeviceIdType.MESH
VMEM = pltpu.VMEM
F32 = jnp.float32

NX, NY, NZ, NC = 4, 4, 2, 4
NV, CX, CY, CZ = 6, 16, 16, 128
ROWS = NV * CX * CY
FACE = NV * CX
EXT = (CX + 2) * CY
TAU = 0.05
DAMP = 0.015
HALF = 2 * FACE + CY
QROW = FACE // NC
QA, QB = 2 * QROW + 8, 2 * QROW
SEGS = ((0, FACE), (FACE, FACE), (2 * FACE, CY))
SEGS_QA = ((0, QROW), (QROW, QROW), (2 * QROW, 8))
SEGS_QB = ((0, QROW), (QROW, QROW))
STRIP = CX // NC
QX = 2 * QROW + CY
SEGS_QX = ((0, QROW), (QROW, QROW), (2 * QROW, CY))


def lanes(shape):
    return lax.broadcasted_iota(jnp.int32, shape, len(shape) - 1)


def rows_of(start, count, step=16):
    return pl.ds(pl.multiple_of(start, step), count)


def cell_rows(v, x):
    return rows_of(v * EXT + (x + 1) * CY, CY)


def pack_xy(ext, pa, pb):
    for seg, x in ((0, CX - 1), (FACE, 0)):
        for v in range(NV):
            pa[pl.ds(seg + v * 16, 16), :] = ext[pl.ds(v * EXT + (x + 1) * CY, CY), :]
    for seg, y in ((0, CY - 1), (FACE, 0)):
        for v in range(NV):
            pb[pl.ds(seg + v * 16, 16), :] = ext[pl.ds(v * EXT + CY + y, CX, stride=CY), :]


def pack_z(values, x, pa, pb):
    lane = lanes((CY, CZ))
    up = pa[pl.ds(2 * FACE, CY), :]
    low = pb[pl.ds(2 * FACE, CY), :]
    for v in range(NV):
        at = v * 16 + x
        here = lane == at
        up = jnp.where(here, pltpu.roll(values[v], at + 1, 1), up)
        low = jnp.where(here, pltpu.roll(values[v], at, 1), low)
    pa[pl.ds(2 * FACE, CY), :] = up
    pb[pl.ds(2 * FACE, CY), :] = low


def clear_z(pa, pb):
    pa[pl.ds(2 * FACE, CY), :] = jnp.zeros((CY, CZ), F32)
    pb[pl.ds(2 * FACE, CY), :] = jnp.zeros((CY, CZ), F32)


def lane_flip(piece, flag, width):
    lane = lanes(piece.shape)
    at = lane & (width - 1)
    return jnp.take_along_axis(piece, lane + flag * (width - 1 - 2 * at), axis=1)


def row_flip(piece, flag):
    row = lax.broadcasted_iota(jnp.int32, (8, CZ), 0)
    index = row + flag * (7 - 2 * row)
    first, second = piece[:8], piece[8:]
    turned = flag == 1
    lower = jnp.where(turned, second, first)
    upper = jnp.where(turned, first, second)
    return [jnp.take_along_axis(lower, index, axis=0), jnp.take_along_axis(upper, index, axis=0)]


def place_ghosts(layer, code, ext, gy, gz):
    for f in range(6):
        first, second = code[f] & 1, (code[f] >> 1) & 1
        if f < 4:
            for v in range(NV):
                for h, piece in enumerate(row_flip(layer(f, v), first)):
                    piece = lane_flip(piece, second, CZ)
                    if f < 2:
                        start = v * EXT + ((CX + 1) * CY if f == 0 else 0)
                        ext[pl.ds(start + 8 * h, 8), :] = piece
                    else:
                        gy[pl.ds((f - 2) * FACE + v * 16 + 8 * h, 8), :] = piece
        else:
            for h, piece in enumerate(row_flip(layer(f, 0), second)):
                gz[pl.ds((f - 4) * CY + 8 * h, 8), :] = lane_flip(piece, first, CX)


def forward_layers(ghost):
    def face(f):
        start = {1: 0, 0: QROW, 3: QA, 2: QA + QROW}[f]
        return jnp.concatenate([ghost[c, pl.ds(start, QROW), :] for c in range(NC)])

    faces = {f: face(f) for f in range(4)}

    def layer(f, v):
        if f < 4:
            return faces[f][v * 16 : v * 16 + 16]
        c = 0 if f == 5 else 2
        return jnp.concatenate([ghost[c, pl.ds(2 * QROW, 8), :], ghost[c + 1, pl.ds(2 * QROW, 8), :]])

    return layer


def strip_layers(ghost):
    lane = lanes((CY, CZ))

    def layer(f, v):
        if f < 2:
            start = (1 - f) * QROW
            rows = range(v * 16, v * 16 + 16, 8)
            return jnp.concatenate(
                [ghost[r // QROW, pl.ds(start + r % QROW, 8), :] for r in rows]
            )
        if f < 4:
            start = QX + (3 - f) * QROW + v * STRIP
            return jnp.concatenate([ghost[c, pl.ds(start, STRIP), :] for c in range(NC)])
        start = 2 * QROW if f == 5 else QX + 2 * QROW
        out = ghost[0, pl.ds(start, CY), :]
        for c in range(1, NC):
            out = jnp.where((lane & 15) // STRIP == c, ghost[c, pl.ds(start, CY), :], out)
        return out

    return layer


def pack_strip(part, c, xface, ba, bb):
    lane = lanes((CY, CZ))
    for seg, y in ((0, CY - 1), (QROW, 0)):
        for v in range(NV):
            bb[0, pl.ds(seg + v * STRIP, STRIP), :] = part[pl.ds(v * 64 + y, STRIP, stride=CY), :]
    up = jnp.zeros((CY, CZ), F32)
    low = jnp.zeros((CY, CZ), F32)
    for v in range(NV):
        for x in range(STRIP):
            value = part[pl.ds(v * 64 + x * CY, CY), :]
            at = v * 16 + c * STRIP + x
            here = lane == at
            up = jnp.where(here, pltpu.roll(value, at + 1, 1), up)
            low = jnp.where(here, pltpu.roll(value, at, 1), low)
            if x == STRIP - 1:
                xface[0, pl.ds(v * 16, 16), :] = value
            if x == 0:
                xface[1, pl.ds(v * 16, 16), :] = value
    ba[0, pl.ds(2 * QROW, CY), :] = up
    bb[0, pl.ds(2 * QROW, CY), :] = low


class EndLayers:
    def __init__(self, place, xface, share, send, recv, base):
        self.place, self.xface, self.share = place, xface, share
        self.send, self.recv, self.base = send, recv, base

    def copy(self, n, who, member):
        return pltpu.make_async_remote_copy(
            src_ref=self.xface.at[n, pl.ds(member * QROW, QROW)],
            dst_ref=self.share.at[n],
            send_sem=self.send.at[self.base + n * NC + member],
            recv_sem=self.recv.at[self.base + n],
            device_id=(member, lax.axis_index("space")),
            device_id_type=MESH,
        )

    def each(self, holder, other):
        for n, who in ((0, NC - 1), (1, 0)):
            members = [m for m in range(NC) if m != who]
            if holder is not None:

                @pl.when(self.place.c == who)
                def _():
                    holder(n, who, members)

            if other is not None:

                @pl.when(self.place.c != who)
                def _():
                    other(n, who, members)

    def begin(self):
        def give(n, who, members):
            for m in members:
                self.copy(n, who, m).start()
            self.share[n] = self.xface[n, pl.ds(who * QROW, QROW), :]

        self.each(give, None)

    def take(self):
        self.each(None, lambda n, who, members: self.copy(n, who, members[0]).wait_recv())

    def drain(self):
        self.each(lambda n, who, members: [self.copy(n, who, m).wait_send() for m in members], None)


class Gather:
    def __init__(self, place, part, stored, send, recv, base):
        self.place, self.part, self.stored = place, part, stored
        self.send, self.recv, self.base = send, recv, base
        self.all = []

    def copy(self, src, slot, member):
        n = self.base + len(self.all)
        made = pltpu.make_async_remote_copy(
            src_ref=src,
            dst_ref=self.stored.at[slot],
            send_sem=self.send.at[n],
            recv_sem=self.recv.at[n],
            device_id=(member, lax.axis_index("space")),
            device_id_type=MESH,
        )
        made.start()
        self.all.append(made)

    def begin(self):
        c = self.place.c
        self.core = c + 1 - 2 * lax.rem(c, 2)
        self.far = lax.rem(c + 2, NC)
        self.copy(self.part, c, self.far)
        self.copy(self.part, c, self.core)
        self.stored[c] = self.part[...]

    def relay(self):
        self.all[0].wait_recv()
        self.copy(self.stored.at[self.far], self.far, self.core)

    def take(self):
        for made in self.all[1:]:
            made.wait_recv()

    def drain(self):
        for made in self.all:
            made.wait_send()


def adjoint_layers(ga, gb):
    def layer(f, v):
        half = ga if f in (0, 1, 5) else gb
        if f < 4:
            return half[pl.ds((1 - f % 2) * FACE + v * 16, 16), :]
        return half[pl.ds(2 * FACE, CY), :]

    return layer


def neighbours_of(grid, x):
    ext, gy, gz = grid
    row = lax.broadcasted_iota(jnp.int32, (CY, CZ), 0)
    lane = lanes((CY, CZ))
    centre = [ext[cell_rows(v, x), :] for v in range(NV)]

    def at(direction):
        ups, lows = [], []
        for v in range(NV):
            u = centre[v]
            at_x = v * 16 + x
            if direction == 0:
                up = ext[cell_rows(v, x + 1), :]
                low = ext[cell_rows(v, x - 1), :]
            elif direction == 1:
                up = jnp.where(row == CY - 1, gy[pl.ds(at_x, 1), :], pltpu.roll(u, CY - 1, 0))
                low = jnp.where(row == 0, gy[pl.ds(FACE + at_x, 1), :], pltpu.roll(u, 1, 0))
            else:
                high = pltpu.roll(gz[pl.ds(0, CY), :], CZ - 1 - at_x, 1)
                deep = pltpu.roll(gz[pl.ds(CY, CY), :], lax.rem(CZ - at_x, CZ), 1)
                up = jnp.where(lane == CZ - 1, high, pltpu.roll(u, CZ - 1, 1))
                low = jnp.where(lane == 0, deep, pltpu.roll(u, 1, 1))
            ups.append(up)
            lows.append(low)
        return ups, lows

    return centre, at


def spread_of(first, second):
    mean = 0.5 * (first + second)
    t = 1.0 + mean * mean
    r = lax.rsqrt(t)
    return t * r, mean * r


def forward_step(mats, rate, grid, out, pa, pb, x):
    u, at = neighbours_of(grid, x)
    total = [jnp.zeros((CY, CZ), F32) for _ in range(NV)]
    for d in range(3):
        up, low = at(d)
        su, _ = spread_of(up[0], u[0])
        sl, _ = spread_of(u[0], low[0])
        diff = [up[v] - low[v] for v in range(NV)]
        for i in range(NV):
            acc = total[i] - (su * (up[i] - u[i]) - sl * (u[i] - low[i]))
            for j in range(NV):
                acc = acc + mats[d, i, j] * diff[j]
            total[i] = acc
    tau = (0.5 * TAU) * rate[rows_of(x * CY, CY), :]
    new = [u[v] - tau * total[v] - DAMP * jnp.tanh(u[v]) for v in range(NV)]
    for v in range(NV):
        out[cell_rows(v, x), :] = new[v]
    pack_z(new, x, pa, pb)


def adjoint_step(mats, rate, grid, wgrid, lam, out, x, final=None, weighted=None, pa=None, pb=None):
    u, at_u = neighbours_of(grid, x)
    w, at_w = neighbours_of(wgrid, x)
    total = [jnp.zeros((CY, CZ), F32) for _ in range(NV)]
    flux = [jnp.zeros((CY, CZ), F32) for _ in range(NV)]
    tilt = jnp.zeros((CY, CZ), F32)
    for d in range(3):
        up, low = at_u(d)
        wup, wlow = at_w(d)
        su, ru = spread_of(up[0], u[0])
        sl, rl = spread_of(u[0], low[0])
        dot_u = jnp.zeros((CY, CZ), F32)
        dot_l = jnp.zeros((CY, CZ), F32)
        diff = []
        wdiff = []
        for i in range(NV):
            du, dl = up[i] - u[i], u[i] - low[i]
            gu, gl = wup[i] - w[i], w[i] - wlow[i]
            dot_u = dot_u + du * gu
            dot_l = dot_l + dl * gl
            total[i] = total[i] + (su * gu - sl * gl)
            wdiff.append(wup[i] - wlow[i])
            if final is not None:
                flux[i] = flux[i] - (su * du - sl * dl)
                diff.append(up[i] - low[i])
        tilt = tilt + ru * dot_u + rl * dot_l
        for i in range(NV):
            acc = total[i]
            for j in range(NV):
                acc = acc + mats[d, j, i] * wdiff[j]
            total[i] = acc
        if final is not None:
            for i in range(NV):
                acc = flux[i]
                for j in range(NV):
                    acc = acc + mats[d, i, j] * diff[j]
                flux[i] = acc
    tau = TAU * rate[rows_of(x * CY, CY), :]
    packed = []
    for v in range(NV):
        here = rows_of(v * 256 + x * CY, CY)
        bent = jnp.tanh(u[v])
        old = lam[here, :]
        new = old - DAMP * (1.0 - bent * bent) * old + 0.5 * total[v]
        if v == 0:
            new = new - 0.25 * tilt
        out[here, :] = new
        if final is not None:
            final[here, :] = u[v] - (0.5 * tau) * flux[v] - DAMP * bent
            packed.append(tau * new)
            weighted[cell_rows(v, x), :] = packed[v]
    if final is not None:
        pack_z(packed, x, pa, pb)


def each_x(step, start=0, stop=CX):
    def body(x, carry):
        step(x)
        return carry

    lax.fori_loop(start, stop, body, 0)


class Place:
    def __init__(self):
        self.c = lax.axis_index("ckpt")
        s = lax.axis_index("space")
        self.z = lax.rem(s, NZ)
        self.x = lax.rem(lax.div(s, NZ), NX)
        self.y = lax.div(s, NZ * NX)

    def space(self, x, y, z):
        return (y * NX + x) * NZ + z

    def along_x(self, k):
        return (self.c, self.space(lax.rem(self.x + k, NX), self.y, self.z))

    def along_y(self, k):
        return (self.c, self.space(self.x, lax.rem(self.y + k, NY), self.z))

    def across_z(self):
        return (self.c, self.space(self.x, self.y, 1 - self.z))

    def member(self, k):
        return (lax.rem(self.c + k, NC), lax.axis_index("space"))


def greet(place, members):
    barrier = pltpu.get_barrier_semaphore()
    partners = [place.across_z()]
    partners += [place.along_x(k) for k in range(1, NX)]
    partners += [place.along_y(k) for k in range(1, NY)]
    if members:
        partners += [place.member(k) for k in range(1, NC)]
    for partner in partners:
        pl.semaphore_signal(barrier, inc=1, device_id=partner, device_id_type=MESH)
    return lambda: pl.semaphore_wait(barrier, len(partners))


class Tables:
    def __init__(self, place, owner, links):
        self.place = place
        spots = [place.space(place.x, lax.rem(place.y + k, NY), place.z) for k in range(NY)]
        spots += [place.space(lax.rem(place.x + k, NX), place.y, place.z) for k in range(1, NX)]

        def find(b, found):
            who = owner[b]
            return tuple(jnp.where(who == s, b, f) for f, s in zip(found, spots))

        blocks = lax.fori_loop(0, NX * NY * NZ, find, tuple(jnp.int32(0) for _ in spots))
        self.own = blocks[0]
        self.down = {"A": list(blocks[:NY]), "B": [blocks[0]] + list(blocks[NY:])}
        self.owner, self.links = owner, links

    def source(self, block, layer):
        s = self.owner[self.links[layer ^ 1, block]]
        return lax.rem(lax.div(s, NZ), NX), lax.div(s, NZ * NX), lax.rem(s, NZ)

    def slot(self, half, k, layer):
        x, y, z = self.source(self.down[half][k], layer)
        turn = jnp.where(z == self.place.z, 0, 1)
        if half == "A":
            return turn * NX + lax.rem(self.place.x - x + NX, NX)
        return turn * NY + lax.rem(self.place.y - y + NY, NY)

    def last(self, half, layer):
        x, y, _ = self.source(self.own, layer)
        if half == "A":
            return lax.rem(self.place.y - y + NY, NY)
        return lax.rem(self.place.x - x + NX, NX)


RING = NX
HOPS = (2, 1, 3)
N_COPIES = 2 + 6 * len(HOPS)


class Exchange:
    def __init__(self, place, bufs, outs, arrivals, send, recv, base):
        self.place, self.bufs, self.outs, self.arrivals = place, bufs, outs, arrivals
        self.send, self.recv, self.base = send, recv, base
        self.all = []
        self.first = {"A": place.along_x, "B": place.along_y}
        self.second = {"A": place.along_y, "B": place.along_x}
        self.across, self.own, self.passed, self.final = {}, {}, {}, {}

    def copy(self, src, dst, device):
        n = self.base + len(self.all)
        made = pltpu.make_async_remote_copy(
            src_ref=src,
            dst_ref=dst,
            send_sem=self.send.at[n],
            recv_sem=self.recv.at[n],
            device_id=device,
            device_id_type=MESH,
        )
        made.start()
        self.all.append(made)
        return made

    def send_across(self, halves="AB"):
        for half in halves:
            buf = self.bufs[half]
            self.across[half] = self.copy(buf.at[0], buf.at[RING], self.place.across_z())

    def send_own(self, halves="AB"):
        for half in halves:
            self.own[half] = []
        for k in HOPS:
            for half in halves:
                buf = self.bufs[half]
                self.own[half].append(self.copy(buf.at[0], buf.at[k], self.first[half](k)))

    def relay(self):
        self.passed = {"A": [], "B": []}
        for half in "AB":
            self.across[half].wait_recv()
        for k in HOPS:
            for half in "AB":
                buf = self.bufs[half]
                self.passed[half].append(self.copy(buf.at[RING], buf.at[RING + k], self.first[half](k)))

    def hand_on(self, tables, segments):
        self.final = {"A": [], "B": []}
        for half in "AB":
            for made in self.own[half] + self.passed[half]:
                made.wait_recv()
            buf, out, arrive = self.bufs[half], self.outs[half], self.arrivals[half]
            for k in HOPS + (0,):
                for start, count, layer in segments[half]:
                    picked = buf[tables.slot(half, k, layer), pl.ds(start, count), :]
                    if k == 0:
                        arrive[0, pl.ds(start, count), :] = picked
                    else:
                        out[k - 1, pl.ds(start, count), :] = picked
                if k:
                    self.final[half].append(
                        self.copy(out.at[k - 1], arrive.at[k], self.second[half](k))
                    )

    def take(self, tables, segments, put):
        for half in "AB":
            for made in self.final[half]:
                made.wait_recv()
            for start, count, layer in segments[half]:
                put(half, start, count, self.arrivals[half][tables.last(half, layer), pl.ds(start, count), :])

    def drain(self):
        for made in self.all:
            made.wait_send()


def full_segments():
    return {
        "A": [(s, n, f) for (s, n), f in zip(SEGS, (0, 1, 4))],
        "B": [(s, n, f) for (s, n), f in zip(SEGS, (2, 3, 5))],
    }


def quarter_segments(c):
    zface = jnp.where(c < 2, 4, 5)
    return {
        "A": [(s, n, f) for (s, n), f in zip(SEGS_QA, (0, 1, zface))],
        "B": [(s, n, f) for (s, n), f in zip(SEGS_QB, (2, 3))],
    }


def strip_segments():
    return {
        "A": [(s, n, f) for (s, n), f in zip(SEGS_QX, (0, 1, 4))],
        "B": [(s, n, f) for (s, n), f in zip(SEGS_QX, (2, 3, 5))],
    }


def exchange_scratch(ra, rb):
    return [
        VMEM((2 * RING, ra, CZ), F32),
        VMEM((2 * RING, rb, CZ), F32),
        VMEM((RING - 1, ra, CZ), F32),
        VMEM((RING - 1, rb, CZ), F32),
        VMEM((RING, ra, CZ), F32),
        VMEM((RING, rb, CZ), F32),
    ]


def exchange_of(place, scratch, send, recv, base):
    ba, bb, oa, ob, ra, rb = scratch
    return Exchange(place, {"A": ba, "B": bb}, {"A": oa, "B": ob}, {"A": ra, "B": rb}, send, recv, base)


def quarter_packet(c, pa, pb, ba, bb):
    part = rows_of(c * QROW, QROW, 8)
    part2 = rows_of(FACE + c * QROW, QROW, 8)
    ba[0, pl.ds(0, QROW), :] = pa[part, :]
    ba[0, pl.ds(QROW, QROW), :] = pa[part2, :]
    bb[0, pl.ds(0, QROW), :] = pb[part, :]
    bb[0, pl.ds(QROW, QROW), :] = pb[part2, :]
    zrows = rows_of(2 * FACE + lax.rem(c, 2) * 8, 8, 8)
    ba[0, pl.ds(2 * QROW, 8), :] = jnp.where(c < 2, pa[zrows, :], pb[zrows, :])


def share(place, mine, ghost, send, recv, base):
    made = []
    for k in range(1, NC):
        copy = pltpu.make_async_remote_copy(
            src_ref=mine,
            dst_ref=ghost.at[place.c],
            send_sem=send.at[base + k - 1],
            recv_sem=recv.at[base + k - 1],
            device_id=place.member(k),
            device_id_type=MESH,
        )
        copy.start()
        made.append(copy)
    ghost[place.c] = mine[...]
    return made


def put_into(mine, second):
    def put(half, start, count, value):
        mine[pl.ds((0 if half == "A" else second) + start, count), :] = value

    return put


def put_halves(wa, wb):
    def put(half, start, count, value):
        (wa if half == "A" else wb)[pl.ds(start, count), :] = value

    return put


def kernel(owner, links, codes, mats, part, seeds, rate, adjoint, final, *scratch):
    first, second = scratch[0:6], scratch[6:12]
    third, fourth = scratch[12:18], scratch[18:24]
    grid0, grid1, wgrid, wgrid1 = (scratch[24 + 3 * n : 27 + 3 * n] for n in range(4))
    pa, pb, mine, mine1, stored, landed, landed1, wa, wb, lam, xface, xshare, send, recv = scratch[36:]
    place = Place()
    early = exchange_of(place, first, send, recv, 0)
    late = exchange_of(place, third, send, recv, N_COPIES)
    again = exchange_of(place, second, send, recv, 2 * N_COPIES)
    back = exchange_of(place, fourth, send, recv, 3 * N_COPIES)
    base = 4 * N_COPIES
    gather = Gather(place, part, stored, send, recv, base + 6)
    ends = EndLayers(place, xface, xshare, send, recv, base + 9)
    strips, quarters, wholes = strip_segments(), quarter_segments(place.c), full_segments()

    met = greet(place, True)
    pack_strip(part, place.c, xface, first[0], first[1])
    met()
    ends.begin()
    early.send_across("B")
    early.send_own("B")
    ends.take()
    for n in range(2):
        first[0][0, pl.ds(n * QROW, QROW), :] = xshare[n]
    early.send_across("A")
    early.send_own("A")
    gather.begin()

    clear_z(pa, pb)

    def weigh(x):
        tau = TAU * rate[rows_of(x * CY, CY), :]
        values = [seeds[rows_of(v * 256 + x * CY, CY), :] * tau for v in range(NV)]
        for v in range(NV):
            wgrid[0][cell_rows(v, x), :] = values[v]
        pack_z(values, x, pa, pb)

    each_x(weigh)
    pack_xy(wgrid[0], pa, pb)
    third[0][0] = pa[...]
    third[1][0] = pb[...]
    early.relay()
    late.send_across()
    tables = Tables(place, owner, links)
    code = [codes[f, tables.own] for f in range(6)]
    gather.relay()
    early.hand_on(tables, strips)
    late.send_own()
    early.take(tables, strips, put_into(mine, QX))
    shared = share(place, mine, landed, send, recv, base)
    gather.take()
    span = CX * CY // NC
    for c in range(NC):
        for v in range(NV):
            grid0[0][pl.ds(v * EXT + CY + c * span, span), :] = stored[c, pl.ds(v * span, span), :]
    clear_z(pa, pb)
    late.relay()
    for copy in shared:
        copy.wait_recv()
    place_ghosts(strip_layers(landed), code, *grid0)

    each_x(lambda x: forward_step(mats, rate, grid0, grid1[0], pa, pb, x))
    pack_xy(grid1[0], pa, pb)

    quarter_packet(place.c, pa, pb, second[0], second[1])
    again.send_across()
    again.send_own()
    again.relay()
    late.hand_on(tables, wholes)
    again.hand_on(tables, quarters)
    again.take(tables, quarters, put_into(mine1, QA))
    shared1 = share(place, mine1, landed1, send, recv, base + 3)
    late.take(tables, wholes, put_halves(wa, wb))
    place_ghosts(adjoint_layers(wa, wb), code, *wgrid)
    clear_z(pa, pb)
    for copy in shared1:
        copy.wait_recv()
    place_ghosts(forward_layers(landed1), code, *grid1)

    def middle(x):
        adjoint_step(mats, rate, grid1, wgrid, seeds, lam, x, final, wgrid1[0], pa, pb)

    each_x(middle)
    pack_xy(wgrid1[0], pa, pb)

    fourth[0][0] = pa[...]
    fourth[1][0] = pb[...]
    back.send_across()
    back.send_own()
    back.relay()
    back.hand_on(tables, wholes)
    back.take(tables, wholes, put_halves(wa, wb))
    place_ghosts(adjoint_layers(wa, wb), code, *wgrid1)
    each_x(lambda x: adjoint_step(mats, rate, grid0, wgrid1, lam, adjoint, x))

    for copy in shared + shared1:
        copy.wait_send()
    ends.drain()
    for exchange in (gather, early, late, again, back):
        exchange.drain()


def on_device(checkpoint, seeds, cell_rate, flux_mats, owner, neighbours, orientation):
    vm, sm = pltpu.VMEM, pltpu.SMEM
    block = jax.ShapeDtypeStruct((ROWS, CZ), F32)
    strip, quarter = exchange_scratch(QX, QX), exchange_scratch(QA, QB)
    whole = exchange_scratch(HALF, HALF)
    grid = [VMEM((NV * EXT, CZ), F32), VMEM((2 * FACE, CZ), F32), VMEM((2 * CY, CZ), F32)]
    half = VMEM((HALF, CZ), F32)
    copies = 17 + 4 * N_COPIES
    adjoint, final = pl.pallas_call(
        kernel,
        out_shape=(block, block),
        in_specs=[pl.BlockSpec(memory_space=m) for m in (sm, sm, sm, sm, vm, vm, vm)],
        out_specs=(pl.BlockSpec(memory_space=vm), pl.BlockSpec(memory_space=vm)),
        scratch_shapes=strip
        + quarter
        + whole * 2
        + grid * 4
        + [half, half, VMEM((2 * QX, CZ), F32), VMEM((QA + QB, CZ), F32)]
        + [VMEM((NC, ROWS // NC, CZ), F32)]
        + [VMEM((NC, 2 * QX, CZ), F32), VMEM((NC, QA + QB, CZ), F32), half, half]
        + [VMEM((ROWS, CZ), F32), VMEM((2, FACE, CZ), F32), VMEM((2, QROW, CZ), F32)]
        + [pltpu.SemaphoreType.DMA((copies,)), pltpu.SemaphoreType.DMA((copies,))],
        compiler_params=pltpu.CompilerParams(collective_id=0, has_side_effects=True),
    )(
        owner,
        neighbours.T,
        orientation.T,
        flux_mats,
        checkpoint.reshape(ROWS // NC, CZ),
        seeds.reshape(ROWS, CZ),
        cell_rate.reshape(CX * CY, CZ),
    )
    return (
        adjoint.reshape(1, 1, NV, CX, CY, CZ),
        final.reshape(1, NV, CX, CY, CZ),
    )


def solution(mesh):
    return jax.shard_map(
        on_device,
        mesh=mesh,
        in_specs=(
            P("space", None, "ckpt", None, None),
            P("ckpt", "space", None, None, None, None),
            P("space", None, None, None),
            P(),
            P(),
            P(),
            P(),
        ),
        out_specs=(P("ckpt", "space", None, None, None, None), P("space", None, None, None, None)),
        check_vma=False,
    )
```

```python
import jax
import jax.numpy as jnp
from jax import lax
from jax.experimental import pallas as pl
from jax.experimental.pallas import tpu as pltpu
from jax.sharding import PartitionSpec as P

MESH = pl.DeviceIdType.MESH
VMEM = pltpu.VMEM
F32 = jnp.float32

NX, NY, NZ, NC = 4, 4, 2, 4
NV, CX, CY, CZ = 6, 16, 16, 128
ROWS = NV * CX * CY
FACE = NV * CX
EXT = (CX + 2) * CY
TAU = 0.05
DAMP = 0.015
HALF = 2 * FACE + CY
QROW = FACE // NC
QA, QB = 2 * QROW + 8, 2 * QROW
SEGS = ((0, FACE), (FACE, FACE), (2 * FACE, CY))
SEGS_QA = ((0, QROW), (QROW, QROW), (2 * QROW, 8))
SEGS_QB = ((0, QROW), (QROW, QROW))
STRIP = CX // NC
QX = 2 * QROW + CY
SEGS_QX = ((0, QROW), (QROW, QROW), (2 * QROW, CY))


def lanes(shape):
    return lax.broadcasted_iota(jnp.int32, shape, len(shape) - 1)


def rows_of(start, count, step=16):
    return pl.ds(pl.multiple_of(start, step), count)


def cell_rows(v, x):
    return rows_of(v * EXT + (x + 1) * CY, CY)


def pack_xy(ext, pa, pb):
    for seg, x in ((0, CX - 1), (FACE, 0)):
        for v in range(NV):
            pa[pl.ds(seg + v * 16, 16), :] = ext[pl.ds(v * EXT + (x + 1) * CY, CY), :]
    for seg, y in ((0, CY - 1), (FACE, 0)):
        for v in range(NV):
            pb[pl.ds(seg + v * 16, 16), :] = ext[pl.ds(v * EXT + CY + y, CX, stride=CY), :]


def pack_z(values, x, pa, pb):
    lane = lanes((CY, CZ))
    up = pa[pl.ds(2 * FACE, CY), :]
    low = pb[pl.ds(2 * FACE, CY), :]
    for v in range(NV):
        at = v * 16 + x
        here = lane == at
        up = jnp.where(here, pltpu.roll(values[v], at + 1, 1), up)
        low = jnp.where(here, pltpu.roll(values[v], at, 1), low)
    pa[pl.ds(2 * FACE, CY), :] = up
    pb[pl.ds(2 * FACE, CY), :] = low


def clear_z(pa, pb):
    pa[pl.ds(2 * FACE, CY), :] = jnp.zeros((CY, CZ), F32)
    pb[pl.ds(2 * FACE, CY), :] = jnp.zeros((CY, CZ), F32)


def lane_flip(piece, flag, width):
    lane = lanes(piece.shape)
    at = lane & (width - 1)
    return jnp.take_along_axis(piece, lane + flag * (width - 1 - 2 * at), axis=1)


def row_flip(piece, flag):
    row = lax.broadcasted_iota(jnp.int32, (8, CZ), 0)
    index = row + flag * (7 - 2 * row)
    first, second = piece[:8], piece[8:]
    turned = flag == 1
    lower = jnp.where(turned, second, first)
    upper = jnp.where(turned, first, second)
    return [jnp.take_along_axis(lower, index, axis=0), jnp.take_along_axis(upper, index, axis=0)]


def place_ghosts(layer, code, ext, gy, gz):
    for f in range(6):
        first, second = code[f] & 1, (code[f] >> 1) & 1
        if f < 4:
            for v in range(NV):
                for h, piece in enumerate(row_flip(layer(f, v), first)):
                    piece = lane_flip(piece, second, CZ)
                    if f < 2:
                        start = v * EXT + ((CX + 1) * CY if f == 0 else 0)
                        ext[pl.ds(start + 8 * h, 8), :] = piece
                    else:
                        gy[pl.ds((f - 2) * FACE + v * 16 + 8 * h, 8), :] = piece
        else:
            for h, piece in enumerate(row_flip(layer(f, 0), second)):
                gz[pl.ds((f - 4) * CY + 8 * h, 8), :] = lane_flip(piece, first, CX)


def forward_layers(ghost):
    def face(f):
        start = {1: 0, 0: QROW, 3: QA, 2: QA + QROW}[f]
        return jnp.concatenate([ghost[c, pl.ds(start, QROW), :] for c in range(NC)])

    faces = {f: face(f) for f in range(4)}

    def layer(f, v):
        if f < 4:
            return faces[f][v * 16 : v * 16 + 16]
        c = 0 if f == 5 else 2
        return jnp.concatenate([ghost[c, pl.ds(2 * QROW, 8), :], ghost[c + 1, pl.ds(2 * QROW, 8), :]])

    return layer


def strip_layers(ghost):
    lane = lanes((CY, CZ))

    def layer(f, v):
        if f < 2:
            start = (1 - f) * QROW
            rows = range(v * 16, v * 16 + 16, 8)
            return jnp.concatenate(
                [ghost[r // QROW, pl.ds(start + r % QROW, 8), :] for r in rows]
            )
        if f < 4:
            start = QX + (3 - f) * QROW + v * STRIP
            return jnp.concatenate([ghost[c, pl.ds(start, STRIP), :] for c in range(NC)])
        start = 2 * QROW if f == 5 else QX + 2 * QROW
        out = ghost[0, pl.ds(start, CY), :]
        for c in range(1, NC):
            out = jnp.where((lane & 15) // STRIP == c, ghost[c, pl.ds(start, CY), :], out)
        return out

    return layer


def pack_strip(part, c, xface, ba, bb):
    lane = lanes((CY, CZ))
    for seg, y in ((0, CY - 1), (QROW, 0)):
        for v in range(NV):
            bb[0, pl.ds(seg + v * STRIP, STRIP), :] = part[pl.ds(v * 64 + y, STRIP, stride=CY), :]
    up = jnp.zeros((CY, CZ), F32)
    low = jnp.zeros((CY, CZ), F32)
    for v in range(NV):
        for x in range(STRIP):
            value = part[pl.ds(v * 64 + x * CY, CY), :]
            at = v * 16 + c * STRIP + x
            here = lane == at
            up = jnp.where(here, pltpu.roll(value, at + 1, 1), up)
            low = jnp.where(here, pltpu.roll(value, at, 1), low)
            if x == STRIP - 1:
                xface[0, pl.ds(v * 16, 16), :] = value
            if x == 0:
                xface[1, pl.ds(v * 16, 16), :] = value
    ba[0, pl.ds(2 * QROW, CY), :] = up
    bb[0, pl.ds(2 * QROW, CY), :] = low


class EndLayers:
    def __init__(self, place, xface, share, send, recv, base):
        self.place, self.xface, self.share = place, xface, share
        self.send, self.recv, self.base = send, recv, base

    def copy(self, n, who, member):
        return pltpu.make_async_remote_copy(
            src_ref=self.xface.at[n, pl.ds(member * QROW, QROW)],
            dst_ref=self.share.at[n],
            send_sem=self.send.at[self.base + n * NC + member],
            recv_sem=self.recv.at[self.base + n],
            device_id=(member, lax.axis_index("space")),
            device_id_type=MESH,
        )

    def each(self, holder, other):
        for n, who in ((0, NC - 1), (1, 0)):
            members = [m for m in range(NC) if m != who]
            if holder is not None:

                @pl.when(self.place.c == who)
                def _():
                    holder(n, who, members)

            if other is not None:

                @pl.when(self.place.c != who)
                def _():
                    other(n, who, members)

    def begin(self):
        def give(n, who, members):
            for m in members:
                self.copy(n, who, m).start()
            self.share[n] = self.xface[n, pl.ds(who * QROW, QROW), :]

        self.each(give, None)

    def take(self):
        self.each(None, lambda n, who, members: self.copy(n, who, members[0]).wait_recv())

    def drain(self):
        self.each(lambda n, who, members: [self.copy(n, who, m).wait_send() for m in members], None)


class Gather:
    def __init__(self, place, part, stored, send, recv, base):
        self.place, self.part, self.stored = place, part, stored
        self.send, self.recv, self.base = send, recv, base
        self.all = []

    def copy(self, src, slot, member):
        n = self.base + len(self.all)
        made = pltpu.make_async_remote_copy(
            src_ref=src,
            dst_ref=self.stored.at[slot],
            send_sem=self.send.at[n],
            recv_sem=self.recv.at[n],
            device_id=(member, lax.axis_index("space")),
            device_id_type=MESH,
        )
        made.start()
        self.all.append(made)

    def begin(self):
        c = self.place.c
        self.core = c + 1 - 2 * lax.rem(c, 2)
        self.far = lax.rem(c + 2, NC)
        self.copy(self.part, c, self.far)
        self.copy(self.part, c, self.core)
        self.stored[c] = self.part[...]

    def relay(self):
        self.all[0].wait_recv()
        self.copy(self.stored.at[self.far], self.far, self.core)

    def take(self):
        for made in self.all[1:]:
            made.wait_recv()

    def drain(self):
        for made in self.all:
            made.wait_send()


def adjoint_layers(ga, gb):
    def layer(f, v):
        half = ga if f in (0, 1, 5) else gb
        if f < 4:
            return half[pl.ds((1 - f % 2) * FACE + v * 16, 16), :]
        return half[pl.ds(2 * FACE, CY), :]

    return layer


def neighbours_of(grid, x):
    ext, gy, gz = grid
    row = lax.broadcasted_iota(jnp.int32, (CY, CZ), 0)
    lane = lanes((CY, CZ))
    centre = [ext[cell_rows(v, x), :] for v in range(NV)]

    def at(direction):
        ups, lows = [], []
        for v in range(NV):
            u = centre[v]
            at_x = v * 16 + x
            if direction == 0:
                up = ext[cell_rows(v, x + 1), :]
                low = ext[cell_rows(v, x - 1), :]
            elif direction == 1:
                up = jnp.where(row == CY - 1, gy[pl.ds(at_x, 1), :], pltpu.roll(u, CY - 1, 0))
                low = jnp.where(row == 0, gy[pl.ds(FACE + at_x, 1), :], pltpu.roll(u, 1, 0))
            else:
                high = pltpu.roll(gz[pl.ds(0, CY), :], CZ - 1 - at_x, 1)
                deep = pltpu.roll(gz[pl.ds(CY, CY), :], lax.rem(CZ - at_x, CZ), 1)
                up = jnp.where(lane == CZ - 1, high, pltpu.roll(u, CZ - 1, 1))
                low = jnp.where(lane == 0, deep, pltpu.roll(u, 1, 1))
            ups.append(up)
            lows.append(low)
        return ups, lows

    return centre, at


def spread_of(first, second):
    mean = 0.5 * (first + second)
    t = 1.0 + mean * mean
    r = lax.rsqrt(t)
    return t * r, mean * r


def forward_step(mats, rate, grid, out, pa, pb, x):
    u, at = neighbours_of(grid, x)
    total = [jnp.zeros((CY, CZ), F32) for _ in range(NV)]
    for d in range(3):
        up, low = at(d)
        su, _ = spread_of(up[0], u[0])
        sl, _ = spread_of(u[0], low[0])
        diff = [up[v] - low[v] for v in range(NV)]
        for i in range(NV):
            acc = total[i] - (su * (up[i] - u[i]) - sl * (u[i] - low[i]))
            for j in range(NV):
                acc = acc + mats[d, i, j] * diff[j]
            total[i] = acc
    tau = (0.5 * TAU) * rate[rows_of(x * CY, CY), :]
    new = [u[v] - tau * total[v] - DAMP * jnp.tanh(u[v]) for v in range(NV)]
    for v in range(NV):
        if pa is None:
            out[rows_of(v * 256 + x * CY, CY), :] = new[v]
        else:
            out[cell_rows(v, x), :] = new[v]
    if pa is not None:
        pack_z(new, x, pa, pb)


def adjoint_step(mats, rate, grid, wgrid, lam, out, x, weighted=None, pa=None, pb=None):
    u, at_u = neighbours_of(grid, x)
    w, at_w = neighbours_of(wgrid, x)
    total = [jnp.zeros((CY, CZ), F32) for _ in range(NV)]
    tilt = jnp.zeros((CY, CZ), F32)
    for d in range(3):
        up, low = at_u(d)
        wup, wlow = at_w(d)
        su, ru = spread_of(up[0], u[0])
        sl, rl = spread_of(u[0], low[0])
        dot_u = jnp.zeros((CY, CZ), F32)
        dot_l = jnp.zeros((CY, CZ), F32)
        wdiff = []
        for i in range(NV):
            du, dl = up[i] - u[i], u[i] - low[i]
            gu, gl = wup[i] - w[i], w[i] - wlow[i]
            dot_u = dot_u + du * gu
            dot_l = dot_l + dl * gl
            total[i] = total[i] + (su * gu - sl * gl)
            wdiff.append(wup[i] - wlow[i])
        tilt = tilt + ru * dot_u + rl * dot_l
        for i in range(NV):
            acc = total[i]
            for j in range(NV):
                acc = acc + mats[d, j, i] * wdiff[j]
            total[i] = acc
    tau = TAU * rate[rows_of(x * CY, CY), :]
    packed = []
    for v in range(NV):
        here = rows_of(v * 256 + x * CY, CY)
        bent = jnp.tanh(u[v])
        old = lam[here, :]
        new = old - DAMP * (1.0 - bent * bent) * old + 0.5 * total[v]
        if v == 0:
            new = new - 0.25 * tilt
        out[here, :] = new
        if weighted is not None:
            packed.append(tau * new)
            weighted[cell_rows(v, x), :] = packed[v]
    if weighted is not None:
        pack_z(packed, x, pa, pb)


def each_x(step, start=0, stop=CX):
    def body(x, carry):
        step(x)
        return carry

    lax.fori_loop(start, stop, body, 0)


class Place:
    def __init__(self):
        self.c = lax.axis_index("ckpt")
        s = lax.axis_index("space")
        self.z = lax.rem(s, NZ)
        self.x = lax.rem(lax.div(s, NZ), NX)
        self.y = lax.div(s, NZ * NX)

    def space(self, x, y, z):
        return (y * NX + x) * NZ + z

    def along_x(self, k):
        return (self.c, self.space(lax.rem(self.x + k, NX), self.y, self.z))

    def along_y(self, k):
        return (self.c, self.space(self.x, lax.rem(self.y + k, NY), self.z))

    def across_z(self):
        return (self.c, self.space(self.x, self.y, 1 - self.z))

    def member(self, k):
        return (lax.rem(self.c + k, NC), lax.axis_index("space"))


def greet(place, members):
    barrier = pltpu.get_barrier_semaphore()
    partners = [place.across_z()]
    partners += [place.along_x(k) for k in range(1, NX)]
    partners += [place.along_y(k) for k in range(1, NY)]
    if members:
        partners += [place.member(k) for k in range(1, NC)]
    for partner in partners:
        pl.semaphore_signal(barrier, inc=1, device_id=partner, device_id_type=MESH)
    return lambda: pl.semaphore_wait(barrier, len(partners))


class Tables:
    def __init__(self, place, owner, links):
        self.place = place
        spots = [place.space(place.x, lax.rem(place.y + k, NY), place.z) for k in range(NY)]
        spots += [place.space(lax.rem(place.x + k, NX), place.y, place.z) for k in range(1, NX)]

        def find(b, found):
            who = owner[b]
            return tuple(jnp.where(who == s, b, f) for f, s in zip(found, spots))

        blocks = lax.fori_loop(0, NX * NY * NZ, find, tuple(jnp.int32(0) for _ in spots))
        self.own = blocks[0]
        self.down = {"A": list(blocks[:NY]), "B": [blocks[0]] + list(blocks[NY:])}
        self.owner, self.links = owner, links

    def source(self, block, layer):
        s = self.owner[self.links[layer ^ 1, block]]
        return lax.rem(lax.div(s, NZ), NX), lax.div(s, NZ * NX), lax.rem(s, NZ)

    def slot(self, half, k, layer):
        x, y, z = self.source(self.down[half][k], layer)
        turn = jnp.where(z == self.place.z, 0, 1)
        if half == "A":
            return turn * NX + lax.rem(self.place.x - x + NX, NX)
        return turn * NY + lax.rem(self.place.y - y + NY, NY)

    def last(self, half, layer):
        x, y, _ = self.source(self.own, layer)
        if half == "A":
            return lax.rem(self.place.y - y + NY, NY)
        return lax.rem(self.place.x - x + NX, NX)


RING = NX
HOPS = (2, 1, 3)
N_COPIES = 1 + 3 * len(HOPS)


class Exchange:
    def __init__(self, place, parts, scratch, send, recv, base):
        self.place, self.parts = place, parts
        self.bufs, self.outs, self.arrivals = (
            dict(zip(parts, scratch[n::3])) for n in range(3)
        )
        self.send, self.recv, self.base = send, recv, base
        self.all = []
        self.first = {"A": place.along_x, "B": place.along_y}
        self.second = {"A": place.along_y, "B": place.along_x}
        self.across = {}
        self.own = {part: [] for part in parts}
        self.passed = {part: [] for part in parts}
        self.final = {part: [] for part in parts}

    def copy(self, src, dst, device):
        n = self.base + len(self.all)
        made = pltpu.make_async_remote_copy(
            src_ref=src,
            dst_ref=dst,
            send_sem=self.send.at[n],
            recv_sem=self.recv.at[n],
            device_id=device,
            device_id_type=MESH,
        )
        made.start()
        self.all.append(made)
        return made

    def send_across(self, parts=None):
        for part in parts or self.parts:
            buf = self.bufs[part]
            self.across[part] = self.copy(buf.at[0], buf.at[RING], self.place.across_z())

    def send_own(self, parts=None):
        for part in parts or self.parts:
            buf, away = self.bufs[part], self.first[part[0]]
            for k in HOPS:
                self.own[part].append(self.copy(buf.at[0], buf.at[k], away(k)))

    def relay(self):
        for part in self.parts:
            buf, away = self.bufs[part], self.first[part[0]]
            self.across[part].wait_recv()
            for k in HOPS:
                self.passed[part].append(self.copy(buf.at[RING], buf.at[RING + k], away(k)))

    def hand_on(self, tables, segments):
        for part in self.parts:
            for made in self.own[part] + self.passed[part]:
                made.wait_recv()
            buf, out, arrive = self.bufs[part], self.outs[part], self.arrivals[part]
            for k in HOPS + (0,):
                for start, count, layer in segments[part]:
                    picked = buf[tables.slot(part[0], k, layer), pl.ds(start, count), :]
                    if k == 0:
                        arrive[0, pl.ds(start, count), :] = picked
                    else:
                        out[k - 1, pl.ds(start, count), :] = picked
                if k:
                    self.final[part].append(
                        self.copy(out.at[k - 1], arrive.at[k], self.second[part[0]](k))
                    )

    def take(self, tables, segments, put):
        for part in self.parts:
            for made in self.final[part]:
                made.wait_recv()
            arrive = self.arrivals[part]
            for start, count, layer in segments[part]:
                put(part, start, count, arrive[tables.last(part[0], layer), pl.ds(start, count), :])

    def drain(self):
        for made in self.all:
            made.wait_send()


WHOLES = ("A1", "B1", "A2", "B2")
BIG = FACE + CY


def full_segments():
    return {
        "A1": [(0, FACE, 0), (FACE, CY, 4)],
        "B1": [(0, FACE, 2), (FACE, CY, 5)],
        "A2": [(0, FACE, 1)],
        "B2": [(0, FACE, 3)],
    }


def whole_packet(pa, pb, exchange):
    for source, name in ((pa, "A"), (pb, "B")):
        one, two = exchange.bufs[name + "1"], exchange.bufs[name + "2"]
        one[0, pl.ds(0, FACE), :] = source[pl.ds(0, FACE), :]
        one[0, pl.ds(FACE, CY), :] = source[pl.ds(2 * FACE, CY), :]
        two[0, pl.ds(0, FACE), :] = source[pl.ds(FACE, FACE), :]


def quarter_segments(c):
    zface = jnp.where(c < 2, 4, 5)
    return {
        "A": [(s, n, f) for (s, n), f in zip(SEGS_QA, (0, 1, zface))],
        "B": [(s, n, f) for (s, n), f in zip(SEGS_QB, (2, 3))],
    }


def strip_segments():
    return {
        "A": [(s, n, f) for (s, n), f in zip(SEGS_QX, (0, 1, 4))],
        "B": [(s, n, f) for (s, n), f in zip(SEGS_QX, (2, 3, 5))],
    }


def exchange_scratch(*rows):
    made = []
    for r in rows:
        for slots in (2 * RING, RING - 1, RING):
            made.append(VMEM((slots, r, CZ), F32))
    return made


def quarter_packet(c, pa, pb, ba, bb):
    part = rows_of(c * QROW, QROW, 8)
    part2 = rows_of(FACE + c * QROW, QROW, 8)
    ba[0, pl.ds(0, QROW), :] = pa[part, :]
    ba[0, pl.ds(QROW, QROW), :] = pa[part2, :]
    bb[0, pl.ds(0, QROW), :] = pb[part, :]
    bb[0, pl.ds(QROW, QROW), :] = pb[part2, :]
    zrows = rows_of(2 * FACE + lax.rem(c, 2) * 8, 8, 8)
    ba[0, pl.ds(2 * QROW, 8), :] = jnp.where(c < 2, pa[zrows, :], pb[zrows, :])


def share(place, mine, ghost, send, recv, base):
    made = []
    for k in range(1, NC):
        copy = pltpu.make_async_remote_copy(
            src_ref=mine,
            dst_ref=ghost.at[place.c],
            send_sem=send.at[base + k - 1],
            recv_sem=recv.at[base + k - 1],
            device_id=place.member(k),
            device_id_type=MESH,
        )
        copy.start()
        made.append(copy)
    ghost[place.c] = mine[...]
    return made


def put_into(mine, second):
    def put(half, start, count, value):
        mine[pl.ds((0 if half == "A" else second) + start, count), :] = value

    return put


def put_halves(wa, wb):
    def put(half, start, count, value):
        at = FACE if half[1] == "2" else 2 * start
        (wa if half[0] == "A" else wb)[pl.ds(at, count), :] = value

    return put


def kernel(owner, links, codes, mats, part, seeds, rate, adjoint, final, *scratch):
    first, second = scratch[0:6], scratch[6:12]
    third, fourth = scratch[12:24], scratch[24:36]
    scratch = scratch[36:]
    grid0, grid1, wgrid, wgrid1 = (scratch[3 * n : 3 * n + 3] for n in range(4))
    pa, pb, mine, mine1, stored, landed, landed1, wa, wb, lam, xface, xshare, send, recv = scratch[12:]
    place = Place()
    early = Exchange(place, "AB", first, send, recv, 0)
    again = Exchange(place, "AB", second, send, recv, 2 * N_COPIES)
    late = Exchange(place, WHOLES, third, send, recv, 4 * N_COPIES)
    back = Exchange(place, WHOLES, fourth, send, recv, 8 * N_COPIES)
    base = 12 * N_COPIES
    gather = Gather(place, part, stored, send, recv, base + 6)
    ends = EndLayers(place, xface, xshare, send, recv, base + 9)
    strips, quarters, wholes = strip_segments(), quarter_segments(place.c), full_segments()

    met = greet(place, True)
    pack_strip(part, place.c, xface, early.bufs["A"], early.bufs["B"])
    met()
    ends.begin()
    early.send_across("B")
    early.send_own("B")
    ends.take()
    for n in range(2):
        early.bufs["A"][0, pl.ds(n * QROW, QROW), :] = xshare[n]
    early.send_across("A")
    early.send_own("A")
    gather.begin()

    clear_z(pa, pb)

    def weigh(x):
        tau = TAU * rate[rows_of(x * CY, CY), :]
        values = [seeds[rows_of(v * 256 + x * CY, CY), :] * tau for v in range(NV)]
        for v in range(NV):
            wgrid[0][cell_rows(v, x), :] = values[v]
        pack_z(values, x, pa, pb)

    each_x(weigh)
    pack_xy(wgrid[0], pa, pb)
    whole_packet(pa, pb, late)
    early.relay()
    late.send_across()
    tables = Tables(place, owner, links)
    code = [codes[f, tables.own] for f in range(6)]
    gather.relay()
    early.hand_on(tables, strips)
    late.send_own()
    early.take(tables, strips, put_into(mine, QX))
    shared = share(place, mine, landed, send, recv, base)
    gather.take()
    span = CX * CY // NC
    for c in range(NC):
        for v in range(NV):
            grid0[0][pl.ds(v * EXT + CY + c * span, span), :] = stored[c, pl.ds(v * span, span), :]
    clear_z(pa, pb)
    late.relay()
    for copy in shared:
        copy.wait_recv()
    place_ghosts(strip_layers(landed), code, *grid0)

    each_x(lambda x: forward_step(mats, rate, grid0, grid1[0], pa, pb, x))
    pack_xy(grid1[0], pa, pb)

    quarter_packet(place.c, pa, pb, again.bufs["A"], again.bufs["B"])
    again.send_across()
    again.send_own()
    again.relay()
    late.hand_on(tables, wholes)
    again.hand_on(tables, quarters)
    again.take(tables, quarters, put_into(mine1, QA))
    shared1 = share(place, mine1, landed1, send, recv, base + 3)
    late.take(tables, wholes, put_halves(wa, wb))
    place_ghosts(adjoint_layers(wa, wb), code, *wgrid)
    clear_z(pa, pb)
    for copy in shared1:
        copy.wait_recv()
    place_ghosts(forward_layers(landed1), code, *grid1)

    def middle(x):
        adjoint_step(mats, rate, grid1, wgrid, seeds, lam, x, wgrid1[0], pa, pb)

    each_x(middle)
    pack_xy(wgrid1[0], pa, pb)

    whole_packet(pa, pb, back)
    back.send_across()
    back.send_own()
    def last(x):
        forward_step(mats, rate, grid1, final, None, None, x)

    each_x(last, 0, 6)
    back.relay()
    each_x(last, 6, 10)
    back.hand_on(tables, wholes)
    each_x(last, 10, CX)
    back.take(tables, wholes, put_halves(wa, wb))
    place_ghosts(adjoint_layers(wa, wb), code, *wgrid1)
    each_x(lambda x: adjoint_step(mats, rate, grid0, wgrid1, lam, adjoint, x))

    for copy in shared + shared1:
        copy.wait_send()
    ends.drain()
    for exchange in (gather, early, late, again, back):
        exchange.drain()


def on_device(checkpoint, seeds, cell_rate, flux_mats, owner, neighbours, orientation):
    vm, sm = pltpu.VMEM, pltpu.SMEM
    block = jax.ShapeDtypeStruct((ROWS, CZ), F32)
    strip, quarter = exchange_scratch(QX, QX), exchange_scratch(QA, QB)
    whole = exchange_scratch(BIG, BIG, FACE, FACE)
    grid = [VMEM((NV * EXT, CZ), F32), VMEM((2 * FACE, CZ), F32), VMEM((2 * CY, CZ), F32)]
    half = VMEM((HALF, CZ), F32)
    copies = 17 + 12 * N_COPIES
    adjoint, final = pl.pallas_call(
        kernel,
        out_shape=(block, block),
        in_specs=[pl.BlockSpec(memory_space=m) for m in (sm, sm, sm, sm, vm, vm, vm)],
        out_specs=(pl.BlockSpec(memory_space=vm), pl.BlockSpec(memory_space=vm)),
        scratch_shapes=strip
        + quarter
        + whole * 2
        + grid * 4
        + [half, half, VMEM((2 * QX, CZ), F32), VMEM((QA + QB, CZ), F32)]
        + [VMEM((NC, ROWS // NC, CZ), F32)]
        + [VMEM((NC, 2 * QX, CZ), F32), VMEM((NC, QA + QB, CZ), F32), half, half]
        + [VMEM((ROWS, CZ), F32), VMEM((2, FACE, CZ), F32), VMEM((2, QROW, CZ), F32)]
        + [pltpu.SemaphoreType.DMA((copies,)), pltpu.SemaphoreType.DMA((copies,))],
        compiler_params=pltpu.CompilerParams(collective_id=0, has_side_effects=True),
    )(
        owner,
        neighbours.T,
        orientation.T,
        flux_mats,
        checkpoint.reshape(ROWS // NC, CZ),
        seeds.reshape(ROWS, CZ),
        cell_rate.reshape(CX * CY, CZ),
    )
    return (
        adjoint.reshape(1, 1, NV, CX, CY, CZ),
        final.reshape(1, NV, CX, CY, CZ),
    )


def solution(mesh):
    return jax.shard_map(
        on_device,
        mesh=mesh,
        in_specs=(
            P("space", None, "ckpt", None, None),
            P("ckpt", "space", None, None, None, None),
            P("space", None, None, None),
            P(),
            P(),
            P(),
            P(),
        ),
        out_specs=(P("ckpt", "space", None, None, None, None), P("space", None, None, None, None)),
        check_vma=False,
    )
```

```python
import jax
import jax.numpy as jnp
from jax import lax
from jax.experimental import pallas as pl
from jax.experimental.pallas import tpu as pltpu
from jax.sharding import PartitionSpec as P

MESH = pl.DeviceIdType.MESH
VMEM = pltpu.VMEM
F32 = jnp.float32

NX, NY, NZ, NC = 4, 4, 2, 4
NV, CX, CY, CZ = 6, 16, 16, 128
ROWS = NV * CX * CY
FACE = NV * CX
EXT = (CX + 2) * CY
TAU = 0.05
DAMP = 0.015
HALF = 2 * FACE + CY
QROW = FACE // NC
QA, QB = 2 * QROW + 8, 2 * QROW
SEGS = ((0, FACE), (FACE, FACE), (2 * FACE, CY))
SEGS_QA = ((0, QROW), (QROW, QROW), (2 * QROW, 8))
SEGS_QB = ((0, QROW), (QROW, QROW))
STRIP = CX // NC
QX = 2 * QROW + CY
SEGS_QX = ((0, QROW), (QROW, QROW), (2 * QROW, CY))


def lanes(shape):
    return lax.broadcasted_iota(jnp.int32, shape, len(shape) - 1)


def rows_of(start, count, step=16):
    return pl.ds(pl.multiple_of(start, step), count)


def cell_rows(v, x):
    return rows_of(v * EXT + (x + 1) * CY, CY)


def pack_xy(ext, pa, pb):
    for seg, x in ((0, CX - 1), (FACE, 0)):
        for v in range(NV):
            pa[pl.ds(seg + v * 16, 16), :] = ext[pl.ds(v * EXT + (x + 1) * CY, CY), :]
    for seg, y in ((0, CY - 1), (FACE, 0)):
        for v in range(NV):
            pb[pl.ds(seg + v * 16, 16), :] = ext[pl.ds(v * EXT + CY + y, CX, stride=CY), :]


def pack_z(values, x, pa, pb):
    lane = lanes((CY, CZ))
    up = pa[pl.ds(2 * FACE, CY), :]
    low = pb[pl.ds(2 * FACE, CY), :]
    for v in range(NV):
        at = v * 16 + x
        here = lane == at
        up = jnp.where(here, pltpu.roll(values[v], at + 1, 1), up)
        low = jnp.where(here, pltpu.roll(values[v], at, 1), low)
    pa[pl.ds(2 * FACE, CY), :] = up
    pb[pl.ds(2 * FACE, CY), :] = low


def clear_z(pa, pb):
    pa[pl.ds(2 * FACE, CY), :] = jnp.zeros((CY, CZ), F32)
    pb[pl.ds(2 * FACE, CY), :] = jnp.zeros((CY, CZ), F32)


def lane_flip(piece, flag, width):
    lane = lanes(piece.shape)
    at = lane & (width - 1)
    return jnp.take_along_axis(piece, lane + flag * (width - 1 - 2 * at), axis=1)


def row_flip(piece, flag):
    row = lax.broadcasted_iota(jnp.int32, (8, CZ), 0)
    index = row + flag * (7 - 2 * row)
    first, second = piece[:8], piece[8:]
    turned = flag == 1
    lower = jnp.where(turned, second, first)
    upper = jnp.where(turned, first, second)
    return [jnp.take_along_axis(lower, index, axis=0), jnp.take_along_axis(upper, index, axis=0)]


def place_ghosts(layer, code, ext, gy, gz):
    for f in range(6):
        first, second = code[f] & 1, (code[f] >> 1) & 1
        if f < 4:
            for v in range(NV):
                for h, piece in enumerate(row_flip(layer(f, v), first)):
                    piece = lane_flip(piece, second, CZ)
                    if f < 2:
                        start = v * EXT + ((CX + 1) * CY if f == 0 else 0)
                        ext[pl.ds(start + 8 * h, 8), :] = piece
                    else:
                        gy[pl.ds((f - 2) * FACE + v * 16 + 8 * h, 8), :] = piece
        else:
            for h, piece in enumerate(row_flip(layer(f, 0), second)):
                gz[pl.ds((f - 4) * CY + 8 * h, 8), :] = lane_flip(piece, first, CX)


def forward_layers(ghost):
    def face(f):
        start = {1: 0, 0: QROW, 3: QA, 2: QA + QROW}[f]
        return jnp.concatenate([ghost[c, pl.ds(start, QROW), :] for c in range(NC)])

    faces = {f: face(f) for f in range(4)}

    def layer(f, v):
        if f < 4:
            return faces[f][v * 16 : v * 16 + 16]
        c = 0 if f == 5 else 2
        return jnp.concatenate([ghost[c, pl.ds(2 * QROW, 8), :], ghost[c + 1, pl.ds(2 * QROW, 8), :]])

    return layer


def strip_layers(ghost):
    lane = lanes((CY, CZ))

    def layer(f, v):
        if f < 2:
            start = (1 - f) * QROW
            rows = range(v * 16, v * 16 + 16, 8)
            return jnp.concatenate(
                [ghost[r // QROW, pl.ds(start + r % QROW, 8), :] for r in rows]
            )
        if f < 4:
            start = QX + (3 - f) * QROW + v * STRIP
            return jnp.concatenate([ghost[c, pl.ds(start, STRIP), :] for c in range(NC)])
        start = 2 * QROW if f == 5 else QX + 2 * QROW
        out = ghost[0, pl.ds(start, CY), :]
        for c in range(1, NC):
            out = jnp.where((lane & 15) // STRIP == c, ghost[c, pl.ds(start, CY), :], out)
        return out

    return layer


def pack_strip(part, c, xface, ba, bb):
    lane = lanes((CY, CZ))
    for seg, y in ((0, CY - 1), (QROW, 0)):
        for v in range(NV):
            bb[0, pl.ds(seg + v * STRIP, STRIP), :] = part[pl.ds(v * 64 + y, STRIP, stride=CY), :]
    up = jnp.zeros((CY, CZ), F32)
    low = jnp.zeros((CY, CZ), F32)
    for v in range(NV):
        for x in range(STRIP):
            value = part[pl.ds(v * 64 + x * CY, CY), :]
            at = v * 16 + c * STRIP + x
            here = lane == at
            up = jnp.where(here, pltpu.roll(value, at + 1, 1), up)
            low = jnp.where(here, pltpu.roll(value, at, 1), low)
            if x == STRIP - 1:
                xface[0, pl.ds(v * 16, 16), :] = value
            if x == 0:
                xface[1, pl.ds(v * 16, 16), :] = value
    ba[0, pl.ds(2 * QROW, CY), :] = up
    bb[0, pl.ds(2 * QROW, CY), :] = low


class EndLayers:
    def __init__(self, place, xface, share, send, recv, base):
        self.place, self.xface, self.share = place, xface, share
        self.send, self.recv, self.base = send, recv, base

    def copy(self, n, who, member):
        return pltpu.make_async_remote_copy(
            src_ref=self.xface.at[n, pl.ds(member * QROW, QROW)],
            dst_ref=self.share.at[n],
            send_sem=self.send.at[self.base + n * NC + member],
            recv_sem=self.recv.at[self.base + n],
            device_id=(member, lax.axis_index("space")),
            device_id_type=MESH,
        )

    def each(self, holder, other):
        for n, who in ((0, NC - 1), (1, 0)):
            members = [m for m in range(NC) if m != who]
            if holder is not None:

                @pl.when(self.place.c == who)
                def _():
                    holder(n, who, members)

            if other is not None:

                @pl.when(self.place.c != who)
                def _():
                    other(n, who, members)

    def begin(self):
        def give(n, who, members):
            for m in members:
                self.copy(n, who, m).start()
            self.share[n] = self.xface[n, pl.ds(who * QROW, QROW), :]

        self.each(give, None)

    def take(self):
        self.each(None, lambda n, who, members: self.copy(n, who, members[0]).wait_recv())

    def drain(self):
        self.each(lambda n, who, members: [self.copy(n, who, m).wait_send() for m in members], None)


class Gather:
    def __init__(self, place, part, stored, send, recv, base):
        self.place, self.part, self.stored = place, part, stored
        self.send, self.recv, self.base = send, recv, base
        self.all = []

    def copy(self, src, slot, member):
        n = self.base + len(self.all)
        made = pltpu.make_async_remote_copy(
            src_ref=src,
            dst_ref=self.stored.at[slot],
            send_sem=self.send.at[n],
            recv_sem=self.recv.at[n],
            device_id=(member, lax.axis_index("space")),
            device_id_type=MESH,
        )
        made.start()
        self.all.append(made)

    def begin(self):
        c = self.place.c
        self.core = c + 1 - 2 * lax.rem(c, 2)
        self.far = lax.rem(c + 2, NC)
        self.copy(self.part, c, self.far)
        self.copy(self.part, c, self.core)
        self.stored[c] = self.part[...]

    def relay(self):
        self.all[0].wait_recv()
        self.copy(self.stored.at[self.far], self.far, self.core)

    def take(self):
        for made in self.all[1:]:
            made.wait_recv()

    def drain(self):
        for made in self.all:
            made.wait_send()


def adjoint_layers(ga, gb):
    def layer(f, v):
        half = ga if f in (0, 1, 5) else gb
        if f < 4:
            return half[pl.ds((1 - f % 2) * FACE + v * 16, 16), :]
        return half[pl.ds(2 * FACE, CY), :]

    return layer


def neighbours_of(grid, x, stand=None):
    ext, gy, gz = grid
    row = lax.broadcasted_iota(jnp.int32, (CY, CZ), 0)
    lane = lanes((CY, CZ))
    centre = [ext[cell_rows(v, x), :] for v in range(NV)]

    def at(direction):
        ups, lows = [], []
        for v in range(NV):
            u = centre[v]
            at_x = v * 16 + x
            if direction == 0:
                up = ext[cell_rows(v, x + 1), :]
                low = ext[cell_rows(v, x - 1), :]
            elif stand is not None:
                axis, size = direction - 1, (CY, CZ)[direction - 1]
                at_side = (row, lane)[axis]
                other = u if stand == "own" else jnp.zeros_like(u)
                up = jnp.where(at_side == size - 1, other, pltpu.roll(u, size - 1, axis))
                low = jnp.where(at_side == 0, other, pltpu.roll(u, 1, axis))
            elif direction == 1:
                up = jnp.where(row == CY - 1, gy[pl.ds(at_x, 1), :], pltpu.roll(u, CY - 1, 0))
                low = jnp.where(row == 0, gy[pl.ds(FACE + at_x, 1), :], pltpu.roll(u, 1, 0))
            else:
                high = pltpu.roll(gz[pl.ds(0, CY), :], CZ - 1 - at_x, 1)
                deep = pltpu.roll(gz[pl.ds(CY, CY), :], lax.rem(CZ - at_x, CZ), 1)
                up = jnp.where(lane == CZ - 1, high, pltpu.roll(u, CZ - 1, 1))
                low = jnp.where(lane == 0, deep, pltpu.roll(u, 1, 1))
            ups.append(up)
            lows.append(low)
        return ups, lows

    return centre, at


def spread_of(first, second):
    mean = 0.5 * (first + second)
    t = 1.0 + mean * mean
    r = lax.rsqrt(t)
    return t * r, mean * r


def forward_step(mats, rate, grid, out, pa, pb, x, stand=None):
    u, at = neighbours_of(grid, x, stand)
    total = [jnp.zeros((CY, CZ), F32) for _ in range(NV)]
    for d in range(3):
        up, low = at(d)
        su, _ = spread_of(up[0], u[0])
        sl, _ = spread_of(u[0], low[0])
        diff = [up[v] - low[v] for v in range(NV)]
        for i in range(NV):
            acc = total[i] - (su * (up[i] - u[i]) - sl * (u[i] - low[i]))
            for j in range(NV):
                acc = acc + mats[d, i, j] * diff[j]
            total[i] = acc
    tau = (0.5 * TAU) * rate[rows_of(x * CY, CY), :]
    new = [u[v] - tau * total[v] - DAMP * jnp.tanh(u[v]) for v in range(NV)]
    for v in range(NV):
        if pa is None:
            out[rows_of(v * 256 + x * CY, CY), :] = new[v]
        else:
            out[cell_rows(v, x), :] = new[v]
    if pa is not None:
        pack_z(new if stand is None else u, x, pa, pb)


def adjoint_step(mats, rate, grid, wgrid, lam, out, x, weighted=None, pa=None, pb=None, stand=None):
    u, at_u = neighbours_of(grid, x)
    w, at_w = neighbours_of(wgrid, x, stand)
    total = [jnp.zeros((CY, CZ), F32) for _ in range(NV)]
    tilt = jnp.zeros((CY, CZ), F32)
    for d in range(3):
        up, low = at_u(d)
        wup, wlow = at_w(d)
        su, ru = spread_of(up[0], u[0])
        sl, rl = spread_of(u[0], low[0])
        dot_u = jnp.zeros((CY, CZ), F32)
        dot_l = jnp.zeros((CY, CZ), F32)
        wdiff = []
        for i in range(NV):
            du, dl = up[i] - u[i], u[i] - low[i]
            gu, gl = wup[i] - w[i], w[i] - wlow[i]
            dot_u = dot_u + du * gu
            dot_l = dot_l + dl * gl
            total[i] = total[i] + (su * gu - sl * gl)
            wdiff.append(wup[i] - wlow[i])
        tilt = tilt + ru * dot_u + rl * dot_l
        for i in range(NV):
            acc = total[i]
            for j in range(NV):
                acc = acc + mats[d, j, i] * wdiff[j]
            total[i] = acc
    tau = TAU * rate[rows_of(x * CY, CY), :]
    packed = []
    for v in range(NV):
        here = rows_of(v * 256 + x * CY, CY)
        bent = jnp.tanh(u[v])
        old = lam[here, :]
        new = old - DAMP * (1.0 - bent * bent) * old + 0.5 * total[v]
        if v == 0:
            new = new - 0.25 * tilt
        out[here, :] = new
        if weighted is not None:
            packed.append(tau * new)
            weighted[cell_rows(v, x), :] = packed[v]
    if weighted is not None:
        pack_z(packed, x, pa, pb)


def own_tile(f, v, pa, pb):
    half = (pa, pa, pb, pb, pa, pb)[f]
    if f < 4:
        return half[pl.ds((f % 2) * FACE + v * 16, 16), :]
    return pltpu.roll(half[pl.ds(2 * FACE, CY), :], (CZ - v * 16) % CZ, 1)


def ghost_tile(f, v, grid):
    ext, gy, gz = grid
    if f < 2:
        return ext[pl.ds(v * EXT + ((CX + 1) * CY if f == 0 else 0), CY), :]
    if f < 4:
        return gy[pl.ds((f - 2) * FACE + v * 16, 16), :]
    return pltpu.roll(gz[pl.ds((f - 4) * CY, CY), :], (CZ - v * 16) % CZ, 1)


def forward_fix(f, mats, grid, pa, pb):
    sign = -0.5 if f % 2 == 0 else 0.5
    own = [own_tile(f, v, pa, pb) for v in range(NV)]
    across = [ghost_tile(f, v, grid) for v in range(NV)]
    delta = [g - u for g, u in zip(across, own)]
    spread, _ = spread_of(across[0], own[0])
    fixes = []
    for i in range(NV):
        acc = mats[f // 2, i, 0] * delta[0]
        for j in range(1, NV):
            acc = acc + mats[f // 2, i, j] * delta[j]
        fixes.append(sign * acc + 0.5 * spread * delta[i])
    return fixes


def adjoint_fix(f, mats, grid, wgrid, pa, pb):
    sign = 0.5 if f % 2 == 0 else -0.5
    own = [own_tile(f, v, pa, pb) for v in range(NV)]
    across = [ghost_tile(f, v, grid) for v in range(NV)]
    w = [ghost_tile(f, v, wgrid) for v in range(NV)]
    spread, ratio = spread_of(across[0], own[0])
    dot = jnp.zeros((CY, CZ), F32)
    for i in range(NV):
        dot = dot + (across[i] - own[i]) * w[i]
    fixes = []
    for i in range(NV):
        acc = mats[f // 2, 0, i] * w[0]
        for j in range(1, NV):
            acc = acc + mats[f // 2, j, i] * w[j]
        fixes.append(sign * acc + 0.5 * spread * w[i])
    fixes[0] = fixes[0] - 0.25 * ratio * dot
    return fixes


def repair(fix, out, stride, offset, fz, rate=None, pa=None, pb=None):
    for f in range(4):
        fixes = fix(f)
        first = f % 2 == 1
        if f < 2:
            x = 0 if first else CX - 1
            tau = None if rate is None else TAU * rate[pl.ds(x * CY, CY), :]
            rows = [pl.ds(v * stride + offset + x * CY, CY) for v in range(NV)]
        else:
            y = 0 if first else CY - 1
            tau = None if rate is None else TAU * rate[pl.ds(y, CX, stride=CY), :]
            rows = [pl.ds(v * stride + offset + y, CX, stride=CY) for v in range(NV)]
        for v in range(NV):
            out[rows[v], :] = out[rows[v], :] + (fixes[v] if tau is None else tau * fixes[v])
    for f in (4, 5):
        for v, value in enumerate(fix(f)):
            fz[pl.ds(((f - 4) * NV + v) * CY, CY), :] = value
    lane = lanes((CY, CZ))

    def sides(x):
        tau = None if rate is None else TAU * rate[rows_of(x * CY, CY), :]
        values = []
        for v in range(NV):
            up = pltpu.roll(fz[pl.ds(v * CY, CY), :], CZ - 1 - x, 1)
            low = pltpu.roll(fz[pl.ds((NV + v) * CY, CY), :], lax.rem(CZ - x, CZ), 1)
            add = jnp.where(lane == CZ - 1, up, jnp.where(lane == 0, low, 0.0))
            here = rows_of(v * stride + offset + x * CY, CY)
            values.append(out[here, :] + (add if tau is None else tau * add))
            out[here, :] = values[v]
        if pa is not None:
            pack_z(values, x, pa, pb)

    each_x(sides)


def each_x(step, start=0, stop=CX):
    def body(x, carry):
        step(x)
        return carry

    lax.fori_loop(start, stop, body, 0)


class Place:
    def __init__(self):
        self.c = lax.axis_index("ckpt")
        s = lax.axis_index("space")
        self.z = lax.rem(s, NZ)
        self.x = lax.rem(lax.div(s, NZ), NX)
        self.y = lax.div(s, NZ * NX)

    def space(self, x, y, z):
        return (y * NX + x) * NZ + z

    def along_x(self, k):
        return (self.c, self.space(lax.rem(self.x + k, NX), self.y, self.z))

    def along_y(self, k):
        return (self.c, self.space(self.x, lax.rem(self.y + k, NY), self.z))

    def across_z(self):
        return (self.c, self.space(self.x, self.y, 1 - self.z))

    def member(self, k):
        return (lax.rem(self.c + k, NC), lax.axis_index("space"))


def greet(place, members):
    barrier = pltpu.get_barrier_semaphore()
    partners = [place.across_z()]
    partners += [place.along_x(k) for k in range(1, NX)]
    partners += [place.along_y(k) for k in range(1, NY)]
    if members:
        partners += [place.member(k) for k in range(1, NC)]
    for partner in partners:
        pl.semaphore_signal(barrier, inc=1, device_id=partner, device_id_type=MESH)
    return lambda: pl.semaphore_wait(barrier, len(partners))


class Tables:
    def __init__(self, place, owner, links):
        self.place = place
        spots = [place.space(place.x, lax.rem(place.y + k, NY), place.z) for k in range(NY)]
        spots += [place.space(lax.rem(place.x + k, NX), place.y, place.z) for k in range(1, NX)]

        def find(b, found):
            who = owner[b]
            return tuple(jnp.where(who == s, b, f) for f, s in zip(found, spots))

        blocks = lax.fori_loop(0, NX * NY * NZ, find, tuple(jnp.int32(0) for _ in spots))
        self.own = blocks[0]
        self.down = {"A": list(blocks[:NY]), "B": [blocks[0]] + list(blocks[NY:])}
        self.owner, self.links = owner, links

    def source(self, block, layer):
        s = self.owner[self.links[layer ^ 1, block]]
        return lax.rem(lax.div(s, NZ), NX), lax.div(s, NZ * NX), lax.rem(s, NZ)

    def slot(self, half, k, layer):
        x, y, z = self.source(self.down[half][k], layer)
        turn = jnp.where(z == self.place.z, 0, 1)
        if half == "A":
            return turn * NX + lax.rem(self.place.x - x + NX, NX)
        return turn * NY + lax.rem(self.place.y - y + NY, NY)

    def last(self, half, layer):
        x, y, _ = self.source(self.own, layer)
        if half == "A":
            return lax.rem(self.place.y - y + NY, NY)
        return lax.rem(self.place.x - x + NX, NX)


RING = NX
HOPS = (2, 1, 3)
N_COPIES = 1 + 3 * len(HOPS)


class Exchange:
    def __init__(self, place, parts, scratch, send, recv, base):
        self.place, self.parts = place, parts
        self.bufs, self.outs, self.arrivals = (
            dict(zip(parts, scratch[n::3])) for n in range(3)
        )
        self.send, self.recv, self.base = send, recv, base
        self.all = []
        self.first = {"A": place.along_x, "B": place.along_y}
        self.second = {"A": place.along_y, "B": place.along_x}
        self.across = {}
        self.own = {part: [] for part in parts}
        self.passed = {part: [] for part in parts}
        self.final = {part: [] for part in parts}

    def copy(self, src, dst, device):
        n = self.base + len(self.all)
        made = pltpu.make_async_remote_copy(
            src_ref=src,
            dst_ref=dst,
            send_sem=self.send.at[n],
            recv_sem=self.recv.at[n],
            device_id=device,
            device_id_type=MESH,
        )
        made.start()
        self.all.append(made)
        return made

    def send_across(self, parts=None):
        for part in parts or self.parts:
            buf = self.bufs[part]
            self.across[part] = self.copy(buf.at[0], buf.at[RING], self.place.across_z())

    def send_own(self, parts=None):
        for part in parts or self.parts:
            buf, away = self.bufs[part], self.first[part[0]]
            for k in HOPS:
                self.own[part].append(self.copy(buf.at[0], buf.at[k], away(k)))

    def relay(self):
        for part in self.parts:
            buf, away = self.bufs[part], self.first[part[0]]
            self.across[part].wait_recv()
            for k in HOPS:
                self.passed[part].append(self.copy(buf.at[RING], buf.at[RING + k], away(k)))

    def hand_on(self, tables, segments):
        for part in self.parts:
            for made in self.own[part] + self.passed[part]:
                made.wait_recv()
            buf, out, arrive = self.bufs[part], self.outs[part], self.arrivals[part]
            for k in HOPS + (0,):
                for start, count, layer in segments[part]:
                    picked = buf[tables.slot(part[0], k, layer), pl.ds(start, count), :]
                    if k == 0:
                        arrive[0, pl.ds(start, count), :] = picked
                    else:
                        out[k - 1, pl.ds(start, count), :] = picked
                if k:
                    self.final[part].append(
                        self.copy(out.at[k - 1], arrive.at[k], self.second[part[0]](k))
                    )

    def take(self, tables, segments, put):
        for part in self.parts:
            for made in self.final[part]:
                made.wait_recv()
            arrive = self.arrivals[part]
            for start, count, layer in segments[part]:
                put(part, start, count, arrive[tables.last(part[0], layer), pl.ds(start, count), :])

    def drain(self):
        for made in self.all:
            made.wait_send()


WHOLES = ("A1", "B1", "A2", "B2")
BIG = FACE + CY


def full_segments():
    return {
        "A1": [(0, FACE, 0), (FACE, CY, 4)],
        "B1": [(0, FACE, 2), (FACE, CY, 5)],
        "A2": [(0, FACE, 1)],
        "B2": [(0, FACE, 3)],
    }


def whole_packet(pa, pb, exchange):
    for source, name in ((pa, "A"), (pb, "B")):
        one, two = exchange.bufs[name + "1"], exchange.bufs[name + "2"]
        one[0, pl.ds(0, FACE), :] = source[pl.ds(0, FACE), :]
        one[0, pl.ds(FACE, CY), :] = source[pl.ds(2 * FACE, CY), :]
        two[0, pl.ds(0, FACE), :] = source[pl.ds(FACE, FACE), :]


def quarter_segments(c):
    zface = jnp.where(c < 2, 4, 5)
    return {
        "A": [(s, n, f) for (s, n), f in zip(SEGS_QA, (0, 1, zface))],
        "B": [(s, n, f) for (s, n), f in zip(SEGS_QB, (2, 3))],
    }


def strip_segments():
    return {
        "A": [(s, n, f) for (s, n), f in zip(SEGS_QX, (0, 1, 4))],
        "B": [(s, n, f) for (s, n), f in zip(SEGS_QX, (2, 3, 5))],
    }


def exchange_scratch(*rows):
    made = []
    for r in rows:
        for slots in (2 * RING, RING - 1, RING):
            made.append(VMEM((slots, r, CZ), F32))
    return made


def quarter_packet(c, pa, pb, ba, bb):
    part = rows_of(c * QROW, QROW, 8)
    part2 = rows_of(FACE + c * QROW, QROW, 8)
    ba[0, pl.ds(0, QROW), :] = pa[part, :]
    ba[0, pl.ds(QROW, QROW), :] = pa[part2, :]
    bb[0, pl.ds(0, QROW), :] = pb[part, :]
    bb[0, pl.ds(QROW, QROW), :] = pb[part2, :]
    zrows = rows_of(2 * FACE + lax.rem(c, 2) * 8, 8, 8)
    ba[0, pl.ds(2 * QROW, 8), :] = jnp.where(c < 2, pa[zrows, :], pb[zrows, :])


def share(place, mine, ghost, send, recv, base):
    made = []
    for k in range(1, NC):
        copy = pltpu.make_async_remote_copy(
            src_ref=mine,
            dst_ref=ghost.at[place.c],
            send_sem=send.at[base + k - 1],
            recv_sem=recv.at[base + k - 1],
            device_id=place.member(k),
            device_id_type=MESH,
        )
        copy.start()
        made.append(copy)
    ghost[place.c] = mine[...]
    return made


def put_into(mine, second):
    def put(half, start, count, value):
        mine[pl.ds((0 if half == "A" else second) + start, count), :] = value

    return put


def put_halves(wa, wb):
    def put(half, start, count, value):
        at = FACE if half[1] == "2" else 2 * start
        (wa if half[0] == "A" else wb)[pl.ds(at, count), :] = value

    return put


def kernel(owner, links, codes, mats, part, seeds, rate, adjoint, final, *scratch):
    first, second = scratch[0:6], scratch[6:12]
    third, fourth = scratch[12:24], scratch[24:36]
    scratch = scratch[36:]
    grid0, grid1, wgrid, wgrid1 = (scratch[3 * n : 3 * n + 3] for n in range(4))
    pa, pb, mine, mine1, stored, landed, landed1, wa, wb, lam, xface, xshare, pu, pw, fz, send, recv = scratch[12:]
    place = Place()
    early = Exchange(place, "AB", first, send, recv, 0)
    again = Exchange(place, "AB", second, send, recv, 2 * N_COPIES)
    late = Exchange(place, WHOLES, third, send, recv, 4 * N_COPIES)
    back = Exchange(place, WHOLES, fourth, send, recv, 8 * N_COPIES)
    base = 12 * N_COPIES
    gather = Gather(place, part, stored, send, recv, base + 6)
    ends = EndLayers(place, xface, xshare, send, recv, base + 9)
    strips, quarters, wholes = strip_segments(), quarter_segments(place.c), full_segments()

    met = greet(place, True)
    pack_strip(part, place.c, xface, early.bufs["A"], early.bufs["B"])
    met()
    ends.begin()
    early.send_across("B")
    early.send_own("B")
    ends.take()
    for n in range(2):
        early.bufs["A"][0, pl.ds(n * QROW, QROW), :] = xshare[n]
    early.send_across("A")
    early.send_own("A")
    gather.begin()

    clear_z(pa, pb)

    def weigh(x):
        tau = TAU * rate[rows_of(x * CY, CY), :]
        values = [seeds[rows_of(v * 256 + x * CY, CY), :] * tau for v in range(NV)]
        for v in range(NV):
            wgrid[0][cell_rows(v, x), :] = values[v]
        pack_z(values, x, pa, pb)

    each_x(weigh)
    pack_xy(wgrid[0], pa, pb)
    whole_packet(pa, pb, late)
    early.relay()
    late.send_across()
    tables = Tables(place, owner, links)
    code = [codes[f, tables.own] for f in range(6)]
    gather.relay()
    early.hand_on(tables, strips)
    late.send_own()
    early.take(tables, strips, put_into(mine, QX))
    shared = share(place, mine, landed, send, recv, base)
    gather.take()
    span = CX * CY // NC
    for c in range(NC):
        for v in range(NV):
            grid0[0][pl.ds(v * EXT + CY + c * span, span), :] = stored[c, pl.ds(v * span, span), :]
    for v in range(NV):
        for ghost, x in ((0, 0), (CX + 1, CX - 1)):
            grid0[0][pl.ds(v * EXT + ghost * CY, CY), :] = grid0[0][pl.ds(v * EXT + (x + 1) * CY, CY), :]
    clear_z(pu, pw)
    pack_xy(grid0[0], pu, pw)
    late.relay()
    each_x(lambda x: forward_step(mats, rate, grid0, grid1[0], pu, pw, x, "own"))
    clear_z(pa, pb)
    for copy in shared:
        copy.wait_recv()
    place_ghosts(strip_layers(landed), code, *grid0)
    repair(
        lambda f: forward_fix(f, mats, grid0, pu, pw), grid1[0], EXT, CY, fz, rate, pa, pb
    )
    pack_xy(grid1[0], pa, pb)

    quarter_packet(place.c, pa, pb, again.bufs["A"], again.bufs["B"])
    again.send_across()
    again.send_own()
    again.relay()
    late.hand_on(tables, wholes)
    again.hand_on(tables, quarters)
    again.take(tables, quarters, put_into(mine1, QA))
    shared1 = share(place, mine1, landed1, send, recv, base + 3)
    late.take(tables, wholes, put_halves(wa, wb))
    place_ghosts(adjoint_layers(wa, wb), code, *wgrid)
    clear_z(pa, pb)
    for copy in shared1:
        copy.wait_recv()
    place_ghosts(forward_layers(landed1), code, *grid1)

    def middle(x):
        adjoint_step(mats, rate, grid1, wgrid, seeds, lam, x, wgrid1[0], pa, pb)

    each_x(middle)
    pack_xy(wgrid1[0], pa, pb)

    whole_packet(pa, pb, back)
    back.send_across()
    back.send_own()
    def last(x):
        forward_step(mats, rate, grid1, final, None, None, x)

    for v in range(NV):
        for ghost in (0, CX + 1):
            wgrid1[0][pl.ds(v * EXT + ghost * CY, CY), :] = jnp.zeros((CY, CZ), F32)

    def end(x):
        adjoint_step(mats, rate, grid0, wgrid1, lam, adjoint, x, stand="zero")

    each_x(last, 0, 10)
    back.relay()
    each_x(last, 10, CX)
    each_x(end, 0, 4)
    back.hand_on(tables, wholes)
    each_x(end, 4, CX)
    back.take(tables, wholes, put_halves(wa, wb))
    place_ghosts(adjoint_layers(wa, wb), code, *wgrid1)
    repair(lambda f: adjoint_fix(f, mats, grid0, wgrid1, pu, pw), adjoint, CX * CY, 0, fz)

    for copy in shared + shared1:
        copy.wait_send()
    ends.drain()
    for exchange in (gather, early, late, again, back):
        exchange.drain()


def on_device(checkpoint, seeds, cell_rate, flux_mats, owner, neighbours, orientation):
    vm, sm = pltpu.VMEM, pltpu.SMEM
    block = jax.ShapeDtypeStruct((ROWS, CZ), F32)
    strip, quarter = exchange_scratch(QX, QX), exchange_scratch(QA, QB)
    whole = exchange_scratch(BIG, BIG, FACE, FACE)
    grid = [VMEM((NV * EXT, CZ), F32), VMEM((2 * FACE, CZ), F32), VMEM((2 * CY, CZ), F32)]
    half = VMEM((HALF, CZ), F32)
    copies = 17 + 12 * N_COPIES
    adjoint, final = pl.pallas_call(
        kernel,
        out_shape=(block, block),
        in_specs=[pl.BlockSpec(memory_space=m) for m in (sm, sm, sm, sm, vm, vm, vm)],
        out_specs=(pl.BlockSpec(memory_space=vm), pl.BlockSpec(memory_space=vm)),
        scratch_shapes=strip
        + quarter
        + whole * 2
        + grid * 4
        + [half, half, VMEM((2 * QX, CZ), F32), VMEM((QA + QB, CZ), F32)]
        + [VMEM((NC, ROWS // NC, CZ), F32)]
        + [VMEM((NC, 2 * QX, CZ), F32), VMEM((NC, QA + QB, CZ), F32), half, half]
        + [VMEM((ROWS, CZ), F32), VMEM((2, FACE, CZ), F32), VMEM((2, QROW, CZ), F32)]
        + [half, half, VMEM((2 * NV * CY, CZ), F32)]
        + [pltpu.SemaphoreType.DMA((copies,)), pltpu.SemaphoreType.DMA((copies,))],
        compiler_params=pltpu.CompilerParams(collective_id=0, has_side_effects=True),
    )(
        owner,
        neighbours.T,
        orientation.T,
        flux_mats,
        checkpoint.reshape(ROWS // NC, CZ),
        seeds.reshape(ROWS, CZ),
        cell_rate.reshape(CX * CY, CZ),
    )
    return (
        adjoint.reshape(1, 1, NV, CX, CY, CZ),
        final.reshape(1, NV, CX, CY, CZ),
    )


def solution(mesh):
    return jax.shard_map(
        on_device,
        mesh=mesh,
        in_specs=(
            P("space", None, "ckpt", None, None),
            P("ckpt", "space", None, None, None, None),
            P("space", None, None, None),
            P(),
            P(),
            P(),
            P(),
        ),
        out_specs=(P("ckpt", "space", None, None, None, None), P("space", None, None, None, None)),
        check_vma=False,
    )
```

```python
import jax
import jax.numpy as jnp
from jax import lax
from jax.experimental import pallas as pl
from jax.experimental.pallas import tpu as pltpu
from jax.sharding import PartitionSpec as P

MESH = pl.DeviceIdType.MESH
VMEM = pltpu.VMEM
F32 = jnp.float32

NX, NY, NZ, NC = 4, 4, 2, 4
NV, CX, CY, CZ = 6, 16, 16, 128
ROWS = NV * CX * CY
FACE = NV * CX
EXT = (CX + 2) * CY
TAU = 0.05
DAMP = 0.015
M0, M1, M2 = 5, 6, 10
HALF = 2 * FACE + CY
QROW = FACE // NC
QA, QB = 2 * QROW + 8, 2 * QROW
SEGS = ((0, FACE), (FACE, FACE), (2 * FACE, CY))
SEGS_QA = ((0, QROW), (QROW, QROW), (2 * QROW, 8))
SEGS_QB = ((0, QROW), (QROW, QROW))
STRIP = CX // NC
QX = 2 * QROW + CY
SEGS_QX = ((0, QROW), (QROW, QROW), (2 * QROW, CY))


def lanes(shape):
    return lax.broadcasted_iota(jnp.int32, shape, len(shape) - 1)


def rows_of(start, count, step=16):
    return pl.ds(pl.multiple_of(start, step), count)


def cell_rows(v, x):
    return rows_of(v * EXT + (x + 1) * CY, CY)


def pack_xy(ext, pa, pb):
    for seg, x in ((0, CX - 1), (FACE, 0)):
        for v in range(NV):
            pa[pl.ds(seg + v * 16, 16), :] = ext[pl.ds(v * EXT + (x + 1) * CY, CY), :]
    for seg, y in ((0, CY - 1), (FACE, 0)):
        for v in range(NV):
            pb[pl.ds(seg + v * 16, 16), :] = ext[pl.ds(v * EXT + CY + y, CX, stride=CY), :]


def pack_z(values, x, pa, pb):
    lane = lanes((CY, CZ))
    up = pa[pl.ds(2 * FACE, CY), :]
    low = pb[pl.ds(2 * FACE, CY), :]
    for v in range(NV):
        at = v * 16 + x
        here = lane == at
        up = jnp.where(here, pltpu.roll(values[v], at + 1, 1), up)
        low = jnp.where(here, pltpu.roll(values[v], at, 1), low)
    pa[pl.ds(2 * FACE, CY), :] = up
    pb[pl.ds(2 * FACE, CY), :] = low


def clear_z(pa, pb):
    pa[pl.ds(2 * FACE, CY), :] = jnp.zeros((CY, CZ), F32)
    pb[pl.ds(2 * FACE, CY), :] = jnp.zeros((CY, CZ), F32)


def lane_flip(piece, flag, width):
    lane = lanes(piece.shape)
    at = lane & (width - 1)
    return jnp.take_along_axis(piece, lane + flag * (width - 1 - 2 * at), axis=1)


def row_flip(piece, flag):
    row = lax.broadcasted_iota(jnp.int32, (8, CZ), 0)
    index = row + flag * (7 - 2 * row)
    first, second = piece[:8], piece[8:]
    turned = flag == 1
    lower = jnp.where(turned, second, first)
    upper = jnp.where(turned, first, second)
    return [jnp.take_along_axis(lower, index, axis=0), jnp.take_along_axis(upper, index, axis=0)]


def place_ghosts(layer, code, ext, gy, gz):
    for f in range(6):
        first, second = code[f] & 1, (code[f] >> 1) & 1
        if f < 4:
            for v in range(NV):
                for h, piece in enumerate(row_flip(layer(f, v), first)):
                    piece = lane_flip(piece, second, CZ)
                    if f < 2:
                        start = v * EXT + ((CX + 1) * CY if f == 0 else 0)
                        ext[pl.ds(start + 8 * h, 8), :] = piece
                    else:
                        gy[pl.ds((f - 2) * FACE + v * 16 + 8 * h, 8), :] = piece
        else:
            for h, piece in enumerate(row_flip(layer(f, 0), second)):
                gz[pl.ds((f - 4) * CY + 8 * h, 8), :] = lane_flip(piece, first, CX)


def forward_layers(ghost):
    def face(f):
        start = {1: 0, 0: QROW, 3: QA, 2: QA + QROW}[f]
        return jnp.concatenate([ghost[c, pl.ds(start, QROW), :] for c in range(NC)])

    faces = {f: face(f) for f in range(4)}

    def layer(f, v):
        if f < 4:
            return faces[f][v * 16 : v * 16 + 16]
        c = 0 if f == 5 else 2
        return jnp.concatenate([ghost[c, pl.ds(2 * QROW, 8), :], ghost[c + 1, pl.ds(2 * QROW, 8), :]])

    return layer


def strip_layers(ghost):
    lane = lanes((CY, CZ))

    def layer(f, v):
        if f < 2:
            start = (1 - f) * QROW
            rows = range(v * 16, v * 16 + 16, 8)
            return jnp.concatenate(
                [ghost[r // QROW, pl.ds(start + r % QROW, 8), :] for r in rows]
            )
        if f < 4:
            start = QX + (3 - f) * QROW + v * STRIP
            return jnp.concatenate([ghost[c, pl.ds(start, STRIP), :] for c in range(NC)])
        start = 2 * QROW if f == 5 else QX + 2 * QROW
        out = ghost[0, pl.ds(start, CY), :]
        for c in range(1, NC):
            out = jnp.where((lane & 15) // STRIP == c, ghost[c, pl.ds(start, CY), :], out)
        return out

    return layer


def pack_strip(part, c, xface, ba, bb):
    lane = lanes((CY, CZ))
    for seg, y in ((0, CY - 1), (QROW, 0)):
        for v in range(NV):
            bb[0, pl.ds(seg + v * STRIP, STRIP), :] = part[pl.ds(v * 64 + y, STRIP, stride=CY), :]
    up = jnp.zeros((CY, CZ), F32)
    low = jnp.zeros((CY, CZ), F32)
    for v in range(NV):
        for x in range(STRIP):
            value = part[pl.ds(v * 64 + x * CY, CY), :]
            at = v * 16 + c * STRIP + x
            here = lane == at
            up = jnp.where(here, pltpu.roll(value, at + 1, 1), up)
            low = jnp.where(here, pltpu.roll(value, at, 1), low)
            if x == STRIP - 1:
                xface[0, pl.ds(v * 16, 16), :] = value
            if x == 0:
                xface[1, pl.ds(v * 16, 16), :] = value
    ba[0, pl.ds(2 * QROW, CY), :] = up
    bb[0, pl.ds(2 * QROW, CY), :] = low


class EndLayers:
    def __init__(self, place, xface, share, send, recv, base):
        self.place, self.xface, self.share = place, xface, share
        self.send, self.recv, self.base = send, recv, base

    def copy(self, n, who, member):
        return pltpu.make_async_remote_copy(
            src_ref=self.xface.at[n, pl.ds(member * QROW, QROW)],
            dst_ref=self.share.at[n],
            send_sem=self.send.at[self.base + n * NC + member],
            recv_sem=self.recv.at[self.base + n],
            device_id=(member, lax.axis_index("space")),
            device_id_type=MESH,
        )

    def each(self, holder, other):
        for n, who in ((0, NC - 1), (1, 0)):
            members = [m for m in range(NC) if m != who]
            if holder is not None:

                @pl.when(self.place.c == who)
                def _():
                    holder(n, who, members)

            if other is not None:

                @pl.when(self.place.c != who)
                def _():
                    other(n, who, members)

    def begin(self):
        def give(n, who, members):
            for m in members:
                self.copy(n, who, m).start()
            self.share[n] = self.xface[n, pl.ds(who * QROW, QROW), :]

        self.each(give, None)

    def take(self):
        self.each(None, lambda n, who, members: self.copy(n, who, members[0]).wait_recv())

    def drain(self):
        self.each(lambda n, who, members: [self.copy(n, who, m).wait_send() for m in members], None)


class Gather:
    def __init__(self, place, part, stored, send, recv, base):
        self.place, self.part, self.stored = place, part, stored
        self.send, self.recv, self.base = send, recv, base
        self.all = []

    def copy(self, src, slot, member):
        n = self.base + len(self.all)
        made = pltpu.make_async_remote_copy(
            src_ref=src,
            dst_ref=self.stored.at[slot],
            send_sem=self.send.at[n],
            recv_sem=self.recv.at[n],
            device_id=(member, lax.axis_index("space")),
            device_id_type=MESH,
        )
        made.start()
        self.all.append(made)

    def begin(self):
        c = self.place.c
        self.core = c + 1 - 2 * lax.rem(c, 2)
        self.far = lax.rem(c + 2, NC)
        self.copy(self.part, c, self.far)
        self.copy(self.part, c, self.core)
        self.stored[c] = self.part[...]

    def relay(self):
        self.all[0].wait_recv()
        self.copy(self.stored.at[self.far], self.far, self.core)

    def take(self):
        for made in self.all[1:]:
            made.wait_recv()

    def drain(self):
        for made in self.all:
            made.wait_send()


def adjoint_layers(ga, gb):
    def layer(f, v):
        half = ga if f in (0, 1, 5) else gb
        if f < 4:
            return half[pl.ds((1 - f % 2) * FACE + v * 16, 16), :]
        return half[pl.ds(2 * FACE, CY), :]

    return layer


def neighbours_of(grid, x, stand=None):
    ext, gy, gz = grid
    row = lax.broadcasted_iota(jnp.int32, (CY, CZ), 0)
    lane = lanes((CY, CZ))
    centre = [ext[cell_rows(v, x), :] for v in range(NV)]

    def at(direction):
        ups, lows = [], []
        for v in range(NV):
            u = centre[v]
            at_x = v * 16 + x
            if direction == 0:
                up = ext[cell_rows(v, x + 1), :]
                low = ext[cell_rows(v, x - 1), :]
            elif stand is not None:
                axis, size = direction - 1, (CY, CZ)[direction - 1]
                at_side = (row, lane)[axis]
                other = u if stand == "own" else jnp.zeros_like(u)
                up = jnp.where(at_side == size - 1, other, pltpu.roll(u, size - 1, axis))
                low = jnp.where(at_side == 0, other, pltpu.roll(u, 1, axis))
            elif direction == 1:
                up = jnp.where(row == CY - 1, gy[pl.ds(at_x, 1), :], pltpu.roll(u, CY - 1, 0))
                low = jnp.where(row == 0, gy[pl.ds(FACE + at_x, 1), :], pltpu.roll(u, 1, 0))
            else:
                high = pltpu.roll(gz[pl.ds(0, CY), :], CZ - 1 - at_x, 1)
                deep = pltpu.roll(gz[pl.ds(CY, CY), :], lax.rem(CZ - at_x, CZ), 1)
                up = jnp.where(lane == CZ - 1, high, pltpu.roll(u, CZ - 1, 1))
                low = jnp.where(lane == 0, deep, pltpu.roll(u, 1, 1))
            ups.append(up)
            lows.append(low)
        return ups, lows

    return centre, at


def spread_of(first, second):
    mean = 0.5 * (first + second)
    t = 1.0 + mean * mean
    r = lax.rsqrt(t)
    return t * r, mean * r


def forward_step(mats, rate, grid, out, pa, pb, x, stand=None):
    u, at = neighbours_of(grid, x, stand)
    total = [jnp.zeros((CY, CZ), F32) for _ in range(NV)]
    for d in range(3):
        up, low = at(d)
        su, _ = spread_of(up[0], u[0])
        sl, _ = spread_of(u[0], low[0])
        diff = [up[v] - low[v] for v in range(NV)]
        for i in range(NV):
            acc = total[i] - (su * (up[i] - u[i]) - sl * (u[i] - low[i]))
            for j in range(NV):
                acc = acc + mats[d, i, j] * diff[j]
            total[i] = acc
    tau = (0.5 * TAU) * rate[rows_of(x * CY, CY), :]
    new = [u[v] - tau * total[v] - DAMP * jnp.tanh(u[v]) for v in range(NV)]
    for v in range(NV):
        if pa is None:
            out[rows_of(v * 256 + x * CY, CY), :] = new[v]
        else:
            out[cell_rows(v, x), :] = new[v]
    if pa is not None:
        pack_z(new if stand is None else u, x, pa, pb)


def adjoint_step(mats, grid, wgrid, lam, out, x, stand=None):
    u, at_u = neighbours_of(grid, x, stand)
    w, at_w = neighbours_of(wgrid, x, "zero")
    total = [jnp.zeros((CY, CZ), F32) for _ in range(NV)]
    tilt = jnp.zeros((CY, CZ), F32)
    for d in range(3):
        up, low = at_u(d)
        wup, wlow = at_w(d)
        su, ru = spread_of(up[0], u[0])
        sl, rl = spread_of(u[0], low[0])
        dot_u = jnp.zeros((CY, CZ), F32)
        dot_l = jnp.zeros((CY, CZ), F32)
        wdiff = []
        for i in range(NV):
            du, dl = up[i] - u[i], u[i] - low[i]
            gu, gl = wup[i] - w[i], w[i] - wlow[i]
            dot_u = dot_u + du * gu
            dot_l = dot_l + dl * gl
            total[i] = total[i] + (su * gu - sl * gl)
            wdiff.append(wup[i] - wlow[i])
        tilt = tilt + ru * dot_u + rl * dot_l
        for i in range(NV):
            acc = total[i]
            for j in range(NV):
                acc = acc + mats[d, j, i] * wdiff[j]
            total[i] = acc
    for v in range(NV):
        here = rows_of(v * 256 + x * CY, CY)
        bent = jnp.tanh(u[v])
        old = lam[here, :]
        new = old - DAMP * (1.0 - bent * bent) * old + 0.5 * total[v]
        if v == 0:
            new = new - 0.25 * tilt
        out[here, :] = new


def own_tile(f, v, pa, pb):
    half = (pa, pa, pb, pb, pa, pb)[f]
    if f < 4:
        return half[pl.ds((f % 2) * FACE + v * 16, 16), :]
    return pltpu.roll(half[pl.ds(2 * FACE, CY), :], (CZ - v * 16) % CZ, 1)


def ghost_tile(f, v, grid):
    ext, gy, gz = grid
    if f < 2:
        return ext[pl.ds(v * EXT + ((CX + 1) * CY if f == 0 else 0), CY), :]
    if f < 4:
        return gy[pl.ds((f - 2) * FACE + v * 16, 16), :]
    return pltpu.roll(gz[pl.ds((f - 4) * CY, CY), :], (CZ - v * 16) % CZ, 1)


def own_planes(ext):
    for v in range(NV):
        for ghost, x in ((0, 0), (CX + 1, CX - 1)):
            ext[pl.ds(v * EXT + ghost * CY, CY), :] = ext[pl.ds(v * EXT + (x + 1) * CY, CY), :]


def forward_fix(f, mats, grid, pa, pb):
    sign = -0.5 if f % 2 == 0 else 0.5
    own = [own_tile(f, v, pa, pb) for v in range(NV)]
    across = [ghost_tile(f, v, grid) for v in range(NV)]
    delta = [g - u for g, u in zip(across, own)]
    spread, _ = spread_of(across[0], own[0])
    fixes = []
    for i in range(NV):
        acc = mats[f // 2, i, 0] * delta[0]
        for j in range(1, NV):
            acc = acc + mats[f // 2, i, j] * delta[j]
        fixes.append(sign * acc + 0.5 * spread * delta[i])
    return fixes


def adjoint_fix(f, mats, grid, wgrid, pa, pb, qa=None, qb=None):
    sign = 0.5 if f % 2 == 0 else -0.5
    own = [own_tile(f, v, pa, pb) for v in range(NV)]
    across = [ghost_tile(f, v, grid) for v in range(NV)]
    w = [ghost_tile(f, v, wgrid) for v in range(NV)]
    spread, ratio = spread_of(across[0], own[0])
    if qa is None:
        jump, kept = w, None
    else:
        mine = [own_tile(f, v, qa, qb) for v in range(NV)]
        jump = [a - b for a, b in zip(w, mine)]
        kept, _ = spread_of(own[0], own[0])
    dot = jnp.zeros((CY, CZ), F32)
    for i in range(NV):
        dot = dot + (across[i] - own[i]) * jump[i]
    fixes = []
    for i in range(NV):
        acc = mats[f // 2, 0, i] * w[0]
        for j in range(1, NV):
            acc = acc + mats[f // 2, j, i] * w[j]
        lean = spread * jump[i]
        if kept is not None:
            lean = lean + kept * mine[i]
        fixes.append(sign * acc + 0.5 * lean)
    fixes[0] = fixes[0] - 0.25 * ratio * dot
    return fixes


def repair(fix, out, stride, offset, fz, rate=None, pa=None, pb=None, weighted=None, weight=None):
    for f in range(4):
        fixes = fix(f)
        first = f % 2 == 1
        if f < 2:
            x = 0 if first else CX - 1
            tau = None if rate is None else TAU * rate[pl.ds(x * CY, CY), :]
            rows = [pl.ds(v * stride + offset + x * CY, CY) for v in range(NV)]
        else:
            y = 0 if first else CY - 1
            tau = None if rate is None else TAU * rate[pl.ds(y, CX, stride=CY), :]
            rows = [pl.ds(v * stride + offset + y, CX, stride=CY) for v in range(NV)]
        for v in range(NV):
            out[rows[v], :] = out[rows[v], :] + (fixes[v] if tau is None else tau * fixes[v])
    for f in (4, 5):
        for v, value in enumerate(fix(f)):
            fz[pl.ds(((f - 4) * NV + v) * CY, CY), :] = value
    lane = lanes((CY, CZ))

    def sides(x):
        tau = None if rate is None else TAU * rate[rows_of(x * CY, CY), :]
        values = []
        for v in range(NV):
            up = pltpu.roll(fz[pl.ds(v * CY, CY), :], CZ - 1 - x, 1)
            low = pltpu.roll(fz[pl.ds((NV + v) * CY, CY), :], lax.rem(CZ - x, CZ), 1)
            add = jnp.where(lane == CZ - 1, up, jnp.where(lane == 0, low, 0.0))
            here = rows_of(v * stride + offset + x * CY, CY)
            value = out[here, :] + (add if tau is None else tau * add)
            out[here, :] = value
            if weighted is not None:
                value = value * (TAU * weight[rows_of(x * CY, CY), :])
                weighted[cell_rows(v, x), :] = value
            values.append(value)
        if pa is not None:
            pack_z(values, x, pa, pb)

    each_x(sides)


def each_x(step, start=0, stop=CX):
    def body(x, carry):
        step(x)
        return carry

    lax.fori_loop(start, stop, body, 0)


class Place:
    def __init__(self):
        self.c = lax.axis_index("ckpt")
        s = lax.axis_index("space")
        self.z = lax.rem(s, NZ)
        self.x = lax.rem(lax.div(s, NZ), NX)
        self.y = lax.div(s, NZ * NX)

    def space(self, x, y, z):
        return (y * NX + x) * NZ + z

    def along_x(self, k):
        return (self.c, self.space(lax.rem(self.x + k, NX), self.y, self.z))

    def along_y(self, k):
        return (self.c, self.space(self.x, lax.rem(self.y + k, NY), self.z))

    def across_z(self):
        return (self.c, self.space(self.x, self.y, 1 - self.z))

    def member(self, k):
        return (lax.rem(self.c + k, NC), lax.axis_index("space"))


def greet(place, members):
    barrier = pltpu.get_barrier_semaphore()
    partners = [place.across_z()]
    partners += [place.along_x(k) for k in range(1, NX)]
    partners += [place.along_y(k) for k in range(1, NY)]
    if members:
        partners += [place.member(k) for k in range(1, NC)]
    for partner in partners:
        pl.semaphore_signal(barrier, inc=1, device_id=partner, device_id_type=MESH)
    return lambda: pl.semaphore_wait(barrier, len(partners))


class Tables:
    def __init__(self, place, owner, links):
        self.place = place
        spots = [place.space(place.x, lax.rem(place.y + k, NY), place.z) for k in range(NY)]
        spots += [place.space(lax.rem(place.x + k, NX), place.y, place.z) for k in range(1, NX)]

        def find(b, found):
            who = owner[b]
            return tuple(jnp.where(who == s, b, f) for f, s in zip(found, spots))

        blocks = lax.fori_loop(0, NX * NY * NZ, find, tuple(jnp.int32(0) for _ in spots))
        self.own = blocks[0]
        self.down = {"A": list(blocks[:NY]), "B": [blocks[0]] + list(blocks[NY:])}
        self.owner, self.links = owner, links

    def source(self, block, layer):
        s = self.owner[self.links[layer ^ 1, block]]
        return lax.rem(lax.div(s, NZ), NX), lax.div(s, NZ * NX), lax.rem(s, NZ)

    def slot(self, half, k, layer):
        x, y, z = self.source(self.down[half][k], layer)
        turn = jnp.where(z == self.place.z, 0, 1)
        if half == "A":
            return turn * NX + lax.rem(self.place.x - x + NX, NX)
        return turn * NY + lax.rem(self.place.y - y + NY, NY)

    def last(self, half, layer):
        x, y, _ = self.source(self.own, layer)
        if half == "A":
            return lax.rem(self.place.y - y + NY, NY)
        return lax.rem(self.place.x - x + NX, NX)


RING = NX
HOPS = (2, 1, 3)
N_COPIES = 1 + 3 * len(HOPS)


class Exchange:
    def __init__(self, place, parts, scratch, send, recv, base):
        self.place, self.parts = place, parts
        self.bufs, self.outs, self.arrivals = (
            dict(zip(parts, scratch[n::3])) for n in range(3)
        )
        self.send, self.recv, self.base = send, recv, base
        self.all = []
        self.first = {"A": place.along_x, "B": place.along_y}
        self.second = {"A": place.along_y, "B": place.along_x}
        self.across = {}
        self.own = {part: [] for part in parts}
        self.passed = {part: [] for part in parts}
        self.final = {part: [] for part in parts}

    def copy(self, src, dst, device):
        n = self.base + len(self.all)
        made = pltpu.make_async_remote_copy(
            src_ref=src,
            dst_ref=dst,
            send_sem=self.send.at[n],
            recv_sem=self.recv.at[n],
            device_id=device,
            device_id_type=MESH,
        )
        made.start()
        self.all.append(made)
        return made

    def send_across(self, parts=None):
        for part in parts or self.parts:
            buf = self.bufs[part]
            self.across[part] = self.copy(buf.at[0], buf.at[RING], self.place.across_z())

    def send_own(self, parts=None):
        for part in parts or self.parts:
            buf, away = self.bufs[part], self.first[part[0]]
            for k in HOPS:
                self.own[part].append(self.copy(buf.at[0], buf.at[k], away(k)))

    def relay(self):
        for part in self.parts:
            buf, away = self.bufs[part], self.first[part[0]]
            self.across[part].wait_recv()
            for k in HOPS:
                self.passed[part].append(self.copy(buf.at[RING], buf.at[RING + k], away(k)))

    def hand_on(self, tables, segments):
        for part in self.parts:
            for made in self.own[part] + self.passed[part]:
                made.wait_recv()
            buf, out, arrive = self.bufs[part], self.outs[part], self.arrivals[part]
            for k in HOPS + (0,):
                for start, count, layer in segments[part]:
                    picked = buf[tables.slot(part[0], k, layer), pl.ds(start, count), :]
                    if k == 0:
                        arrive[0, pl.ds(start, count), :] = picked
                    else:
                        out[k - 1, pl.ds(start, count), :] = picked
                if k:
                    self.final[part].append(
                        self.copy(out.at[k - 1], arrive.at[k], self.second[part[0]](k))
                    )

    def take(self, tables, segments, put):
        for part in self.parts:
            for made in self.final[part]:
                made.wait_recv()
            arrive = self.arrivals[part]
            for start, count, layer in segments[part]:
                put(part, start, count, arrive[tables.last(part[0], layer), pl.ds(start, count), :])

    def drain(self):
        for made in self.all:
            made.wait_send()


WHOLES = ("A1", "B1", "A2", "B2")
BIG = FACE + CY


def full_segments():
    return {
        "A1": [(0, FACE, 0), (FACE, CY, 4)],
        "B1": [(0, FACE, 2), (FACE, CY, 5)],
        "A2": [(0, FACE, 1)],
        "B2": [(0, FACE, 3)],
    }


def whole_packet(pa, pb, exchange):
    for source, name in ((pa, "A"), (pb, "B")):
        one, two = exchange.bufs[name + "1"], exchange.bufs[name + "2"]
        one[0, pl.ds(0, FACE), :] = source[pl.ds(0, FACE), :]
        one[0, pl.ds(FACE, CY), :] = source[pl.ds(2 * FACE, CY), :]
        two[0, pl.ds(0, FACE), :] = source[pl.ds(FACE, FACE), :]


def quarter_segments(c):
    zface = jnp.where(c < 2, 4, 5)
    return {
        "A": [(s, n, f) for (s, n), f in zip(SEGS_QA, (0, 1, zface))],
        "B": [(s, n, f) for (s, n), f in zip(SEGS_QB, (2, 3))],
    }


def strip_segments():
    return {
        "A": [(s, n, f) for (s, n), f in zip(SEGS_QX, (0, 1, 4))],
        "B": [(s, n, f) for (s, n), f in zip(SEGS_QX, (2, 3, 5))],
    }


def exchange_scratch(*rows):
    made = []
    for r in rows:
        for slots in (2 * RING, RING - 1, RING):
            made.append(VMEM((slots, r, CZ), F32))
    return made


def quarter_packet(c, pa, pb, ba, bb):
    part = rows_of(c * QROW, QROW, 8)
    part2 = rows_of(FACE + c * QROW, QROW, 8)
    ba[0, pl.ds(0, QROW), :] = pa[part, :]
    ba[0, pl.ds(QROW, QROW), :] = pa[part2, :]
    bb[0, pl.ds(0, QROW), :] = pb[part, :]
    bb[0, pl.ds(QROW, QROW), :] = pb[part2, :]
    zrows = rows_of(2 * FACE + lax.rem(c, 2) * 8, 8, 8)
    ba[0, pl.ds(2 * QROW, 8), :] = jnp.where(c < 2, pa[zrows, :], pb[zrows, :])


def share(place, mine, ghost, send, recv, base):
    made = []
    for k in range(1, NC):
        copy = pltpu.make_async_remote_copy(
            src_ref=mine,
            dst_ref=ghost.at[place.c],
            send_sem=send.at[base + k - 1],
            recv_sem=recv.at[base + k - 1],
            device_id=place.member(k),
            device_id_type=MESH,
        )
        copy.start()
        made.append(copy)
    ghost[place.c] = mine[...]
    return made


def put_into(mine, second):
    def put(half, start, count, value):
        mine[pl.ds((0 if half == "A" else second) + start, count), :] = value

    return put


def put_halves(wa, wb):
    def put(half, start, count, value):
        at = FACE if half[1] == "2" else 2 * start
        (wa if half[0] == "A" else wb)[pl.ds(at, count), :] = value

    return put


def kernel(owner, links, codes, mats, part, seeds, rate, adjoint, final, *scratch):
    first, second = scratch[0:6], scratch[6:12]
    third, fourth = scratch[12:24], scratch[24:36]
    scratch = scratch[36:]
    grid0, grid1, wgrid, wgrid1 = (scratch[3 * n : 3 * n + 3] for n in range(4))
    pa, pb, mine, mine1, stored, landed, landed1, wa, wb, lam, xface, xshare, pu, pw, qa, qb, fz, send, recv = scratch[12:]
    place = Place()
    early = Exchange(place, "AB", first, send, recv, 0)
    again = Exchange(place, "AB", second, send, recv, 2 * N_COPIES)
    late = Exchange(place, WHOLES, third, send, recv, 4 * N_COPIES)
    back = Exchange(place, WHOLES, fourth, send, recv, 8 * N_COPIES)
    base = 12 * N_COPIES
    gather = Gather(place, part, stored, send, recv, base + 6)
    ends = EndLayers(place, xface, xshare, send, recv, base + 9)
    strips, quarters, wholes = strip_segments(), quarter_segments(place.c), full_segments()

    met = greet(place, True)
    pack_strip(part, place.c, xface, early.bufs["A"], early.bufs["B"])
    met()
    ends.begin()
    early.send_across("B")
    early.send_own("B")
    ends.take()
    for n in range(2):
        early.bufs["A"][0, pl.ds(n * QROW, QROW), :] = xshare[n]
    early.send_across("A")
    early.send_own("A")
    gather.begin()

    clear_z(qa, qb)
    for v in range(NV):
        for ghost in (0, CX + 1):
            wgrid[0][pl.ds(v * EXT + ghost * CY, CY), :] = jnp.zeros((CY, CZ), F32)
            wgrid1[0][pl.ds(v * EXT + ghost * CY, CY), :] = jnp.zeros((CY, CZ), F32)

    def weigh(x):
        tau = TAU * rate[rows_of(x * CY, CY), :]
        values = [seeds[rows_of(v * 256 + x * CY, CY), :] * tau for v in range(NV)]
        for v in range(NV):
            wgrid[0][cell_rows(v, x), :] = values[v]
        pack_z(values, x, qa, qb)

    each_x(weigh)
    pack_xy(wgrid[0], qa, qb)
    whole_packet(qa, qb, late)
    early.relay()
    late.send_across()
    tables = Tables(place, owner, links)
    code = [codes[f, tables.own] for f in range(6)]
    gather.relay()
    early.hand_on(tables, strips)
    late.send_own()
    early.take(tables, strips, put_into(mine, QX))
    shared = share(place, mine, landed, send, recv, base)
    gather.take()
    span = CX * CY // NC
    for c in range(NC):
        for v in range(NV):
            grid0[0][pl.ds(v * EXT + CY + c * span, span), :] = stored[c, pl.ds(v * span, span), :]
    own_planes(grid0[0])
    clear_z(pu, pw)
    pack_xy(grid0[0], pu, pw)
    late.relay()
    each_x(lambda x: forward_step(mats, rate, grid0, grid1[0], pu, pw, x, "own"))
    clear_z(pa, pb)
    for copy in shared:
        copy.wait_recv()
    place_ghosts(strip_layers(landed), code, *grid0)
    repair(
        lambda f: forward_fix(f, mats, grid0, pu, pw), grid1[0], EXT, CY, fz, rate, pa, pb
    )
    pack_xy(grid1[0], pa, pb)

    quarter_packet(place.c, pa, pb, again.bufs["A"], again.bufs["B"])
    again.send_across()
    again.send_own()
    own_planes(grid1[0])

    def middle(x):
        adjoint_step(mats, grid1, wgrid, seeds, lam, x, "own")

    each_x(middle, 0, M0)
    again.relay()
    late.hand_on(tables, wholes)
    each_x(middle, M0, M1)
    again.hand_on(tables, quarters)
    each_x(middle, M1, M2)
    again.take(tables, quarters, put_into(mine1, QA))
    shared1 = share(place, mine1, landed1, send, recv, base + 3)
    each_x(middle, M2, CX)
    late.take(tables, wholes, put_halves(wa, wb))
    place_ghosts(adjoint_layers(wa, wb), code, *wgrid)
    for copy in shared1:
        copy.wait_recv()
    place_ghosts(forward_layers(landed1), code, *grid1)
    repair(
        lambda f: adjoint_fix(f, mats, grid1, wgrid, pa, pb, qa, qb),
        lam,
        CX * CY,
        0,
        fz,
        pa=qa,
        pb=qb,
        weighted=wgrid1[0],
        weight=rate,
    )
    pack_xy(wgrid1[0], qa, qb)

    whole_packet(qa, qb, back)
    back.send_across()
    back.send_own()

    def last(x):
        forward_step(mats, rate, grid1, final, None, None, x)

    def end(x):
        adjoint_step(mats, grid0, wgrid1, lam, adjoint, x)

    each_x(last, 0, 10)
    back.relay()
    each_x(last, 10, CX)
    each_x(end, 0, 4)
    back.hand_on(tables, wholes)
    each_x(end, 4, CX)
    back.take(tables, wholes, put_halves(wa, wb))
    place_ghosts(adjoint_layers(wa, wb), code, *wgrid1)
    repair(lambda f: adjoint_fix(f, mats, grid0, wgrid1, pu, pw), adjoint, CX * CY, 0, fz)

    for copy in shared + shared1:
        copy.wait_send()
    ends.drain()
    for exchange in (gather, early, late, again, back):
        exchange.drain()


def on_device(checkpoint, seeds, cell_rate, flux_mats, owner, neighbours, orientation):
    vm, sm = pltpu.VMEM, pltpu.SMEM
    block = jax.ShapeDtypeStruct((ROWS, CZ), F32)
    strip, quarter = exchange_scratch(QX, QX), exchange_scratch(QA, QB)
    whole = exchange_scratch(BIG, BIG, FACE, FACE)
    grid = [VMEM((NV * EXT, CZ), F32), VMEM((2 * FACE, CZ), F32), VMEM((2 * CY, CZ), F32)]
    half = VMEM((HALF, CZ), F32)
    copies = 17 + 12 * N_COPIES
    adjoint, final = pl.pallas_call(
        kernel,
        out_shape=(block, block),
        in_specs=[pl.BlockSpec(memory_space=m) for m in (sm, sm, sm, sm, vm, vm, vm)],
        out_specs=(pl.BlockSpec(memory_space=vm), pl.BlockSpec(memory_space=vm)),
        scratch_shapes=strip
        + quarter
        + whole * 2
        + grid * 4
        + [half, half, VMEM((2 * QX, CZ), F32), VMEM((QA + QB, CZ), F32)]
        + [VMEM((NC, ROWS // NC, CZ), F32)]
        + [VMEM((NC, 2 * QX, CZ), F32), VMEM((NC, QA + QB, CZ), F32), half, half]
        + [VMEM((ROWS, CZ), F32), VMEM((2, FACE, CZ), F32), VMEM((2, QROW, CZ), F32)]
        + [half, half, half, half, VMEM((2 * NV * CY, CZ), F32)]
        + [pltpu.SemaphoreType.DMA((copies,)), pltpu.SemaphoreType.DMA((copies,))],
        compiler_params=pltpu.CompilerParams(collective_id=0, has_side_effects=True),
    )(
        owner,
        neighbours.T,
        orientation.T,
        flux_mats,
        checkpoint.reshape(ROWS // NC, CZ),
        seeds.reshape(ROWS, CZ),
        cell_rate.reshape(CX * CY, CZ),
    )
    return (
        adjoint.reshape(1, 1, NV, CX, CY, CZ),
        final.reshape(1, NV, CX, CY, CZ),
    )


def solution(mesh):
    return jax.shard_map(
        on_device,
        mesh=mesh,
        in_specs=(
            P("space", None, "ckpt", None, None),
            P("ckpt", "space", None, None, None, None),
            P("space", None, None, None),
            P(),
            P(),
            P(),
            P(),
        ),
        out_specs=(P("ckpt", "space", None, None, None, None), P("space", None, None, None, None)),
        check_vma=False,
    )
```

```python
import jax
import jax.numpy as jnp
from jax import lax
from jax.experimental import pallas as pl
from jax.experimental.pallas import tpu as pltpu
from jax.sharding import PartitionSpec as P

MESH = pl.DeviceIdType.MESH
VMEM = pltpu.VMEM
F32 = jnp.float32

NX, NY, NZ, NC = 4, 4, 2, 4
NV, CX, CY, CZ = 6, 16, 16, 128
ROWS = NV * CX * CY
FACE = NV * CX
EXT = (CX + 2) * CY
TAU = 0.05
DAMP = 0.015
M0, M1, M2 = 5, 6, 10
HALF = 2 * FACE + CY
QROW = FACE // NC
QA, QB = 2 * QROW + 8, 2 * QROW
SEGS = ((0, FACE), (FACE, FACE), (2 * FACE, CY))
SEGS_QA = ((0, QROW), (QROW, QROW), (2 * QROW, 8))
SEGS_QB = ((0, QROW), (QROW, QROW))
STRIP = CX // NC
QX = 2 * QROW + CY
SEGS_QX = ((0, QROW), (QROW, QROW), (2 * QROW, CY))


def lanes(shape):
    return lax.broadcasted_iota(jnp.int32, shape, len(shape) - 1)


def rows_of(start, count, step=16):
    return pl.ds(pl.multiple_of(start, step), count)


def cell_rows(v, x):
    return rows_of(v * EXT + (x + 1) * CY, CY)


def pack_xy(ext, pa, pb):
    for seg, x in ((0, CX - 1), (FACE, 0)):
        for v in range(NV):
            pa[pl.ds(seg + v * 16, 16), :] = ext[pl.ds(v * EXT + (x + 1) * CY, CY), :]
    for seg, y in ((0, CY - 1), (FACE, 0)):
        for v in range(NV):
            pb[pl.ds(seg + v * 16, 16), :] = ext[pl.ds(v * EXT + CY + y, CX, stride=CY), :]


def pack_z(values, x, pa, pb):
    lane = lanes((CY, CZ))
    up = pa[pl.ds(2 * FACE, CY), :]
    low = pb[pl.ds(2 * FACE, CY), :]
    for v in range(NV):
        at = v * 16 + x
        here = lane == at
        up = jnp.where(here, pltpu.roll(values[v], at + 1, 1), up)
        low = jnp.where(here, pltpu.roll(values[v], at, 1), low)
    pa[pl.ds(2 * FACE, CY), :] = up
    pb[pl.ds(2 * FACE, CY), :] = low


def clear_z(pa, pb):
    pa[pl.ds(2 * FACE, CY), :] = jnp.zeros((CY, CZ), F32)
    pb[pl.ds(2 * FACE, CY), :] = jnp.zeros((CY, CZ), F32)


def lane_flip(piece, flag, width):
    lane = lanes(piece.shape)
    at = lane & (width - 1)
    return jnp.take_along_axis(piece, lane + flag * (width - 1 - 2 * at), axis=1)


def row_flip(piece, flag):
    row = lax.broadcasted_iota(jnp.int32, (8, CZ), 0)
    index = row + flag * (7 - 2 * row)
    first, second = piece[:8], piece[8:]
    turned = flag == 1
    lower = jnp.where(turned, second, first)
    upper = jnp.where(turned, first, second)
    return [jnp.take_along_axis(lower, index, axis=0), jnp.take_along_axis(upper, index, axis=0)]


def place_ghosts(layer, code, ext, gy, gz):
    for f in range(6):
        first, second = code[f] & 1, (code[f] >> 1) & 1
        if f < 4:
            for v in range(NV):
                for h, piece in enumerate(row_flip(layer(f, v), first)):
                    piece = lane_flip(piece, second, CZ)
                    if f < 2:
                        start = v * EXT + ((CX + 1) * CY if f == 0 else 0)
                        ext[pl.ds(start + 8 * h, 8), :] = piece
                    else:
                        gy[pl.ds((f - 2) * FACE + v * 16 + 8 * h, 8), :] = piece
        else:
            for h, piece in enumerate(row_flip(layer(f, 0), second)):
                gz[pl.ds((f - 4) * CY + 8 * h, 8), :] = lane_flip(piece, first, CX)


def forward_layers(ghost):
    def face(f):
        start = {1: 0, 0: QROW, 3: QA, 2: QA + QROW}[f]
        return jnp.concatenate([ghost[c, pl.ds(start, QROW), :] for c in range(NC)])

    faces = {f: face(f) for f in range(4)}

    def layer(f, v):
        if f < 4:
            return faces[f][v * 16 : v * 16 + 16]
        c = 0 if f == 5 else 2
        return jnp.concatenate([ghost[c, pl.ds(2 * QROW, 8), :], ghost[c + 1, pl.ds(2 * QROW, 8), :]])

    return layer


def strip_layers(ghost):
    lane = lanes((CY, CZ))

    def layer(f, v):
        if f < 2:
            start = (1 - f) * QROW
            rows = range(v * 16, v * 16 + 16, 8)
            return jnp.concatenate(
                [ghost[r // QROW, pl.ds(start + r % QROW, 8), :] for r in rows]
            )
        if f < 4:
            start = QX + (3 - f) * QROW + v * STRIP
            return jnp.concatenate([ghost[c, pl.ds(start, STRIP), :] for c in range(NC)])
        start = 2 * QROW if f == 5 else QX + 2 * QROW
        out = ghost[0, pl.ds(start, CY), :]
        for c in range(1, NC):
            out = jnp.where((lane & 15) // STRIP == c, ghost[c, pl.ds(start, CY), :], out)
        return out

    return layer


def pack_strip(part, c, xface, ba, bb):
    lane = lanes((CY, CZ))
    for seg, y in ((0, CY - 1), (QROW, 0)):
        for v in range(NV):
            bb[0, pl.ds(seg + v * STRIP, STRIP), :] = part[pl.ds(v * 64 + y, STRIP, stride=CY), :]
    up = jnp.zeros((CY, CZ), F32)
    low = jnp.zeros((CY, CZ), F32)
    for v in range(NV):
        for x in range(STRIP):
            value = part[pl.ds(v * 64 + x * CY, CY), :]
            at = v * 16 + c * STRIP + x
            here = lane == at
            up = jnp.where(here, pltpu.roll(value, at + 1, 1), up)
            low = jnp.where(here, pltpu.roll(value, at, 1), low)
            if x == STRIP - 1:
                xface[0, pl.ds(v * 16, 16), :] = value
            if x == 0:
                xface[1, pl.ds(v * 16, 16), :] = value
    ba[0, pl.ds(2 * QROW, CY), :] = up
    bb[0, pl.ds(2 * QROW, CY), :] = low


class EndLayers:
    def __init__(self, place, xface, share, send, recv, base):
        self.place, self.xface, self.share = place, xface, share
        self.send, self.recv, self.base = send, recv, base

    def copy(self, n, who, member):
        return pltpu.make_async_remote_copy(
            src_ref=self.xface.at[n, pl.ds(member * QROW, QROW)],
            dst_ref=self.share.at[n],
            send_sem=self.send.at[self.base + n * NC + member],
            recv_sem=self.recv.at[self.base + n],
            device_id=(member, lax.axis_index("space")),
            device_id_type=MESH,
        )

    def each(self, holder, other):
        for n, who in ((0, NC - 1), (1, 0)):
            members = [m for m in range(NC) if m != who]
            if holder is not None:

                @pl.when(self.place.c == who)
                def _():
                    holder(n, who, members)

            if other is not None:

                @pl.when(self.place.c != who)
                def _():
                    other(n, who, members)

    def begin(self):
        def give(n, who, members):
            for m in members:
                self.copy(n, who, m).start()
            self.share[n] = self.xface[n, pl.ds(who * QROW, QROW), :]

        self.each(give, None)

    def take(self):
        self.each(None, lambda n, who, members: self.copy(n, who, members[0]).wait_recv())

    def drain(self):
        self.each(lambda n, who, members: [self.copy(n, who, m).wait_send() for m in members], None)


class Gather:
    def __init__(self, place, part, stored, send, recv, base):
        self.place, self.part, self.stored = place, part, stored
        self.send, self.recv, self.base = send, recv, base
        self.all = []

    def copy(self, src, slot, member):
        n = self.base + len(self.all)
        made = pltpu.make_async_remote_copy(
            src_ref=src,
            dst_ref=self.stored.at[slot],
            send_sem=self.send.at[n],
            recv_sem=self.recv.at[n],
            device_id=(member, lax.axis_index("space")),
            device_id_type=MESH,
        )
        made.start()
        self.all.append(made)

    def begin(self):
        c = self.place.c
        self.core = c + 1 - 2 * lax.rem(c, 2)
        self.far = lax.rem(c + 2, NC)
        self.copy(self.part, c, self.far)
        self.copy(self.part, c, self.core)
        self.stored[c] = self.part[...]

    def relay(self):
        self.all[0].wait_recv()
        self.copy(self.stored.at[self.far], self.far, self.core)

    def take(self):
        for made in self.all[1:]:
            made.wait_recv()

    def drain(self):
        for made in self.all:
            made.wait_send()


def adjoint_layers(ga, gb):
    def layer(f, v):
        half = ga if f in (0, 1, 5) else gb
        if f < 4:
            return half[pl.ds((1 - f % 2) * FACE + v * 16, 16), :]
        return half[pl.ds(2 * FACE, CY), :]

    return layer


def neighbours_of(grid, x, stand=None):
    ext, gy, gz = grid
    row = lax.broadcasted_iota(jnp.int32, (CY, CZ), 0)
    lane = lanes((CY, CZ))
    centre = [ext[cell_rows(v, x), :] for v in range(NV)]

    def at(direction):
        ups, lows = [], []
        for v in range(NV):
            u = centre[v]
            at_x = v * 16 + x
            if direction == 0:
                up = ext[cell_rows(v, x + 1), :]
                low = ext[cell_rows(v, x - 1), :]
            elif stand is not None:
                axis, size = direction - 1, (CY, CZ)[direction - 1]
                at_side = (row, lane)[axis]
                other = u if stand == "own" else jnp.zeros_like(u)
                up = jnp.where(at_side == size - 1, other, pltpu.roll(u, size - 1, axis))
                low = jnp.where(at_side == 0, other, pltpu.roll(u, 1, axis))
            elif direction == 1:
                up = jnp.where(row == CY - 1, gy[pl.ds(at_x, 1), :], pltpu.roll(u, CY - 1, 0))
                low = jnp.where(row == 0, gy[pl.ds(FACE + at_x, 1), :], pltpu.roll(u, 1, 0))
            else:
                high = pltpu.roll(gz[pl.ds(0, CY), :], CZ - 1 - at_x, 1)
                deep = pltpu.roll(gz[pl.ds(CY, CY), :], lax.rem(CZ - at_x, CZ), 1)
                up = jnp.where(lane == CZ - 1, high, pltpu.roll(u, CZ - 1, 1))
                low = jnp.where(lane == 0, deep, pltpu.roll(u, 1, 1))
            ups.append(up)
            lows.append(low)
        return ups, lows

    return centre, at


def spread_of(first, second):
    mean = 0.5 * (first + second)
    t = 1.0 + mean * mean
    r = lax.rsqrt(t)
    return t * r, mean * r


def forward_step(mats, rate, grid, out, pa, pb, x, stand=None):
    u, at = neighbours_of(grid, x, stand)
    total = [jnp.zeros((CY, CZ), F32) for _ in range(NV)]
    for d in range(3):
        up, low = at(d)
        su, _ = spread_of(up[0], u[0])
        sl, _ = spread_of(u[0], low[0])
        diff = [up[v] - low[v] for v in range(NV)]
        for i in range(NV):
            acc = total[i] - (su * (up[i] - u[i]) - sl * (u[i] - low[i]))
            for j in range(NV):
                acc = acc + mats[d, i, j] * diff[j]
            total[i] = acc
    tau = (0.5 * TAU) * rate[rows_of(x * CY, CY), :]
    new = [u[v] - tau * total[v] - DAMP * jnp.tanh(u[v]) for v in range(NV)]
    for v in range(NV):
        if pa is None:
            out[rows_of(v * 256 + x * CY, CY), :] = new[v]
        else:
            out[cell_rows(v, x), :] = new[v]
    if pa is not None:
        pack_z(new if stand is None else u, x, pa, pb)


def adjoint_step(mats, grid, wgrid, lam, out, x, stand=None):
    u, at_u = neighbours_of(grid, x, stand)
    w, at_w = neighbours_of(wgrid, x, "zero")
    total = [jnp.zeros((CY, CZ), F32) for _ in range(NV)]
    tilt = jnp.zeros((CY, CZ), F32)
    for d in range(3):
        up, low = at_u(d)
        wup, wlow = at_w(d)
        su, ru = spread_of(up[0], u[0])
        sl, rl = spread_of(u[0], low[0])
        dot_u = jnp.zeros((CY, CZ), F32)
        dot_l = jnp.zeros((CY, CZ), F32)
        wdiff = []
        for i in range(NV):
            du, dl = up[i] - u[i], u[i] - low[i]
            gu, gl = wup[i] - w[i], w[i] - wlow[i]
            dot_u = dot_u + du * gu
            dot_l = dot_l + dl * gl
            total[i] = total[i] + (su * gu - sl * gl)
            wdiff.append(wup[i] - wlow[i])
        tilt = tilt + ru * dot_u + rl * dot_l
        for i in range(NV):
            acc = total[i]
            for j in range(NV):
                acc = acc + mats[d, j, i] * wdiff[j]
            total[i] = acc
    for v in range(NV):
        here = rows_of(v * 256 + x * CY, CY)
        bent = jnp.tanh(u[v])
        old = lam[here, :]
        new = old - DAMP * (1.0 - bent * bent) * old + 0.5 * total[v]
        if v == 0:
            new = new - 0.25 * tilt
        out[here, :] = new


def own_tile(f, v, pa, pb):
    half = (pa, pa, pb, pb, pa, pb)[f]
    if f < 4:
        return half[pl.ds((f % 2) * FACE + v * 16, 16), :]
    return pltpu.roll(half[pl.ds(2 * FACE, CY), :], (CZ - v * 16) % CZ, 1)


def ghost_tile(f, v, grid):
    ext, gy, gz = grid
    if f < 2:
        return ext[pl.ds(v * EXT + ((CX + 1) * CY if f == 0 else 0), CY), :]
    if f < 4:
        return gy[pl.ds((f - 2) * FACE + v * 16, 16), :]
    return pltpu.roll(gz[pl.ds((f - 4) * CY, CY), :], (CZ - v * 16) % CZ, 1)


def own_planes(ext):
    for v in range(NV):
        for ghost, x in ((0, 0), (CX + 1, CX - 1)):
            ext[pl.ds(v * EXT + ghost * CY, CY), :] = ext[pl.ds(v * EXT + (x + 1) * CY, CY), :]


def forward_fix(f, mats, grid, pa, pb):
    sign = -0.5 if f % 2 == 0 else 0.5
    own = [own_tile(f, v, pa, pb) for v in range(NV)]
    across = [ghost_tile(f, v, grid) for v in range(NV)]
    delta = [g - u for g, u in zip(across, own)]
    spread, _ = spread_of(across[0], own[0])
    fixes = []
    for i in range(NV):
        acc = mats[f // 2, i, 0] * delta[0]
        for j in range(1, NV):
            acc = acc + mats[f // 2, i, j] * delta[j]
        fixes.append(sign * acc + 0.5 * spread * delta[i])
    return fixes


def adjoint_fix(f, mats, grid, wgrid, pa, pb, qa=None, qb=None):
    sign = 0.5 if f % 2 == 0 else -0.5
    own = [own_tile(f, v, pa, pb) for v in range(NV)]
    across = [ghost_tile(f, v, grid) for v in range(NV)]
    w = [ghost_tile(f, v, wgrid) for v in range(NV)]
    spread, ratio = spread_of(across[0], own[0])
    if qa is None:
        jump, kept = w, None
    else:
        mine = [own_tile(f, v, qa, qb) for v in range(NV)]
        jump = [a - b for a, b in zip(w, mine)]
        kept, _ = spread_of(own[0], own[0])
    dot = jnp.zeros((CY, CZ), F32)
    for i in range(NV):
        dot = dot + (across[i] - own[i]) * jump[i]
    fixes = []
    for i in range(NV):
        acc = mats[f // 2, 0, i] * w[0]
        for j in range(1, NV):
            acc = acc + mats[f // 2, j, i] * w[j]
        lean = spread * jump[i]
        if kept is not None:
            lean = lean + kept * mine[i]
        fixes.append(sign * acc + 0.5 * lean)
    fixes[0] = fixes[0] - 0.25 * ratio * dot
    return fixes


def repair(fix, out, stride, offset, fz, rate=None, pa=None, pb=None, weighted=None, weight=None):
    for f in range(4):
        fixes = fix(f)
        first = f % 2 == 1
        if f < 2:
            x = 0 if first else CX - 1
            tau = None if rate is None else TAU * rate[pl.ds(x * CY, CY), :]
            rows = [pl.ds(v * stride + offset + x * CY, CY) for v in range(NV)]
        else:
            y = 0 if first else CY - 1
            tau = None if rate is None else TAU * rate[pl.ds(y, CX, stride=CY), :]
            rows = [pl.ds(v * stride + offset + y, CX, stride=CY) for v in range(NV)]
        for v in range(NV):
            out[rows[v], :] = out[rows[v], :] + (fixes[v] if tau is None else tau * fixes[v])
    for f in (4, 5):
        for v, value in enumerate(fix(f)):
            fz[pl.ds(((f - 4) * NV + v) * CY, CY), :] = value
    lane = lanes((CY, CZ))

    def sides(x):
        tau = None if rate is None else TAU * rate[rows_of(x * CY, CY), :]
        values = []
        for v in range(NV):
            up = pltpu.roll(fz[pl.ds(v * CY, CY), :], CZ - 1 - x, 1)
            low = pltpu.roll(fz[pl.ds((NV + v) * CY, CY), :], lax.rem(CZ - x, CZ), 1)
            add = jnp.where(lane == CZ - 1, up, jnp.where(lane == 0, low, 0.0))
            here = rows_of(v * stride + offset + x * CY, CY)
            value = out[here, :] + (add if tau is None else tau * add)
            out[here, :] = value
            if weighted is not None:
                value = value * (TAU * weight[rows_of(x * CY, CY), :])
                weighted[cell_rows(v, x), :] = value
            values.append(value)
        if pa is not None:
            pack_z(values, x, pa, pb)

    each_x(sides)


def each_x(step, start=0, stop=CX):
    def body(x, carry):
        step(x)
        return carry

    lax.fori_loop(start, stop, body, 0)


class Place:
    def __init__(self):
        self.c = lax.axis_index("ckpt")
        s = lax.axis_index("space")
        self.z = lax.rem(s, NZ)
        self.x = lax.rem(lax.div(s, NZ), NX)
        self.y = lax.div(s, NZ * NX)

    def space(self, x, y, z):
        return (y * NX + x) * NZ + z

    def along_x(self, k):
        return (self.c, self.space(lax.rem(self.x + k, NX), self.y, self.z))

    def along_y(self, k):
        return (self.c, self.space(self.x, lax.rem(self.y + k, NY), self.z))

    def across_z(self):
        return (self.c, self.space(self.x, self.y, 1 - self.z))

    def member(self, k):
        return (lax.rem(self.c + k, NC), lax.axis_index("space"))


def greet(place, members):
    barrier = pltpu.get_barrier_semaphore()
    partners = [place.across_z()]
    partners += [place.along_x(k) for k in range(1, NX)]
    partners += [place.along_y(k) for k in range(1, NY)]
    if members:
        partners += [place.member(k) for k in range(1, NC)]
    for partner in partners:
        pl.semaphore_signal(barrier, inc=1, device_id=partner, device_id_type=MESH)
    return lambda: pl.semaphore_wait(barrier, len(partners))


class Tables:
    def __init__(self, place, owner, links):
        self.place = place
        spots = [place.space(place.x, lax.rem(place.y + k, NY), place.z) for k in range(NY)]
        spots += [place.space(lax.rem(place.x + k, NX), place.y, place.z) for k in range(1, NX)]

        def find(b, found):
            who = owner[b]
            return tuple(jnp.where(who == s, b, f) for f, s in zip(found, spots))

        blocks = lax.fori_loop(0, NX * NY * NZ, find, tuple(jnp.int32(0) for _ in spots))
        self.own = blocks[0]
        self.down = {"A": list(blocks[:NY]), "B": [blocks[0]] + list(blocks[NY:])}
        self.owner, self.links = owner, links

    def source(self, block, layer):
        s = self.owner[self.links[layer ^ 1, block]]
        return lax.rem(lax.div(s, NZ), NX), lax.div(s, NZ * NX), lax.rem(s, NZ)

    def slot(self, half, k, layer):
        x, y, z = self.source(self.down[half][k], layer)
        turn = jnp.where(z == self.place.z, 0, 1)
        if half == "A":
            return turn * NX + lax.rem(self.place.x - x + NX, NX)
        return turn * NY + lax.rem(self.place.y - y + NY, NY)

    def last(self, half, layer):
        x, y, _ = self.source(self.own, layer)
        if half == "A":
            return lax.rem(self.place.y - y + NY, NY)
        return lax.rem(self.place.x - x + NX, NX)


RING = NX
HOPS = (2, 1, 3)
N_COPIES = 1 + 3 * len(HOPS)


class Exchange:
    def __init__(self, place, parts, scratch, send, recv, base):
        self.place, self.parts = place, parts
        self.bufs, self.outs, self.arrivals = (
            dict(zip(parts, scratch[n::3])) for n in range(3)
        )
        self.send, self.recv, self.base = send, recv, base
        self.all = []
        self.first = {"A": place.along_x, "B": place.along_y}
        self.second = {"A": place.along_y, "B": place.along_x}
        self.across = {}
        self.own = {part: [] for part in parts}
        self.passed = {part: [] for part in parts}
        self.final = {part: [] for part in parts}

    def copy(self, src, dst, device):
        n = self.base + len(self.all)
        made = pltpu.make_async_remote_copy(
            src_ref=src,
            dst_ref=dst,
            send_sem=self.send.at[n],
            recv_sem=self.recv.at[n],
            device_id=device,
            device_id_type=MESH,
        )
        made.start()
        self.all.append(made)
        return made

    def send_across(self, parts=None):
        for part in parts or self.parts:
            buf = self.bufs[part]
            self.across[part] = self.copy(buf.at[0], buf.at[RING], self.place.across_z())

    def send_own(self, parts=None):
        for part in parts or self.parts:
            buf, away = self.bufs[part], self.first[part[0]]
            for k in HOPS:
                self.own[part].append(self.copy(buf.at[0], buf.at[k], away(k)))

    def relay(self):
        for part in self.parts:
            buf, away = self.bufs[part], self.first[part[0]]
            self.across[part].wait_recv()
            for k in HOPS:
                self.passed[part].append(self.copy(buf.at[RING], buf.at[RING + k], away(k)))

    def hand_on(self, tables, segments):
        for part in self.parts:
            for made in self.own[part] + self.passed[part]:
                made.wait_recv()
            buf, out, arrive = self.bufs[part], self.outs[part], self.arrivals[part]
            for k in HOPS + (0,):
                for start, count, layer in segments[part]:
                    picked = buf[tables.slot(part[0], k, layer), pl.ds(start, count), :]
                    if k == 0:
                        arrive[0, pl.ds(start, count), :] = picked
                    else:
                        out[k - 1, pl.ds(start, count), :] = picked
                if k:
                    self.final[part].append(
                        self.copy(out.at[k - 1], arrive.at[k], self.second[part[0]](k))
                    )

    def take(self, tables, segments, put):
        for part in self.parts:
            for made in self.final[part]:
                made.wait_recv()
            arrive = self.arrivals[part]
            for start, count, layer in segments[part]:
                put(part, start, count, arrive[tables.last(part[0], layer), pl.ds(start, count), :])

    def drain(self):
        for made in self.all:
            made.wait_send()


WHOLES = ("A1", "B1", "A2", "B2")
BIG = FACE + CY


def full_segments():
    return {
        "A1": [(0, FACE, 0), (FACE, CY, 4)],
        "B1": [(0, FACE, 2), (FACE, CY, 5)],
        "A2": [(0, FACE, 1)],
        "B2": [(0, FACE, 3)],
    }


def whole_packet(pa, pb, exchange):
    for source, name in ((pa, "A"), (pb, "B")):
        one, two = exchange.bufs[name + "1"], exchange.bufs[name + "2"]
        one[0, pl.ds(0, FACE), :] = source[pl.ds(0, FACE), :]
        one[0, pl.ds(FACE, CY), :] = source[pl.ds(2 * FACE, CY), :]
        two[0, pl.ds(0, FACE), :] = source[pl.ds(FACE, FACE), :]


def quarter_segments(c):
    zface = jnp.where(c < 2, 4, 5)
    return {
        "A": [(s, n, f) for (s, n), f in zip(SEGS_QA, (0, 1, zface))],
        "B": [(s, n, f) for (s, n), f in zip(SEGS_QB, (2, 3))],
    }


def strip_segments():
    return {
        "A": [(s, n, f) for (s, n), f in zip(SEGS_QX, (0, 1, 4))],
        "B": [(s, n, f) for (s, n), f in zip(SEGS_QX, (2, 3, 5))],
    }


def exchange_scratch(*rows):
    made = []
    for r in rows:
        for slots in (2 * RING, RING - 1, RING):
            made.append(VMEM((slots, r, CZ), F32))
    return made


def quarter_packet(c, pa, pb, ba, bb):
    part = rows_of(c * QROW, QROW, 8)
    part2 = rows_of(FACE + c * QROW, QROW, 8)
    ba[0, pl.ds(0, QROW), :] = pa[part, :]
    ba[0, pl.ds(QROW, QROW), :] = pa[part2, :]
    bb[0, pl.ds(0, QROW), :] = pb[part, :]
    bb[0, pl.ds(QROW, QROW), :] = pb[part2, :]
    zrows = rows_of(2 * FACE + lax.rem(c, 2) * 8, 8, 8)
    ba[0, pl.ds(2 * QROW, 8), :] = jnp.where(c < 2, pa[zrows, :], pb[zrows, :])


def share(place, mine, ghost, send, recv, base):
    made = []
    for k in range(1, NC):
        copy = pltpu.make_async_remote_copy(
            src_ref=mine,
            dst_ref=ghost.at[place.c],
            send_sem=send.at[base + k - 1],
            recv_sem=recv.at[base + k - 1],
            device_id=place.member(k),
            device_id_type=MESH,
        )
        copy.start()
        made.append(copy)
    ghost[place.c] = mine[...]
    return made


def put_into(mine, second):
    def put(half, start, count, value):
        mine[pl.ds((0 if half == "A" else second) + start, count), :] = value

    return put


def put_halves(wa, wb):
    def put(half, start, count, value):
        at = FACE if half[1] == "2" else 2 * start
        (wa if half[0] == "A" else wb)[pl.ds(at, count), :] = value

    return put


def kernel(owner, links, codes, mats, part, seeds, rate, adjoint, final, *scratch):
    first, second = scratch[0:6], scratch[6:12]
    third, fourth = scratch[12:24], scratch[24:36]
    scratch = scratch[36:]
    grid0, grid1, wgrid, wgrid1 = (scratch[3 * n : 3 * n + 3] for n in range(4))
    pa, pb, mine, mine1, stored, landed, landed1, wa, wb, lam, xface, xshare, pu, pw, qa, qb, fz, send, recv = scratch[12:]
    place = Place()
    early = Exchange(place, "AB", first, send, recv, 0)
    again = Exchange(place, "AB", second, send, recv, 2 * N_COPIES)
    late = Exchange(place, WHOLES, third, send, recv, 4 * N_COPIES)
    back = Exchange(place, WHOLES, fourth, send, recv, 8 * N_COPIES)
    base = 12 * N_COPIES
    gather = Gather(place, part, stored, send, recv, base + 6)
    ends = EndLayers(place, xface, xshare, send, recv, base + 9)
    strips, quarters, wholes = strip_segments(), quarter_segments(place.c), full_segments()

    met = greet(place, True)
    pack_strip(part, place.c, xface, early.bufs["A"], early.bufs["B"])
    met()
    ends.begin()
    early.send_across("B")
    early.send_own("B")
    ends.take()
    for n in range(2):
        early.bufs["A"][0, pl.ds(n * QROW, QROW), :] = xshare[n]
    early.send_across("A")
    early.send_own("A")
    gather.begin()

    clear_z(qa, qb)
    for v in range(NV):
        for ghost in (0, CX + 1):
            wgrid[0][pl.ds(v * EXT + ghost * CY, CY), :] = jnp.zeros((CY, CZ), F32)
            wgrid1[0][pl.ds(v * EXT + ghost * CY, CY), :] = jnp.zeros((CY, CZ), F32)

    def weigh(x):
        tau = TAU * rate[rows_of(x * CY, CY), :]
        values = [seeds[rows_of(v * 256 + x * CY, CY), :] * tau for v in range(NV)]
        for v in range(NV):
            wgrid[0][cell_rows(v, x), :] = values[v]
        pack_z(values, x, qa, qb)

    each_x(weigh)
    pack_xy(wgrid[0], qa, qb)
    whole_packet(qa, qb, late)
    early.relay()
    late.send_across()
    tables = Tables(place, owner, links)
    code = [codes[f, tables.own] for f in range(6)]
    gather.relay()
    early.hand_on(tables, strips)
    late.send_own()
    early.take(tables, strips, put_into(mine, QX))
    shared = share(place, mine, landed, send, recv, base)
    gather.take()
    span = CX * CY // NC
    for c in range(NC):
        for v in range(NV):
            grid0[0][pl.ds(v * EXT + CY + c * span, span), :] = stored[c, pl.ds(v * span, span), :]
    own_planes(grid0[0])
    clear_z(pu, pw)
    pack_xy(grid0[0], pu, pw)
    late.relay()
    each_x(lambda x: forward_step(mats, rate, grid0, grid1[0], pu, pw, x, "own"))
    clear_z(pa, pb)
    for copy in shared:
        copy.wait_recv()
    place_ghosts(strip_layers(landed), code, *grid0)
    repair(
        lambda f: forward_fix(f, mats, grid0, pu, pw), grid1[0], EXT, CY, fz, rate, pa, pb
    )
    pack_xy(grid1[0], pa, pb)

    quarter_packet(place.c, pa, pb, again.bufs["A"], again.bufs["B"])
    again.send_across()
    again.send_own()
    own_planes(grid1[0])

    def middle(x):
        adjoint_step(mats, grid1, wgrid, seeds, lam, x, "own")

    each_x(middle, 0, M0)
    again.relay()
    each_x(middle, M0, M1)
    again.hand_on(tables, quarters)
    each_x(middle, M1, M2)
    again.take(tables, quarters, put_into(mine1, QA))
    shared1 = share(place, mine1, landed1, send, recv, base + 3)
    late.hand_on(tables, wholes)
    each_x(middle, M2, CX)
    late.take(tables, wholes, put_halves(wa, wb))
    place_ghosts(adjoint_layers(wa, wb), code, *wgrid)
    for copy in shared1:
        copy.wait_recv()
    place_ghosts(forward_layers(landed1), code, *grid1)
    repair(
        lambda f: adjoint_fix(f, mats, grid1, wgrid, pa, pb, qa, qb),
        lam,
        CX * CY,
        0,
        fz,
        pa=qa,
        pb=qb,
        weighted=wgrid1[0],
        weight=rate,
    )
    pack_xy(wgrid1[0], qa, qb)

    whole_packet(qa, qb, back)
    back.send_across()
    back.send_own()

    def last(x):
        forward_step(mats, rate, grid1, final, None, None, x)

    def end(x):
        adjoint_step(mats, grid0, wgrid1, lam, adjoint, x)

    each_x(last, 0, 10)
    back.relay()
    each_x(last, 10, CX)
    each_x(end, 0, 4)
    back.hand_on(tables, wholes)
    each_x(end, 4, CX)
    back.take(tables, wholes, put_halves(wa, wb))
    place_ghosts(adjoint_layers(wa, wb), code, *wgrid1)
    repair(lambda f: adjoint_fix(f, mats, grid0, wgrid1, pu, pw), adjoint, CX * CY, 0, fz)

    for copy in shared + shared1:
        copy.wait_send()
    ends.drain()
    for exchange in (gather, early, late, again, back):
        exchange.drain()


def on_device(checkpoint, seeds, cell_rate, flux_mats, owner, neighbours, orientation):
    vm, sm = pltpu.VMEM, pltpu.SMEM
    block = jax.ShapeDtypeStruct((ROWS, CZ), F32)
    strip, quarter = exchange_scratch(QX, QX), exchange_scratch(QA, QB)
    whole = exchange_scratch(BIG, BIG, FACE, FACE)
    grid = [VMEM((NV * EXT, CZ), F32), VMEM((2 * FACE, CZ), F32), VMEM((2 * CY, CZ), F32)]
    half = VMEM((HALF, CZ), F32)
    copies = 17 + 12 * N_COPIES
    adjoint, final = pl.pallas_call(
        kernel,
        out_shape=(block, block),
        in_specs=[pl.BlockSpec(memory_space=m) for m in (sm, sm, sm, sm, vm, vm, vm)],
        out_specs=(pl.BlockSpec(memory_space=vm), pl.BlockSpec(memory_space=vm)),
        scratch_shapes=strip
        + quarter
        + whole * 2
        + grid * 4
        + [half, half, VMEM((2 * QX, CZ), F32), VMEM((QA + QB, CZ), F32)]
        + [VMEM((NC, ROWS // NC, CZ), F32)]
        + [VMEM((NC, 2 * QX, CZ), F32), VMEM((NC, QA + QB, CZ), F32), half, half]
        + [VMEM((ROWS, CZ), F32), VMEM((2, FACE, CZ), F32), VMEM((2, QROW, CZ), F32)]
        + [half, half, half, half, VMEM((2 * NV * CY, CZ), F32)]
        + [pltpu.SemaphoreType.DMA((copies,)), pltpu.SemaphoreType.DMA((copies,))],
        compiler_params=pltpu.CompilerParams(collective_id=0, has_side_effects=True),
    )(
        owner,
        neighbours.T,
        orientation.T,
        flux_mats,
        checkpoint.reshape(ROWS // NC, CZ),
        seeds.reshape(ROWS, CZ),
        cell_rate.reshape(CX * CY, CZ),
    )
    return (
        adjoint.reshape(1, 1, NV, CX, CY, CZ),
        final.reshape(1, NV, CX, CY, CZ),
    )


def solution(mesh):
    return jax.shard_map(
        on_device,
        mesh=mesh,
        in_specs=(
            P("space", None, "ckpt", None, None),
            P("ckpt", "space", None, None, None, None),
            P("space", None, None, None),
            P(),
            P(),
            P(),
            P(),
        ),
        out_specs=(P("ckpt", "space", None, None, None, None), P("space", None, None, None, None)),
        check_vma=False,
    )
```

```python
import jax
import jax.numpy as jnp
from jax import lax
from jax.experimental import pallas as pl
from jax.experimental.pallas import tpu as pltpu
from jax.sharding import PartitionSpec as P

MESH = pl.DeviceIdType.MESH
VMEM = pltpu.VMEM
F32 = jnp.float32

NX, NY, NZ, NC = 4, 4, 2, 4
NV, CX, CY, CZ = 6, 16, 16, 128
ROWS = NV * CX * CY
FACE = NV * CX
EXT = (CX + 2) * CY
TAU = 0.05
DAMP = 0.015
M0, M1, M2 = 5, 6, 10
HALF = 2 * FACE + CY
QROW = FACE // NC
QA, QB = 2 * QROW + 8, 2 * QROW
SEGS = ((0, FACE), (FACE, FACE), (2 * FACE, CY))
SEGS_QA = ((0, QROW), (QROW, QROW), (2 * QROW, 8))
SEGS_QB = ((0, QROW), (QROW, QROW))
STRIP = CX // NC
QX = 2 * QROW + CY
SEGS_QX = ((0, QROW), (QROW, QROW), (2 * QROW, CY))


def lanes(shape):
    return lax.broadcasted_iota(jnp.int32, shape, len(shape) - 1)


def rows_of(start, count, step=16):
    return pl.ds(pl.multiple_of(start, step), count)


def cell_rows(v, x):
    return rows_of(v * EXT + (x + 1) * CY, CY)


def pack_xy(ext, pa, pb):
    for seg, x in ((0, CX - 1), (FACE, 0)):
        for v in range(NV):
            pa[pl.ds(seg + v * 16, 16), :] = ext[pl.ds(v * EXT + (x + 1) * CY, CY), :]
    for seg, y in ((0, CY - 1), (FACE, 0)):
        for v in range(NV):
            pb[pl.ds(seg + v * 16, 16), :] = ext[pl.ds(v * EXT + CY + y, CX, stride=CY), :]


def pack_z(values, x, pa, pb):
    lane = lanes((CY, CZ))
    up = pa[pl.ds(2 * FACE, CY), :]
    low = pb[pl.ds(2 * FACE, CY), :]
    for v in range(NV):
        at = v * 16 + x
        here = lane == at
        up = jnp.where(here, pltpu.roll(values[v], at + 1, 1), up)
        low = jnp.where(here, pltpu.roll(values[v], at, 1), low)
    pa[pl.ds(2 * FACE, CY), :] = up
    pb[pl.ds(2 * FACE, CY), :] = low


def clear_z(pa, pb):
    pa[pl.ds(2 * FACE, CY), :] = jnp.zeros((CY, CZ), F32)
    pb[pl.ds(2 * FACE, CY), :] = jnp.zeros((CY, CZ), F32)


def lane_flip(piece, flag, width):
    lane = lanes(piece.shape)
    at = lane & (width - 1)
    return jnp.take_along_axis(piece, lane + flag * (width - 1 - 2 * at), axis=1)


def row_flip(piece, flag):
    row = lax.broadcasted_iota(jnp.int32, (8, CZ), 0)
    index = row + flag * (7 - 2 * row)
    first, second = piece[:8], piece[8:]
    turned = flag == 1
    lower = jnp.where(turned, second, first)
    upper = jnp.where(turned, first, second)
    return [jnp.take_along_axis(lower, index, axis=0), jnp.take_along_axis(upper, index, axis=0)]


def place_ghosts(layer, code, ext, gy, gz):
    for f in range(6):
        first, second = code[f] & 1, (code[f] >> 1) & 1
        if f < 4:
            for v in range(NV):
                for h, piece in enumerate(row_flip(layer(f, v), first)):
                    piece = lane_flip(piece, second, CZ)
                    if f < 2:
                        start = v * EXT + ((CX + 1) * CY if f == 0 else 0)
                        ext[pl.ds(start + 8 * h, 8), :] = piece
                    else:
                        gy[pl.ds((f - 2) * FACE + v * 16 + 8 * h, 8), :] = piece
        else:
            for h, piece in enumerate(row_flip(layer(f, 0), second)):
                gz[pl.ds((f - 4) * CY + 8 * h, 8), :] = lane_flip(piece, first, CX)


def forward_layers(ghost):
    def face(f):
        start = {1: 0, 0: QROW, 3: QA, 2: QA + QROW}[f]
        return jnp.concatenate([ghost[c, pl.ds(start, QROW), :] for c in range(NC)])

    faces = {f: face(f) for f in range(4)}

    def layer(f, v):
        if f < 4:
            return faces[f][v * 16 : v * 16 + 16]
        c = 0 if f == 5 else 2
        return jnp.concatenate([ghost[c, pl.ds(2 * QROW, 8), :], ghost[c + 1, pl.ds(2 * QROW, 8), :]])

    return layer


def strip_layers(ghost):
    lane = lanes((CY, CZ))

    def layer(f, v):
        if f < 2:
            start = (1 - f) * QROW
            rows = range(v * 16, v * 16 + 16, 8)
            return jnp.concatenate(
                [ghost[r // QROW, pl.ds(start + r % QROW, 8), :] for r in rows]
            )
        if f < 4:
            start = QX + (3 - f) * QROW + v * STRIP
            return jnp.concatenate([ghost[c, pl.ds(start, STRIP), :] for c in range(NC)])
        start = 2 * QROW if f == 5 else QX + 2 * QROW
        out = ghost[0, pl.ds(start, CY), :]
        for c in range(1, NC):
            out = jnp.where((lane & 15) // STRIP == c, ghost[c, pl.ds(start, CY), :], out)
        return out

    return layer


def pack_strip(part, c, xface, ba, bb):
    lane = lanes((CY, CZ))
    for seg, y in ((0, CY - 1), (QROW, 0)):
        for v in range(NV):
            bb[0, pl.ds(seg + v * STRIP, STRIP), :] = part[pl.ds(v * 64 + y, STRIP, stride=CY), :]
    up = jnp.zeros((CY, CZ), F32)
    low = jnp.zeros((CY, CZ), F32)
    for v in range(NV):
        for x in range(STRIP):
            value = part[pl.ds(v * 64 + x * CY, CY), :]
            at = v * 16 + c * STRIP + x
            here = lane == at
            up = jnp.where(here, pltpu.roll(value, at + 1, 1), up)
            low = jnp.where(here, pltpu.roll(value, at, 1), low)
            if x == STRIP - 1:
                xface[0, pl.ds(v * 16, 16), :] = value
            if x == 0:
                xface[1, pl.ds(v * 16, 16), :] = value
    ba[0, pl.ds(2 * QROW, CY), :] = up
    bb[0, pl.ds(2 * QROW, CY), :] = low


class EndLayers:
    def __init__(self, place, xface, share, send, recv, base):
        self.place, self.xface, self.share = place, xface, share
        self.send, self.recv, self.base = send, recv, base

    def copy(self, n, who, member):
        return pltpu.make_async_remote_copy(
            src_ref=self.xface.at[n, pl.ds(member * QROW, QROW)],
            dst_ref=self.share.at[n],
            send_sem=self.send.at[self.base + n * NC + member],
            recv_sem=self.recv.at[self.base + n],
            device_id=(member, lax.axis_index("space")),
            device_id_type=MESH,
        )

    def each(self, holder, other):
        for n, who in ((0, NC - 1), (1, 0)):
            members = [m for m in range(NC) if m != who]
            if holder is not None:

                @pl.when(self.place.c == who)
                def _():
                    holder(n, who, members)

            if other is not None:

                @pl.when(self.place.c != who)
                def _():
                    other(n, who, members)

    def begin(self):
        def give(n, who, members):
            for m in members:
                self.copy(n, who, m).start()
            self.share[n] = self.xface[n, pl.ds(who * QROW, QROW), :]

        self.each(give, None)

    def take(self):
        self.each(None, lambda n, who, members: self.copy(n, who, members[0]).wait_recv())

    def drain(self):
        self.each(lambda n, who, members: [self.copy(n, who, m).wait_send() for m in members], None)


class Gather:
    def __init__(self, place, part, stored, send, recv, base):
        self.place, self.part, self.stored = place, part, stored
        self.send, self.recv, self.base = send, recv, base
        self.all = []

    def copy(self, src, slot, member):
        n = self.base + len(self.all)
        made = pltpu.make_async_remote_copy(
            src_ref=src,
            dst_ref=self.stored.at[slot],
            send_sem=self.send.at[n],
            recv_sem=self.recv.at[n],
            device_id=(member, lax.axis_index("space")),
            device_id_type=MESH,
        )
        made.start()
        self.all.append(made)

    def begin(self):
        c = self.place.c
        self.core = c + 1 - 2 * lax.rem(c, 2)
        self.far = lax.rem(c + 2, NC)
        self.copy(self.part, c, self.far)
        self.copy(self.part, c, self.core)
        self.stored[c] = self.part[...]

    def relay(self):
        self.all[0].wait_recv()
        self.copy(self.stored.at[self.far], self.far, self.core)

    def take(self):
        for made in self.all[1:]:
            made.wait_recv()

    def drain(self):
        for made in self.all:
            made.wait_send()


def adjoint_layers(ga, gb):
    def layer(f, v):
        half = ga if f in (0, 1, 5) else gb
        if f < 4:
            return half[pl.ds((1 - f % 2) * FACE + v * 16, 16), :]
        return half[pl.ds(2 * FACE, CY), :]

    return layer


def neighbours_of(grid, x, stand=None):
    ext, gy, gz = grid
    row = lax.broadcasted_iota(jnp.int32, (CY, CZ), 0)
    lane = lanes((CY, CZ))
    centre = [ext[cell_rows(v, x), :] for v in range(NV)]

    def at(direction):
        ups, lows = [], []
        for v in range(NV):
            u = centre[v]
            at_x = v * 16 + x
            if direction == 0:
                up = ext[cell_rows(v, x + 1), :]
                low = ext[cell_rows(v, x - 1), :]
            elif stand is not None:
                axis, size = direction - 1, (CY, CZ)[direction - 1]
                at_side = (row, lane)[axis]
                other = u if stand == "own" else jnp.zeros_like(u)
                up = jnp.where(at_side == size - 1, other, pltpu.roll(u, size - 1, axis))
                low = jnp.where(at_side == 0, other, pltpu.roll(u, 1, axis))
            elif direction == 1:
                up = jnp.where(row == CY - 1, gy[pl.ds(at_x, 1), :], pltpu.roll(u, CY - 1, 0))
                low = jnp.where(row == 0, gy[pl.ds(FACE + at_x, 1), :], pltpu.roll(u, 1, 0))
            else:
                high = pltpu.roll(gz[pl.ds(0, CY), :], CZ - 1 - at_x, 1)
                deep = pltpu.roll(gz[pl.ds(CY, CY), :], lax.rem(CZ - at_x, CZ), 1)
                up = jnp.where(lane == CZ - 1, high, pltpu.roll(u, CZ - 1, 1))
                low = jnp.where(lane == 0, deep, pltpu.roll(u, 1, 1))
            ups.append(up)
            lows.append(low)
        return ups, lows

    return centre, at


def spread_of(first, second):
    mean = 0.5 * (first + second)
    t = 1.0 + mean * mean
    r = lax.rsqrt(t)
    return t * r, mean * r


def forward_step(mats, rate, grid, out, pa, pb, x, stand=None):
    u, at = neighbours_of(grid, x, stand)
    total = [jnp.zeros((CY, CZ), F32) for _ in range(NV)]
    for d in range(3):
        up, low = at(d)
        su, _ = spread_of(up[0], u[0])
        sl, _ = spread_of(u[0], low[0])
        diff = [up[v] - low[v] for v in range(NV)]
        for i in range(NV):
            acc = total[i] - (su * (up[i] - u[i]) - sl * (u[i] - low[i]))
            for j in range(NV):
                acc = acc + mats[d, i, j] * diff[j]
            total[i] = acc
    tau = (0.5 * TAU) * rate[rows_of(x * CY, CY), :]
    new = [u[v] - tau * total[v] - DAMP * jnp.tanh(u[v]) for v in range(NV)]
    for v in range(NV):
        if pa is None:
            out[rows_of(v * 256 + x * CY, CY), :] = new[v]
        else:
            out[cell_rows(v, x), :] = new[v]
    if pa is not None:
        pack_z(new if stand is None else u, x, pa, pb)


def adjoint_step(mats, grid, wgrid, lam, out, x, stand=None):
    u, at_u = neighbours_of(grid, x, stand)
    w, at_w = neighbours_of(wgrid, x, "zero")
    total = [jnp.zeros((CY, CZ), F32) for _ in range(NV)]
    tilt = jnp.zeros((CY, CZ), F32)
    for d in range(3):
        up, low = at_u(d)
        wup, wlow = at_w(d)
        su, ru = spread_of(up[0], u[0])
        sl, rl = spread_of(u[0], low[0])
        dot_u = jnp.zeros((CY, CZ), F32)
        dot_l = jnp.zeros((CY, CZ), F32)
        wdiff = []
        for i in range(NV):
            du, dl = up[i] - u[i], u[i] - low[i]
            gu, gl = wup[i] - w[i], w[i] - wlow[i]
            dot_u = dot_u + du * gu
            dot_l = dot_l + dl * gl
            total[i] = total[i] + (su * gu - sl * gl)
            wdiff.append(wup[i] - wlow[i])
        tilt = tilt + ru * dot_u + rl * dot_l
        for i in range(NV):
            acc = total[i]
            for j in range(NV):
                acc = acc + mats[d, j, i] * wdiff[j]
            total[i] = acc
    for v in range(NV):
        here = rows_of(v * 256 + x * CY, CY)
        bent = jnp.tanh(u[v])
        old = lam[here, :]
        new = old - DAMP * (1.0 - bent * bent) * old + 0.5 * total[v]
        if v == 0:
            new = new - 0.25 * tilt
        out[here, :] = new


def own_tile(f, v, pa, pb):
    half = (pa, pa, pb, pb, pa, pb)[f]
    if f < 4:
        return half[pl.ds((f % 2) * FACE + v * 16, 16), :]
    return pltpu.roll(half[pl.ds(2 * FACE, CY), :], (CZ - v * 16) % CZ, 1)


def ghost_tile(f, v, grid):
    ext, gy, gz = grid
    if f < 2:
        return ext[pl.ds(v * EXT + ((CX + 1) * CY if f == 0 else 0), CY), :]
    if f < 4:
        return gy[pl.ds((f - 2) * FACE + v * 16, 16), :]
    return pltpu.roll(gz[pl.ds((f - 4) * CY, CY), :], (CZ - v * 16) % CZ, 1)


def own_planes(ext):
    for v in range(NV):
        for ghost, x in ((0, 0), (CX + 1, CX - 1)):
            ext[pl.ds(v * EXT + ghost * CY, CY), :] = ext[pl.ds(v * EXT + (x + 1) * CY, CY), :]


def forward_fix(f, mats, grid, pa, pb):
    sign = -0.5 if f % 2 == 0 else 0.5
    own = [own_tile(f, v, pa, pb) for v in range(NV)]
    across = [ghost_tile(f, v, grid) for v in range(NV)]
    delta = [g - u for g, u in zip(across, own)]
    spread, _ = spread_of(across[0], own[0])
    fixes = []
    for i in range(NV):
        acc = mats[f // 2, i, 0] * delta[0]
        for j in range(1, NV):
            acc = acc + mats[f // 2, i, j] * delta[j]
        fixes.append(sign * acc + 0.5 * spread * delta[i])
    return fixes


def adjoint_fix(f, mats, grid, wgrid, pa, pb, qa=None, qb=None):
    sign = 0.5 if f % 2 == 0 else -0.5
    own = [own_tile(f, v, pa, pb) for v in range(NV)]
    across = [ghost_tile(f, v, grid) for v in range(NV)]
    w = [ghost_tile(f, v, wgrid) for v in range(NV)]
    spread, ratio = spread_of(across[0], own[0])
    if qa is None:
        jump, kept = w, None
    else:
        mine = [own_tile(f, v, qa, qb) for v in range(NV)]
        jump = [a - b for a, b in zip(w, mine)]
        kept, _ = spread_of(own[0], own[0])
    dot = jnp.zeros((CY, CZ), F32)
    for i in range(NV):
        dot = dot + (across[i] - own[i]) * jump[i]
    fixes = []
    for i in range(NV):
        acc = mats[f // 2, 0, i] * w[0]
        for j in range(1, NV):
            acc = acc + mats[f // 2, j, i] * w[j]
        lean = spread * jump[i]
        if kept is not None:
            lean = lean + kept * mine[i]
        fixes.append(sign * acc + 0.5 * lean)
    fixes[0] = fixes[0] - 0.25 * ratio * dot
    return fixes


def repair(fix, out, stride, offset, fz, rate=None, pa=None, pb=None, weighted=None, weight=None):
    for f in range(4):
        fixes = fix(f)
        first = f % 2 == 1
        if f < 2:
            x = 0 if first else CX - 1
            tau = None if rate is None else TAU * rate[pl.ds(x * CY, CY), :]
            rows = [pl.ds(v * stride + offset + x * CY, CY) for v in range(NV)]
        else:
            y = 0 if first else CY - 1
            tau = None if rate is None else TAU * rate[pl.ds(y, CX, stride=CY), :]
            rows = [pl.ds(v * stride + offset + y, CX, stride=CY) for v in range(NV)]
        for v in range(NV):
            out[rows[v], :] = out[rows[v], :] + (fixes[v] if tau is None else tau * fixes[v])
    for f in (4, 5):
        for v, value in enumerate(fix(f)):
            fz[pl.ds(((f - 4) * NV + v) * CY, CY), :] = value
    lane = lanes((CY, CZ))

    def sides(x):
        tau = None if rate is None else TAU * rate[rows_of(x * CY, CY), :]
        values = []
        for v in range(NV):
            up = pltpu.roll(fz[pl.ds(v * CY, CY), :], CZ - 1 - x, 1)
            low = pltpu.roll(fz[pl.ds((NV + v) * CY, CY), :], lax.rem(CZ - x, CZ), 1)
            add = jnp.where(lane == CZ - 1, up, jnp.where(lane == 0, low, 0.0))
            here = rows_of(v * stride + offset + x * CY, CY)
            value = out[here, :] + (add if tau is None else tau * add)
            out[here, :] = value
            if weighted is not None:
                value = value * (TAU * weight[rows_of(x * CY, CY), :])
                weighted[cell_rows(v, x), :] = value
            values.append(value)
        if pa is not None:
            pack_z(values, x, pa, pb)

    each_x(sides)


def each_x(step, start=0, stop=CX):
    def body(x, carry):
        step(x)
        return carry

    lax.fori_loop(start, stop, body, 0)


class Place:
    def __init__(self):
        self.c = lax.axis_index("ckpt")
        s = lax.axis_index("space")
        self.z = lax.rem(s, NZ)
        self.x = lax.rem(lax.div(s, NZ), NX)
        self.y = lax.div(s, NZ * NX)

    def space(self, x, y, z):
        return (y * NX + x) * NZ + z

    def along_x(self, k):
        return (self.c, self.space(lax.rem(self.x + k, NX), self.y, self.z))

    def along_y(self, k):
        return (self.c, self.space(self.x, lax.rem(self.y + k, NY), self.z))

    def across_z(self):
        return (self.c, self.space(self.x, self.y, 1 - self.z))

    def member(self, k):
        return (lax.rem(self.c + k, NC), lax.axis_index("space"))


def greet(place, members):
    barrier = pltpu.get_barrier_semaphore()
    partners = [place.across_z()]
    partners += [place.along_x(k) for k in range(1, NX)]
    partners += [place.along_y(k) for k in range(1, NY)]
    if members:
        partners += [place.member(k) for k in range(1, NC)]
    for partner in partners:
        pl.semaphore_signal(barrier, inc=1, device_id=partner, device_id_type=MESH)
    return lambda: pl.semaphore_wait(barrier, len(partners))


class Tables:
    def __init__(self, place, owner, links):
        self.place = place
        spots = [place.space(place.x, lax.rem(place.y + k, NY), place.z) for k in range(NY)]
        spots += [place.space(lax.rem(place.x + k, NX), place.y, place.z) for k in range(1, NX)]

        def find(b, found):
            who = owner[b]
            return tuple(jnp.where(who == s, b, f) for f, s in zip(found, spots))

        blocks = lax.fori_loop(0, NX * NY * NZ, find, tuple(jnp.int32(0) for _ in spots))
        self.own = blocks[0]
        self.down = {"A": list(blocks[:NY]), "B": [blocks[0]] + list(blocks[NY:])}
        self.owner, self.links = owner, links

    def source(self, block, layer):
        s = self.owner[self.links[layer ^ 1, block]]
        return lax.rem(lax.div(s, NZ), NX), lax.div(s, NZ * NX), lax.rem(s, NZ)

    def slot(self, half, k, layer):
        x, y, z = self.source(self.down[half][k], layer)
        turn = jnp.where(z == self.place.z, 0, 1)
        if half == "A":
            return turn * NX + lax.rem(self.place.x - x + NX, NX)
        return turn * NY + lax.rem(self.place.y - y + NY, NY)

    def last(self, half, layer):
        x, y, _ = self.source(self.own, layer)
        if half == "A":
            return lax.rem(self.place.y - y + NY, NY)
        return lax.rem(self.place.x - x + NX, NX)


RING = NX
HOPS = (2, 1, 3)
N_COPIES = 1 + 3 * len(HOPS)


class Exchange:
    def __init__(self, place, parts, scratch, send, recv, base):
        self.place, self.parts = place, parts
        self.bufs, self.outs, self.arrivals = (
            dict(zip(parts, scratch[n::3])) for n in range(3)
        )
        self.send, self.recv, self.base = send, recv, base
        self.all = []
        self.first = {"A": place.along_x, "B": place.along_y}
        self.second = {"A": place.along_y, "B": place.along_x}
        self.across = {}
        self.own = {part: [] for part in parts}
        self.passed = {part: [] for part in parts}
        self.final = {part: [] for part in parts}

    def copy(self, src, dst, device):
        n = self.base + len(self.all)
        made = pltpu.make_async_remote_copy(
            src_ref=src,
            dst_ref=dst,
            send_sem=self.send.at[n],
            recv_sem=self.recv.at[n],
            device_id=device,
            device_id_type=MESH,
        )
        made.start()
        self.all.append(made)
        return made

    def send_across(self, parts=None):
        for part in parts or self.parts:
            buf = self.bufs[part]
            self.across[part] = self.copy(buf.at[0], buf.at[RING], self.place.across_z())

    def send_own(self, parts=None):
        for part in parts or self.parts:
            buf, away = self.bufs[part], self.first[part[0]]
            for k in HOPS:
                self.own[part].append(self.copy(buf.at[0], buf.at[k], away(k)))

    def relay(self):
        for part in self.parts:
            buf, away = self.bufs[part], self.first[part[0]]
            self.across[part].wait_recv()
            for k in HOPS:
                self.passed[part].append(self.copy(buf.at[RING], buf.at[RING + k], away(k)))

    def hand_on(self, tables, segments):
        for part in self.parts:
            for made in self.own[part] + self.passed[part]:
                made.wait_recv()
            buf, out, arrive = self.bufs[part], self.outs[part], self.arrivals[part]
            for k in HOPS + (0,):
                for start, count, layer in segments[part]:
                    picked = buf[tables.slot(part[0], k, layer), pl.ds(start, count), :]
                    if k == 0:
                        arrive[0, pl.ds(start, count), :] = picked
                    else:
                        out[k - 1, pl.ds(start, count), :] = picked
                if k:
                    self.final[part].append(
                        self.copy(out.at[k - 1], arrive.at[k], self.second[part[0]](k))
                    )

    def take(self, tables, segments, put, parts=None):
        for part in parts or self.parts:
            for made in self.final[part]:
                made.wait_recv()
            arrive = self.arrivals[part]
            for start, count, layer in segments[part]:
                put(part, start, count, arrive[tables.last(part[0], layer), pl.ds(start, count), :])

    def drain(self):
        for made in self.all:
            made.wait_send()


WHOLES = ("A1", "B1", "A2", "B2")
BIG = FACE + CY


def full_segments():
    return {
        "A1": [(0, FACE, 0), (FACE, CY, 4)],
        "B1": [(0, FACE, 2), (FACE, CY, 5)],
        "A2": [(0, FACE, 1)],
        "B2": [(0, FACE, 3)],
    }


def whole_packet(pa, pb, exchange):
    for source, name in ((pa, "A"), (pb, "B")):
        one, two = exchange.bufs[name + "1"], exchange.bufs[name + "2"]
        one[0, pl.ds(0, FACE), :] = source[pl.ds(0, FACE), :]
        one[0, pl.ds(FACE, CY), :] = source[pl.ds(2 * FACE, CY), :]
        two[0, pl.ds(0, FACE), :] = source[pl.ds(FACE, FACE), :]


def quarter_segments(c):
    zface = jnp.where(c < 2, 4, 5)
    return {
        "A": [(s, n, f) for (s, n), f in zip(SEGS_QA, (0, 1, zface))],
        "B": [(s, n, f) for (s, n), f in zip(SEGS_QB, (2, 3))],
    }


def strip_segments():
    return {
        "A": [(s, n, f) for (s, n), f in zip(SEGS_QX, (0, 1, 4))],
        "B": [(s, n, f) for (s, n), f in zip(SEGS_QX, (2, 3, 5))],
    }


def exchange_scratch(*rows):
    made = []
    for r in rows:
        for slots in (2 * RING, RING - 1, RING):
            made.append(VMEM((slots, r, CZ), F32))
    return made


def quarter_packet(c, pa, pb, ba, bb):
    part = rows_of(c * QROW, QROW, 8)
    part2 = rows_of(FACE + c * QROW, QROW, 8)
    ba[0, pl.ds(0, QROW), :] = pa[part, :]
    ba[0, pl.ds(QROW, QROW), :] = pa[part2, :]
    bb[0, pl.ds(0, QROW), :] = pb[part, :]
    bb[0, pl.ds(QROW, QROW), :] = pb[part2, :]
    zrows = rows_of(2 * FACE + lax.rem(c, 2) * 8, 8, 8)
    ba[0, pl.ds(2 * QROW, 8), :] = jnp.where(c < 2, pa[zrows, :], pb[zrows, :])


def share(place, mine, ghost, send, recv, base, start, count):
    made = []
    for k in range(1, NC):
        copy = pltpu.make_async_remote_copy(
            src_ref=mine.at[pl.ds(start, count)],
            dst_ref=ghost.at[place.c, pl.ds(start, count)],
            send_sem=send.at[base + k - 1],
            recv_sem=recv.at[base + k - 1],
            device_id=place.member(k),
            device_id_type=MESH,
        )
        copy.start()
        made.append(copy)
    ghost[place.c, pl.ds(start, count), :] = mine[pl.ds(start, count), :]
    return made


def put_into(mine, second):
    def put(half, start, count, value):
        mine[pl.ds((0 if half == "A" else second) + start, count), :] = value

    return put


def put_halves(wa, wb):
    def put(half, start, count, value):
        at = FACE if half[1] == "2" else 2 * start
        (wa if half[0] == "A" else wb)[pl.ds(at, count), :] = value

    return put


def kernel(owner, links, codes, mats, part, seeds, rate, adjoint, final, *scratch):
    first, second = scratch[0:6], scratch[6:12]
    third, fourth = scratch[12:24], scratch[24:36]
    scratch = scratch[36:]
    grid0, grid1, wgrid, wgrid1 = (scratch[3 * n : 3 * n + 3] for n in range(4))
    pa, pb, mine, mine1, stored, landed, landed1, wa, wb, lam, xface, xshare, pu, pw, qa, qb, fz, send, recv = scratch[12:]
    place = Place()
    early = Exchange(place, "AB", first, send, recv, 0)
    again = Exchange(place, "AB", second, send, recv, 2 * N_COPIES)
    late = Exchange(place, WHOLES, third, send, recv, 4 * N_COPIES)
    back = Exchange(place, WHOLES, fourth, send, recv, 8 * N_COPIES)
    base = 12 * N_COPIES
    gather = Gather(place, part, stored, send, recv, base + 6)
    ends = EndLayers(place, xface, xshare, send, recv, base + 9)
    strips, quarters, wholes = strip_segments(), quarter_segments(place.c), full_segments()

    met = greet(place, True)
    pack_strip(part, place.c, xface, early.bufs["A"], early.bufs["B"])
    met()
    ends.begin()
    early.send_across("B")
    early.send_own("B")
    ends.take()
    for n in range(2):
        early.bufs["A"][0, pl.ds(n * QROW, QROW), :] = xshare[n]
    early.send_across("A")
    early.send_own("A")
    gather.begin()

    clear_z(qa, qb)
    for v in range(NV):
        for ghost in (0, CX + 1):
            wgrid[0][pl.ds(v * EXT + ghost * CY, CY), :] = jnp.zeros((CY, CZ), F32)
            wgrid1[0][pl.ds(v * EXT + ghost * CY, CY), :] = jnp.zeros((CY, CZ), F32)

    def weigh(x):
        tau = TAU * rate[rows_of(x * CY, CY), :]
        values = [seeds[rows_of(v * 256 + x * CY, CY), :] * tau for v in range(NV)]
        for v in range(NV):
            wgrid[0][cell_rows(v, x), :] = values[v]
        pack_z(values, x, qa, qb)

    each_x(weigh)
    pack_xy(wgrid[0], qa, qb)
    whole_packet(qa, qb, late)
    early.relay()
    late.send_across()
    tables = Tables(place, owner, links)
    code = [codes[f, tables.own] for f in range(6)]
    gather.relay()
    early.hand_on(tables, strips)
    late.send_own()
    early.take(tables, strips, put_into(mine, QX), "A")
    shared = share(place, mine, landed, send, recv, base, 0, QX)
    early.take(tables, strips, put_into(mine, QX), "B")
    shared += share(place, mine, landed, send, recv, base + 17, QX, QX)
    gather.take()
    span = CX * CY // NC
    for c in range(NC):
        for v in range(NV):
            grid0[0][pl.ds(v * EXT + CY + c * span, span), :] = stored[c, pl.ds(v * span, span), :]
    own_planes(grid0[0])
    clear_z(pu, pw)
    pack_xy(grid0[0], pu, pw)
    late.relay()
    each_x(lambda x: forward_step(mats, rate, grid0, grid1[0], pu, pw, x, "own"))
    clear_z(pa, pb)
    for copy in shared:
        copy.wait_recv()
    place_ghosts(strip_layers(landed), code, *grid0)
    repair(
        lambda f: forward_fix(f, mats, grid0, pu, pw), grid1[0], EXT, CY, fz, rate, pa, pb
    )
    pack_xy(grid1[0], pa, pb)

    quarter_packet(place.c, pa, pb, again.bufs["A"], again.bufs["B"])
    again.send_across()
    again.send_own()
    own_planes(grid1[0])

    def middle(x):
        adjoint_step(mats, grid1, wgrid, seeds, lam, x, "own")

    each_x(middle, 0, M0)
    again.relay()
    each_x(middle, M0, M1)
    again.hand_on(tables, quarters)
    each_x(middle, M1, M2)
    again.take(tables, quarters, put_into(mine1, QA), "A")
    shared1 = share(place, mine1, landed1, send, recv, base + 3, 0, QA)
    again.take(tables, quarters, put_into(mine1, QA), "B")
    shared1 += share(place, mine1, landed1, send, recv, base + 20, QA, QB)
    late.hand_on(tables, wholes)
    each_x(middle, M2, CX)
    late.take(tables, wholes, put_halves(wa, wb))
    place_ghosts(adjoint_layers(wa, wb), code, *wgrid)
    for copy in shared1:
        copy.wait_recv()
    place_ghosts(forward_layers(landed1), code, *grid1)
    repair(
        lambda f: adjoint_fix(f, mats, grid1, wgrid, pa, pb, qa, qb),
        lam,
        CX * CY,
        0,
        fz,
        pa=qa,
        pb=qb,
        weighted=wgrid1[0],
        weight=rate,
    )
    pack_xy(wgrid1[0], qa, qb)

    whole_packet(qa, qb, back)
    back.send_across()
    back.send_own()

    def last(x):
        forward_step(mats, rate, grid1, final, None, None, x)

    def end(x):
        adjoint_step(mats, grid0, wgrid1, lam, adjoint, x)

    each_x(last, 0, 10)
    back.relay()
    each_x(last, 10, CX)
    each_x(end, 0, 4)
    back.hand_on(tables, wholes)
    each_x(end, 4, CX)
    back.take(tables, wholes, put_halves(wa, wb))
    place_ghosts(adjoint_layers(wa, wb), code, *wgrid1)
    repair(lambda f: adjoint_fix(f, mats, grid0, wgrid1, pu, pw), adjoint, CX * CY, 0, fz)

    for copy in shared + shared1:
        copy.wait_send()
    ends.drain()
    for exchange in (gather, early, late, again, back):
        exchange.drain()


def on_device(checkpoint, seeds, cell_rate, flux_mats, owner, neighbours, orientation):
    vm, sm = pltpu.VMEM, pltpu.SMEM
    block = jax.ShapeDtypeStruct((ROWS, CZ), F32)
    strip, quarter = exchange_scratch(QX, QX), exchange_scratch(QA, QB)
    whole = exchange_scratch(BIG, BIG, FACE, FACE)
    grid = [VMEM((NV * EXT, CZ), F32), VMEM((2 * FACE, CZ), F32), VMEM((2 * CY, CZ), F32)]
    half = VMEM((HALF, CZ), F32)
    copies = 23 + 12 * N_COPIES
    adjoint, final = pl.pallas_call(
        kernel,
        out_shape=(block, block),
        in_specs=[pl.BlockSpec(memory_space=m) for m in (sm, sm, sm, sm, vm, vm, vm)],
        out_specs=(pl.BlockSpec(memory_space=vm), pl.BlockSpec(memory_space=vm)),
        scratch_shapes=strip
        + quarter
        + whole * 2
        + grid * 4
        + [half, half, VMEM((2 * QX, CZ), F32), VMEM((QA + QB, CZ), F32)]
        + [VMEM((NC, ROWS // NC, CZ), F32)]
        + [VMEM((NC, 2 * QX, CZ), F32), VMEM((NC, QA + QB, CZ), F32), half, half]
        + [VMEM((ROWS, CZ), F32), VMEM((2, FACE, CZ), F32), VMEM((2, QROW, CZ), F32)]
        + [half, half, half, half, VMEM((2 * NV * CY, CZ), F32)]
        + [pltpu.SemaphoreType.DMA((copies,)), pltpu.SemaphoreType.DMA((copies,))],
        compiler_params=pltpu.CompilerParams(collective_id=0, has_side_effects=True),
    )(
        owner,
        neighbours.T,
        orientation.T,
        flux_mats,
        checkpoint.reshape(ROWS // NC, CZ),
        seeds.reshape(ROWS, CZ),
        cell_rate.reshape(CX * CY, CZ),
    )
    return (
        adjoint.reshape(1, 1, NV, CX, CY, CZ),
        final.reshape(1, NV, CX, CY, CZ),
    )


def solution(mesh):
    return jax.shard_map(
        on_device,
        mesh=mesh,
        in_specs=(
            P("space", None, "ckpt", None, None),
            P("ckpt", "space", None, None, None, None),
            P("space", None, None, None),
            P(),
            P(),
            P(),
            P(),
        ),
        out_specs=(P("ckpt", "space", None, None, None, None), P("space", None, None, None, None)),
        check_vma=False,
    )
```
